256 devices in a mesh: lat: 8 (over x_hi, y), lon: 32 (over x_lo, z, core).
Axes of the slice: x: 4 (x_hi: 2, x_lo: 2; x = x_hi * 2 + x_lo), y: 4, z: 8, core: 2. Of those that a mesh axis runs over, the one named last changes fastest.
Arguments:
- tracer: float32 [100, 64, 4096], P(None, 'lat', 'lon'), may hold values from -100 to 100
- cotangent: float32 [100, 64, 4096], P(None, 'lat', 'lon'), may hold values from -6 to 6
- land_mask: int32 [64, 4096], P('lat', 'lon'), may hold values 0 or 1
- bottom: int32 [64, 4096], P('lat', 'lon'), may hold values from 25 to 100
- kappa: float32 [100], replicated, may hold values from 0.05 to 8
- w_in: bfloat16 [100, 512], replicated, may hold values from -0.625 to 0.625
- b_in: float32 [512], replicated, may hold values from -4 to 4
- w_out: bfloat16 [512, 100], replicated, may hold values from -0.25 to 0.25
- b_out: float32 [100], replicated, may hold values from 6 to 24
Outputs:
- tracer_adjoint: float32 [100, 64, 4096], P(None, 'lat', 'lon')
- grad_w_in: float32 [100, 512], replicated
- grad_b_in: float32 [512], replicated
- grad_w_out: float32 [512, 100], replicated
- grad_b_out: float32 [100], replicated
The draws below stay inside these ranges and needn't reach their ends.
All inputs are finite; a program needn't handle non-finite values. No bound on the sum of `land_mask` on one device may be relied on, other than what follows from the above.
Results may differ from the reference program's by a relative error of at most 0.0069.
Values sent between devices are 32-bit elements; how exact they have to be, the bound alone decides.
A program may use at most 64 MiB of HBM per device.

```python
import math
import jax
import jax.numpy as jnp
from jax import lax

K = 100
HID = 512
CLAT = 8
CLON = 128
NLAT = 64
NLON = 4096


def draw_tracer(key, part):
    noise_key, level_key, block_key = jax.random.split(jax.random.fold_in(key, 17), 3)
    lat_pos = jnp.arange(NLAT, dtype=jnp.float32) / max(NLAT - 1, 1)
    lon_pos = jnp.arange(NLON, dtype=jnp.float32) / max(NLON - 1, 1)
    trend = jnp.sqrt((1.0 + 2.0 * lat_pos)[:, None] * (1.0 + 2.0 * lon_pos)[None, :])
    block_scale = jnp.exp(jax.random.uniform(block_key, (K, NLON // CLON), minval=-1.0, maxval=1.0))
    block_cols = jnp.repeat(block_scale, CLON, axis=1)
    level_scale = jnp.exp(jax.random.uniform(level_key, (K,), minval=-0.7, maxval=0.7))
    noise = jnp.clip(jax.random.normal(noise_key, (K, NLAT, NLON)), -4.0, 4.0)
    return (level_scale[:, None, None] * block_cols[:, None, :] * trend[None] * noise).astype(jnp.float32)


def place_ends(drawn, rng, low, largest):
    index_at = [jax.random.randint(jax.random.fold_in(rng, axis), (), 0, length) for axis, length in enumerate(drawn.shape)]
    longest = drawn.shape.index(max(drawn.shape))
    next_to = index_at[:longest] + [(index_at[longest] + 1) % drawn.shape[longest]] + index_at[longest + 1:]
    return drawn.at[tuple(index_at)].set(low).at[tuple(next_to)].set(largest)


def level_of(rng, extent, cuts, least, largest):
    level = 1.0
    for dim, parts in cuts:
        heights = jax.random.uniform(jax.random.fold_in(jax.random.fold_in(rng, 6), dim), (parts,), jnp.float32, least / len(cuts), largest / len(cuts))
        level = level * jnp.repeat(jnp.exp(heights), extent[dim] // parts).reshape((-1,) + (1,) * (len(extent) - 1 - dim))
    return level


def bell_draw(stream_key, shape, scale, bound, cuts=(), kind=jnp.bfloat16):
    factor_of = level_of(stream_key, shape, cuts, -0.22, 0.18) if cuts else 1.0
    result = jax.random.normal(stream_key, shape, jnp.float32) * scale * factor_of
    return jnp.minimum(jnp.maximum(result, -bound), bound).astype(kind)


def setup_inputs(seed: int = 0) -> dict:
    streams_of = jax.random.split(jax.random.key(seed), 10)
    return {
        "tracer": draw_tracer(jax.random.fold_in(streams_of[9], 71), 0),
        "cotangent": bell_draw(streams_of[1], (K, NLAT, NLON), 1.0, 6.0, ((1, 8), (2, 32)), jnp.float32),
        "land_mask": place_ends((jax.random.randint(streams_of[2], (NLAT, NLON), 0, 5) < 4).astype(jnp.int32), jax.random.fold_in(streams_of[2], 1), 0, 1),
        "bottom": place_ends(jax.random.randint(streams_of[3], (NLAT, NLON), K // 4, K + 1), jax.random.fold_in(streams_of[3], 1), K // 4, K).astype(jnp.int32),
        "kappa": jnp.clip(jnp.exp(jax.random.uniform(streams_of[4], (K,), jnp.float32, math.log(0.05), math.log(8.0))), 0.05, 8.0),
        "w_in": bell_draw(streams_of[5], (K, HID), K ** -0.5, 0.625),
        "b_in": bell_draw(streams_of[6], (HID,), 1.0, 4.0, (), jnp.float32),
        "w_out": bell_draw(streams_of[7], (HID, K), HID ** -0.5, 0.25),
        "b_out": jnp.clip(jax.random.uniform(streams_of[8], (K,), jnp.float32, 6.0, 24.0), 6.0, 24.0),
    }


spread_coef = 0.15
level_eps = 1e-05

def spread(center, wet_cells):
    field_pad = jnp.pad(center, ((0, 0), (1, 1), (0, 0)))
    wet_pad = jnp.pad(wet_cells, ((0, 0), (1, 1), (0, 0)))
    neighbours = ((field_pad[:, 2:], wet_pad[:, 2:]), (field_pad[:, :-2], wet_pad[:, :-2]), (jnp.roll(center, 1, 2), jnp.roll(wet_cells, 1, 2)), (jnp.roll(center, -1, 2), jnp.roll(wet_cells, -1, 2)))
    flux_total = jnp.zeros_like(center)
    for near_field, near_wet in neighbours:
        flux_total = flux_total + wet_cells * near_wet * (near_field - center)
    return center + spread_coef * flux_total

def column_solve(below, diagonal, above, right_side):

    def sweep_down(state_pair, row_items):
        ratio_prev, value_prev = state_pair
        below_row, diag_row, above_row, right_row = row_items
        pivot = diag_row - below_row * ratio_prev
        ratio_next = above_row / pivot
        value_next = (right_row - below_row * value_prev) / pivot
        return ((ratio_next, value_next), (ratio_next, value_next))
    zeros_row = jnp.zeros_like(right_side[0])
    _, (ratios, values) = lax.scan(sweep_down, (zeros_row, zeros_row), (below, diagonal, above, right_side))

    def sweep_up(later, row_items):
        ratio_row, value_row = row_items
        result_row = value_row - ratio_row * later
        return (result_row, result_row)
    _, solved = lax.scan(sweep_up, zeros_row, (ratios, values), reverse=True)
    return solved

def vertical_matrix(wet_cells, kappa, sinking):
    open_face = wet_cells * jnp.concatenate([wet_cells[1:], jnp.zeros_like(wet_cells[:1])], 0)
    kappa_col = kappa[:, None, None]
    down_coef = open_face * (kappa_col + sinking)
    up_coef = open_face * kappa_col
    prev_down = jnp.concatenate([jnp.zeros_like(down_coef[:1]), down_coef[:-1]], 0)
    prev_up = jnp.concatenate([jnp.zeros_like(up_coef[:1]), up_coef[:-1]], 0)
    diagonal = 1.0 + down_coef + prev_up
    return (open_face, down_coef, up_coef, prev_down, prev_up, diagonal)

def column_block(block_items, radius, kappa, w_in, b_in, w_out, b_out):
    tracer_blk, cot_blk, wet_blk, mixed_blk = block_items
    block_shape = tracer_blk.shape
    wet_tracer = (wet_blk * tracer_blk).reshape(block_shape[0], -1)
    inputs = (wet_tracer / radius[:, None]).astype(jnp.bfloat16)
    pre_act = jnp.dot(w_in.T, inputs, preferred_element_type=jnp.float32) + b_in[:, None]
    hidden = jax.nn.silu(pre_act).astype(jnp.bfloat16)
    logits = jnp.dot(w_out.T, hidden, preferred_element_type=jnp.float32) + b_out[:, None]
    sinking = jax.nn.softplus(logits).reshape(block_shape)
    open_face, down_coef, up_coef, prev_down, prev_up, diagonal = vertical_matrix(wet_blk, kappa, sinking)
    new_tracer = column_solve(-prev_down, diagonal, -up_coef, mixed_blk)
    adjoint = column_solve(-prev_up, diagonal, -down_coef, cot_blk)
    adjoint_next = jnp.concatenate([adjoint[1:], jnp.zeros_like(adjoint[:1])], 0)
    d_sinking = open_face * new_tracer * (adjoint_next - adjoint)
    d_logits = (d_sinking.reshape(block_shape[0], -1) * jax.nn.sigmoid(logits)).astype(jnp.bfloat16)
    grad_out_t = jnp.dot(d_logits, hidden.T, preferred_element_type=jnp.float32)
    grad_bout = lax.optimization_barrier(jnp.sum(d_logits.astype(jnp.float32), axis=1))
    d_hidden = jnp.dot(w_out, d_logits, preferred_element_type=jnp.float32)
    gate_sig = jax.nn.sigmoid(pre_act)
    d_pre = (d_hidden * gate_sig * (1.0 + pre_act * (1.0 - gate_sig))).astype(jnp.bfloat16)
    grad_in = jnp.dot(inputs, d_pre.T, preferred_element_type=jnp.float32)
    grad_bin = lax.optimization_barrier(jnp.sum(d_pre.astype(jnp.float32), axis=1))
    d_inputs = jnp.dot(w_in, d_pre, preferred_element_type=jnp.float32)
    level_part = lax.optimization_barrier(jnp.sum(d_inputs * wet_tracer, axis=1))
    return (adjoint, d_inputs.reshape(block_shape), grad_in, grad_out_t, grad_bin, grad_bout, level_part)

def reference(tracer, cotangent, land_mask, bottom, kappa, w_in, b_in, w_out, b_out):
    column_depth = land_mask * bottom
    level_ids = jnp.arange(K, dtype=jnp.int32)[:, None, None]
    wet_cells = (level_ids < column_depth[None]).astype(jnp.float32)
    wet_tracer = wet_cells * tracer
    energy = lax.optimization_barrier(jnp.sum(wet_tracer * wet_tracer, axis=(1, 2)))
    column_count = NLAT * NLON
    radius = jnp.sqrt(energy / column_count + level_eps)
    mixed = spread(tracer, wet_cells)
    block_count = NLAT // CLAT

    def to_blocks(whole):
        return whole.reshape(K, block_count, CLAT, NLON).transpose(1, 0, 2, 3)

    def from_blocks(pieces):
        return pieces.transpose(1, 0, 2, 3).reshape(K, NLAT, NLON)
    adj_blocks, din_blocks, grad_in, grad_out_t, grad_bin, grad_bout, level_parts = lax.map(lambda block_items: column_block(block_items, radius, kappa, w_in, b_in, w_out, b_out), (to_blocks(tracer), to_blocks(cotangent), to_blocks(wet_cells), to_blocks(mixed)))
    adjoint = from_blocks(adj_blocks)
    d_inputs = from_blocks(din_blocks)
    level_sum = lax.optimization_barrier(jnp.sum(level_parts, axis=0))
    column_scale = column_count ** (-0.5)
    d_wet = d_inputs / radius[:, None, None] - wet_tracer * (level_sum / (column_count * radius ** 3))[:, None, None]
    tracer_adjoint = spread(adjoint, wet_cells) + wet_cells * d_wet
    grad_w_in = lax.optimization_barrier(jnp.sum(grad_in, axis=0)) * column_scale
    grad_b_in = lax.optimization_barrier(jnp.sum(grad_bin, axis=0)) * column_scale
    grad_w_out = lax.optimization_barrier(jnp.sum(grad_out_t, axis=0)).T * column_scale
    grad_b_out = lax.optimization_barrier(jnp.sum(grad_bout, axis=0)) * column_scale
    return (tracer_adjoint, grad_w_in, grad_b_in, grad_w_out, grad_b_out)
```

```python
import functools
import math

import jax
import jax.numpy as jnp
from jax import lax
from jax.experimental import pallas as pl
from jax.experimental.pallas import tpu as pltpu
from jax.sharding import PartitionSpec as P

MESH = pl.DeviceIdType.MESH
F32 = jnp.float32
BF16 = jnp.bfloat16

spread_coef = 0.15
level_eps = 1e-05

LEVELS = 100
ROWS = 8
LANES = 128
HIDDEN = 512
COLS = ROWS * LANES
PAD = 104
LAT = 8
LON = 32
PLANE = 32
DEPTH = 8


def split_lon(lon):
    return lon // 16, (lon // 2) % 8, lon % 2


def plane_peer(q, z):
    return q // 4, ((q // 2) % 2) * 16 + z * 2 + q % 2


def z_peer(z, lat, lon_hi, core):
    return lat, lon_hi * 16 + z * 2 + core


def kernel(
    tracer_hbm, cot_hbm, land_ref, bottom_ref, kappa_s, w_in_ref, b_in_ref, w_out_ref, b_out_s,
    out_ref, gw_in_ref, gb_in_ref, gw_out_ref, gb_out_ref,
    tr_v, cot_v, slabs, adj_slabs, edge_hi, edge_lo, edge2_hi, edge2_lo,
    halo, halo2, near_depth,
    small_src, small_r1, small_mid, small_r2,
    small2_src, small2_r1, small2_mid, small2_r2,
    wi_f, wo_f, wi_b, w1t, wot, wo_b,
    inp, hid, slope, dpre, dlog, din,
    logit, mixed, val_x, val_y, mul_x, mul_y, gate, adj, dlev,
    g_in, g_out, ra_in, ra_out, mid_in, mid_out, rz_in, rz_out, ch_in, ch_out, fin_in, fin_out,
    load_sems, send_sems, recv_sems, halo_send, halo_recv,
):
    lat = lax.axis_index("lat")
    lon = lax.axis_index("lon")
    lon_hi, z_me, core = split_lon(lon)
    q_me = lat * 4 + lon_hi * 2 + core

    load_tr = pltpu.make_async_copy(tracer_hbm, tr_v, load_sems.at[0])
    load_tr.start()
    load_cot = pltpu.make_async_copy(cot_hbm, cot_v, load_sems.at[1])
    load_cot.start()

    def plane_id(d):
        q = (q_me + d) % PLANE
        return q, plane_peer(q, z_me)

    def z_id(d):
        z = (z_me + d) % DEPTH
        return z, z_peer(z, lat, lon_hi, core)

    barrier = pltpu.get_barrier_semaphore()

    def greet_plane(d, carry):
        _, dev = plane_id(d)
        pl.semaphore_signal(barrier, inc=1, device_id=dev, device_id_type=MESH)
        return carry

    def greet_z(d, carry):
        _, dev = z_id(d)
        pl.semaphore_signal(barrier, inc=1, device_id=dev, device_id_type=MESH)
        return carry

    lax.fori_loop(1, PLANE, greet_plane, 0)
    lax.fori_loop(1, DEPTH, greet_z, 0)
    far_lon = (lon + 2 * core - 1 + LON) % LON
    pl.semaphore_signal(barrier, inc=1, device_id=(lat, far_lon), device_id_type=MESH)

    row_id = lax.broadcasted_iota(jnp.int32, (PAD, LANES), 0)
    lane_id = lax.broadcasted_iota(jnp.int32, (PAD, LANES), 1)
    row_f = row_id.astype(F32)
    diag = row_id == lane_id

    def as_row(column):
        return jnp.sum(jnp.where(diag, column, 0.0), axis=0, keepdims=True)

    def as_column(row):
        return jnp.sum(jnp.where(diag, row, 0.0), axis=1, keepdims=True)

    depth_all = (land_ref[...] * bottom_ref[...]).astype(F32)

    load_tr.wait()
    energy = jnp.zeros((PAD, LANES), F32)
    hi = jnp.zeros((PAD, LANES), F32)
    lo = jnp.zeros((PAD, LANES), F32)
    for i in range(ROWS):
        slabs[i, 0:LEVELS, :] = tr_v[:, i, :]
        slabs[i, LEVELS:PAD, :] = jnp.broadcast_to(depth_all[i : i + 1, :], (PAD - LEVELS, LANES))
        x = slabs[i]
        wet_x = jnp.where(row_f < depth_all[i : i + 1, :], x, 0.0)
        energy = energy + wet_x * wet_x
        hi = jnp.where(lane_id == i, pltpu.roll(x, i + 1, 1), hi)
        lo = jnp.where(lane_id == i, pltpu.roll(x, i, 1) if i else x, lo)
    edge_hi[...] = hi
    edge_lo[...] = lo
    small_src[...] = as_row(jnp.sum(energy, axis=1, keepdims=True))
    small_r1[q_me] = small_src[...]

    pl.semaphore_wait(barrier, PLANE - 1 + DEPTH - 1 + 1)

    def small_plane(src, dst, which):
        def send(d, carry):
            _, dev = plane_id(d)
            pltpu.make_async_remote_copy(
                src, dst.at[q_me], send_sems.at[which], recv_sems.at[which],
                device_id=dev, device_id_type=MESH,
            ).start()
            return carry

        lax.fori_loop(1, PLANE, send, 0)

    def small_z(src, dst, which):
        def send(d, carry):
            _, dev = z_id(d)
            pltpu.make_async_remote_copy(
                src, dst.at[z_me], send_sems.at[which], recv_sems.at[which],
                device_id=dev, device_id_type=MESH,
            ).start()
            return carry

        lax.fori_loop(1, DEPTH, send, 0)

    def drain(ref, sem):
        pltpu.make_async_copy(ref, ref, sem).wait()

    def send_halo(k, pieces, dst):
        up = (lat + 1) % LAT
        down = (lat + LAT - 1) % LAT
        right = (lon + 1) % LON
        left = (lon + LON - 1) % LON
        targets = ((up, lon), (down, lon), (lat, right), (lat, left))
        copies = []
        for n, (src, dev) in enumerate(zip(pieces, targets)):
            copy = pltpu.make_async_remote_copy(
                src, dst.at[n], halo_send.at[4 * k + n], halo_recv.at[4 * k + n],
                device_id=dev, device_id_type=MESH,
            )
            copy.start()
            copies.append(copy)
        return copies

    small_plane(small_src, small_r1, 0)
    halo_copies = send_halo(0, (slabs.at[ROWS - 1], slabs.at[0], edge_hi, edge_lo), halo)

    bias = b_in_ref[...]
    bias_hi = bias.astype(BF16).astype(F32)
    bias_mid = (bias - bias_hi).astype(BF16).astype(F32)
    bias_lo = bias - bias_hi - bias_mid
    wi_f[LEVELS:LANES, :] = jnp.zeros((LANES - LEVELS, HIDDEN), F32)
    wi_f[0:LEVELS, :] = w_in_ref[...].astype(F32)
    wi_f[LEVELS : LEVELS + 1, :] = bias_hi
    wi_f[LEVELS + 1 : LEVELS + 2, :] = bias_mid
    wi_f[LEVELS + 2 : LEVELS + 3, :] = bias_lo
    wi_b[...] = wi_f[...].astype(BF16)
    w1t[...] = wi_f[...].T.astype(BF16)
    wo_f[...] = jnp.zeros((HIDDEN, LANES), F32)
    wo_f[:, 0:LEVELS] = w_out_ref[...].astype(F32)
    wo_b[...] = wo_f[...].astype(BF16)
    wot[...] = wo_f[...].T.astype(BF16)
    dlev[LEVELS:LANES] = jnp.zeros((LANES - LEVELS, ROWS, LANES), F32)

    drain(small_r1.at[pl.ds(0, PLANE - 1)], recv_sems.at[0])
    small_mid[...] = jnp.sum(small_r1[...], axis=0)
    small_r2[z_me] = small_mid[...]
    small_z(small_mid, small_r2, 1)

    for copy in halo_copies:
        copy.wait_recv()

    def neighbours(field, edges, i):
        centre = field[i]
        below = field[i + 1] if i + 1 < ROWS else edges[1]
        above = field[i - 1] if i else edges[0]
        from_left = pltpu.roll(edges[2], LANES - i, 1) if i else edges[2]
        left = jnp.where(lane_id == 0, from_left, pltpu.roll(centre, 1, 1))
        right = jnp.where(
            lane_id == LANES - 1, pltpu.roll(edges[3], LANES - 1 - i, 1), pltpu.roll(centre, LANES - 1, 1)
        )
        return centre, (below, above, left, right)

    def flux(centre, near, i):
        total = jnp.zeros((PAD, LANES), F32)
        for n in range(4):
            total = total + jnp.where(
                row_f < near_depth[n * ROWS + i : n * ROWS + i + 1, :], near[n] - centre, 0.0
            )
        return centre + spread_coef * total

    has_above = jnp.where(lat > 0, 1.0, 0.0)
    has_below = jnp.where(lat < LAT - 1, 1.0, 0.0)
    for i in range(ROWS):
        centre, near = neighbours(slabs, halo, i)
        own = centre[LEVELS : LEVELS + 1, :]
        for n in range(4):
            other = near[n][LEVELS : LEVELS + 1, :]
            if n == 0 and i == ROWS - 1:
                other = other * has_below
            if n == 1 and i == 0:
                other = other * has_above
            near_depth[n * ROWS + i : n * ROWS + i + 1, :] = jnp.minimum(own, other)
        mixed[:, i, :] = flux(centre, near, i)[0:LEVELS]

    drain(small_r2.at[pl.ds(0, DEPTH - 1)], recv_sems.at[1])
    energy_all = as_column(jnp.sum(small_r2[...], axis=0))
    count = float(LAT * LON * COLS)
    radius = jnp.sqrt(energy_all / count + level_eps)
    inv_radius = 1.0 / radius

    def wet_slab(i):
        x = slabs[i]
        return jnp.where(row_f < x[LEVELS : LEVELS + 1, :], x, 0.0)

    inp[PAD - 8 : LANES, :] = jnp.zeros((LANES - PAD + 8, COLS), BF16)
    one_rows = jnp.where(row_id < LEVELS + 3, 1.0, 0.0)
    for i in range(ROWS):
        scaled = jnp.where(row_id < LEVELS, wet_slab(i) * inv_radius, one_rows)
        scaled = jnp.concatenate([scaled, jnp.zeros((LANES - PAD, LANES), F32)], axis=0)
        inp[:, i * LANES : (i + 1) * LANES] = scaled.astype(BF16)

    width = 256
    for j in range(COLS // width):
        cols = slice(j * width, (j + 1) * width)
        pre = jnp.dot(w1t[...], inp[:, cols], preferred_element_type=F32)
        sig = 1.0 / (1.0 + jnp.exp(-pre))
        act = pre * sig
        hid[:, cols] = act.astype(BF16)
        slope[:, cols] = sig * (1.0 + pre * (1.0 - sig))
        out = jnp.dot(wot[...], hid[:, cols], preferred_element_type=F32)
        for s in range(width // LANES):
            logit[:, j * (width // LANES) + s, :] = out[0:LEVELS, s * LANES : (s + 1) * LANES]

    load_cot.wait()
    depth = depth_all
    half = LEVELS // 2

    def level_terms(k):
        x = logit[k] + b_out_s[k]
        ex = jnp.exp(-jnp.abs(x))
        soft = jnp.maximum(x, 0.0) + jnp.log1p(ex)
        sig = jnp.where(x >= 0.0, 1.0, ex) / (1.0 + ex)
        kf = (k + 1).astype(F32)
        open_face = kf < depth
        kap = kappa_s[k]
        down = jnp.where(open_face, kap + soft, 0.0)
        up = jnp.where(open_face, kap, 0.0)
        gate[k] = jnp.where(open_face, sig, 0.0)
        return down, up

    def eliminate(s, carry):
        down_p, up_p, r_p, v_p, w_p, sb_n, u_n, z_n = carry
        k = s
        down, up = level_terms(k)
        pivot = 1.0 + down + up_p - down_p * up_p * r_p
        r = 1.0 / pivot
        v = (mixed[k] + down_p * v_p) * r
        w = (cot_v[k] + up_p * w_p) * r
        val_x[k] = v
        val_y[k] = w
        mul_x[k] = up * r
        mul_y[k] = down * r
        b = LEVELS - 1 - s
        down_b, up_b = level_terms(b)
        up_above = jnp.where(b.astype(F32) < depth, kappa_s[b - 1], 0.0)
        pivot_b = 1.0 + down_b + up_above - down_b * up_b * sb_n
        sb = 1.0 / pivot_b
        u = (mixed[b] + up_b * u_n) * sb
        zz = (cot_v[b] + down_b * z_n) * sb
        val_x[b] = u
        val_y[b] = zz
        mul_y[b] = up_above * sb
        mul_x[b + 1] = down_b * sb_n
        return down, up, r, v, w, sb, u, zz

    zero = jnp.zeros((ROWS, LANES), F32)
    down_m, up_m, r_m, v_m, w_m, sb_m, u_m, z_m = lax.fori_loop(
        0, half, eliminate, (zero,) * 8, unroll=5
    )
    ratio_x = up_m * r_m
    ratio_y = down_m * r_m
    back_x = down_m * sb_m
    back_y = up_m * sb_m
    inv_det = 1.0 / (1.0 - ratio_x * back_x)
    x_top = (v_m + ratio_x * u_m) * inv_det
    x_bot = u_m + back_x * x_top
    y_top = (w_m + ratio_y * z_m) * inv_det
    y_bot = z_m + back_y * y_top
    adj[half - 1] = y_top
    adj[half] = y_bot
    dlev[half - 1] = gate[half - 1] * x_top * (y_bot - y_top)

    def substitute(s, carry):
        x_t, y_t, x_b, y_b = carry
        k = half - 1 - s
        x_n = val_x[k] + mul_x[k] * x_t
        y_n = val_y[k] + mul_y[k] * y_t
        adj[k] = y_n
        dlev[k] = gate[k] * x_n * (y_t - y_n)
        b = half + s
        x_c = val_x[b] + mul_x[b] * x_b
        y_c = val_y[b] + mul_y[b] * y_b
        adj[b] = y_c
        dlev[b - 1] = gate[b - 1] * x_b * (y_c - y_b)
        return x_n, y_n, x_c, y_c

    lax.fori_loop(1, half, substitute, (x_top, y_top, x_bot, y_bot), unroll=7)
    dlev[LEVELS - 1] = zero

    hi = jnp.zeros((LEVELS, LANES), F32)
    lo = jnp.zeros((LEVELS, LANES), F32)
    lane_l = lane_id[0:LEVELS]
    for i in range(ROWS):
        x = adj[:, i, :]
        adj_slabs[i, 0:LEVELS, :] = x
        hi = jnp.where(lane_l == i, pltpu.roll(x, i + 1, 1), hi)
        lo = jnp.where(lane_l == i, pltpu.roll(x, i, 1) if i else x, lo)
    edge2_hi[0:LEVELS, :] = hi
    edge2_lo[0:LEVELS, :] = lo
    for i in range(ROWS):
        adj_slabs[i, LEVELS:PAD, :] = jnp.zeros((PAD - LEVELS, LANES), F32)
    edge2_hi[LEVELS:PAD, :] = jnp.zeros((PAD - LEVELS, LANES), F32)
    edge2_lo[LEVELS:PAD, :] = jnp.zeros((PAD - LEVELS, LANES), F32)
    for i in range(ROWS):
        dlog[:, i * LANES : (i + 1) * LANES] = dlev[:, i, :].astype(BF16)
    halo2_copies = send_halo(
        1, (adj_slabs.at[ROWS - 1], adj_slabs.at[0], edge2_hi, edge2_lo), halo2
    )

    contract_last = (((1,), (1,)), ((), ()))
    grad_out = lax.dot_general(hid[...], dlog[...], contract_last, preferred_element_type=F32)
    g_out[...] = grad_out.reshape(PLANE, HIDDEN // PLANE, LANES)
    ra_out[q_me] = g_out[q_me]
    bout_row = lax.dot_general(
        jnp.ones((16, COLS), BF16), dlog[...], contract_last, preferred_element_type=F32
    )[0:1]

    def scatter(src, dst, which):
        def send(d, carry):
            q, dev = plane_id(d)
            pltpu.make_async_remote_copy(
                src.at[q], dst.at[q_me], send_sems.at[which], recv_sems.at[which],
                device_id=dev, device_id_type=MESH,
            ).start()
            return carry

        lax.fori_loop(1, PLANE, send, 0)

    def gather(src, dst, which):
        small_plane(src, dst, which)

    scatter(g_out, ra_out, 2)

    for j in range(COLS // width):
        cols = slice(j * width, (j + 1) * width)
        back = jnp.dot(wo_b[...], dlog[:, cols], preferred_element_type=F32)
        dpre[:, cols] = (back * slope[:, cols]).astype(BF16)
    grad_in = lax.dot_general(inp[...], dpre[...], contract_last, preferred_element_type=F32)
    for p in range(PLANE // 2):
        g_in[2 * p] = grad_in[8 * p : 8 * p + 8, 0:256]
        g_in[2 * p + 1] = grad_in[8 * p : 8 * p + 8, 256:512]
    ra_in[q_me] = g_in[q_me]
    scatter(g_in, ra_in, 3)

    level = jnp.zeros((PAD, LANES), F32)
    for j in range(COLS // width):
        cols = slice(j * width, (j + 1) * width)
        out = jnp.dot(wi_b[...], dpre[:, cols], preferred_element_type=F32)
        for s in range(width // LANES):
            i = j * (width // LANES) + s
            part = out[0:PAD, s * LANES : (s + 1) * LANES]
            din[i] = part
            level = level + part * wet_slab(i)
    small2_src[:, 0:LANES] = as_row(jnp.sum(level, axis=1, keepdims=True))
    small2_src[:, LANES : 2 * LANES] = bout_row
    small2_r1[q_me] = small2_src[...]
    small_plane(small2_src, small2_r1, 4)

    drain(ra_out.at[pl.ds(0, PLANE - 1)], recv_sems.at[2])
    mid_out[...] = jnp.sum(ra_out[...], axis=0)
    rz_out[z_me] = mid_out[...]
    small_z(mid_out, rz_out, 5)
    drain(ra_in.at[pl.ds(0, PLANE - 1)], recv_sems.at[3])
    mid_in[...] = jnp.sum(ra_in[...], axis=0)
    rz_in[z_me] = mid_in[...]
    small_z(mid_in, rz_in, 6)
    drain(small2_r1.at[pl.ds(0, PLANE - 1)], recv_sems.at[4])
    small2_mid[...] = jnp.sum(small2_r1[...], axis=0)
    small2_r2[z_me] = small2_mid[...]
    small_z(small2_mid, small2_r2, 7)

    scale = 1.0 / math.sqrt(count)
    drain(rz_out.at[pl.ds(0, DEPTH - 1)], recv_sems.at[5])
    ch_out[...] = jnp.sum(rz_out[...], axis=0) * scale
    fin_out[q_me] = ch_out[...]
    gather(ch_out, fin_out, 8)
    drain(rz_in.at[pl.ds(0, DEPTH - 1)], recv_sems.at[6])
    ch_in[...] = jnp.sum(rz_in[...], axis=0) * scale
    fin_in[q_me] = ch_in[...]
    gather(ch_in, fin_in, 9)

    for copy in halo2_copies:
        copy.wait_recv()
    drain(small2_r2.at[pl.ds(0, DEPTH - 1)], recv_sems.at[7])
    small2 = jnp.sum(small2_r2[...], axis=0)
    level_sum = as_column(small2[:, 0:LANES])
    gb_out_ref[...] = small2[:, LANES : 2 * LANES] * scale
    level_scale = level_sum / (count * radius * radius * radius)
    for i in range(ROWS):
        centre, near = neighbours(adj_slabs, halo2, i)
        mix = flux(centre, near, i)
        x = slabs[i]
        wet = row_f < x[LEVELS : LEVELS + 1, :]
        total = mix + jnp.where(wet, din[i] * inv_radius - x * level_scale, 0.0)
        out_ref[:, i, :] = total[0:LEVELS]

    drain(fin_out.at[pl.ds(0, PLANE - 1)], recv_sems.at[8])
    gw_out_ref[...] = fin_out[...].reshape(HIDDEN, LANES)[:, 0:LEVELS]
    drain(fin_in.at[pl.ds(0, PLANE - 1)], recv_sems.at[9])
    for p in range(LEVELS // 8 + 1):
        rows = min(8, LEVELS - 8 * p)
        gw_in_ref[8 * p : 8 * p + rows, 0:256] = fin_in[2 * p, 0:rows, :]
        gw_in_ref[8 * p : 8 * p + rows, 256:512] = fin_in[2 * p + 1, 0:rows, :]
    bias_tile, bias_row = LEVELS // 8, LEVELS % 8
    gb_in_ref[:, 0:256] = fin_in[2 * bias_tile, bias_row : bias_row + 1, :]
    gb_in_ref[:, 256:512] = fin_in[2 * bias_tile + 1, bias_row : bias_row + 1, :]

    for copy in halo_copies + halo2_copies:
        copy.wait_send()
    drain(small_r1.at[pl.ds(0, PLANE - 1)], send_sems.at[0])
    drain(small_r2.at[pl.ds(0, DEPTH - 1)], send_sems.at[1])
    drain(ra_out.at[pl.ds(0, PLANE - 1)], send_sems.at[2])
    drain(ra_in.at[pl.ds(0, PLANE - 1)], send_sems.at[3])
    drain(small2_r1.at[pl.ds(0, PLANE - 1)], send_sems.at[4])
    drain(rz_out.at[pl.ds(0, DEPTH - 1)], send_sems.at[5])
    drain(rz_in.at[pl.ds(0, DEPTH - 1)], send_sems.at[6])
    drain(small2_r2.at[pl.ds(0, DEPTH - 1)], send_sems.at[7])
    drain(fin_out.at[pl.ds(0, PLANE - 1)], send_sems.at[8])
    drain(fin_in.at[pl.ds(0, PLANE - 1)], send_sems.at[9])


def shards(tracer, cotangent, land_mask, bottom, kappa, w_in, b_in, w_out, b_out):
    vmem = pl.BlockSpec(memory_space=pltpu.VMEM)
    smem = pl.BlockSpec(memory_space=pltpu.SMEM)
    anyw = pl.BlockSpec(memory_space=pl.ANY)
    slab = (ROWS, PAD, LANES)
    levels = (LEVELS, ROWS, LANES)

    def v(*shape, dtype=F32):
        return pltpu.VMEM(shape, dtype)

    scratch = [
        v(*levels), v(*levels), v(*slab), v(*slab),
        v(PAD, LANES), v(PAD, LANES), v(PAD, LANES), v(PAD, LANES),
        v(4, PAD, LANES), v(4, PAD, LANES), v(4 * ROWS, LANES),
        v(1, LANES), v(PLANE, 1, LANES), v(1, LANES), v(DEPTH, 1, LANES),
        v(1, 2 * LANES), v(PLANE, 1, 2 * LANES), v(1, 2 * LANES), v(DEPTH, 1, 2 * LANES),
        v(LANES, HIDDEN), v(HIDDEN, LANES), v(LANES, HIDDEN, dtype=BF16),
        v(HIDDEN, LANES, dtype=BF16), v(LANES, HIDDEN, dtype=BF16), v(HIDDEN, LANES, dtype=BF16),
        v(LANES, COLS, dtype=BF16), v(HIDDEN, COLS, dtype=BF16), v(HIDDEN, COLS),
        v(HIDDEN, COLS, dtype=BF16), v(LANES, COLS, dtype=BF16), v(*slab),
        v(*levels), v(*levels), v(*levels), v(*levels), v(LEVELS + 1, ROWS, LANES),
        v(*levels), v(*levels), v(*levels), v(LANES, ROWS, LANES),
        v(PLANE, 8, 256), v(PLANE, 16, LANES), v(PLANE, 8, 256), v(PLANE, 16, LANES),
        v(8, 256), v(16, LANES), v(DEPTH, 8, 256), v(DEPTH, 16, LANES),
        v(8, 256), v(16, LANES), v(PLANE, 8, 256), v(PLANE, 16, LANES),
        pltpu.SemaphoreType.DMA((2,)), pltpu.SemaphoreType.DMA((10,)),
        pltpu.SemaphoreType.DMA((10,)), pltpu.SemaphoreType.DMA((8,)),
        pltpu.SemaphoreType.DMA((8,)),
    ]
    out, gw_in, gb_in, gw_out, gb_out = pl.pallas_call(
        kernel,
        out_shape=(
            jax.ShapeDtypeStruct(tracer.shape, F32),
            jax.ShapeDtypeStruct((LEVELS, HIDDEN), F32),
            jax.ShapeDtypeStruct((1, HIDDEN), F32),
            jax.ShapeDtypeStruct((HIDDEN, LEVELS), F32),
            jax.ShapeDtypeStruct((1, LANES), F32),
        ),
        in_specs=[anyw, anyw, vmem, vmem, smem, vmem, vmem, vmem, smem],
        out_specs=(vmem,) * 5,
        scratch_shapes=scratch,
        compiler_params=pltpu.CompilerParams(
            collective_id=0, has_side_effects=True, vmem_limit_bytes=40 * 1024 * 1024
        ),
        name="step_adjoint",
    )(
        tracer, cotangent, land_mask, bottom, kappa, w_in, b_in.reshape(1, HIDDEN), w_out, b_out
    )
    return out, gw_in, gb_in[0], gw_out, gb_out[0, :LEVELS]


def solution(mesh):
    placed = (
        P(None, "lat", "lon"),
        P(None, "lat", "lon"),
        P("lat", "lon"),
        P("lat", "lon"),
        P(),
        P(),
        P(),
        P(),
        P(),
    )
    return jax.shard_map(
        shards,
        mesh=mesh,
        in_specs=placed,
        out_specs=(P(None, "lat", "lon"), P(), P(), P(), P()),
        check_vma=False,
    )
```

```python
import functools
import math

import jax
import jax.numpy as jnp
from jax import lax
from jax.experimental import pallas as pl
from jax.experimental.pallas import tpu as pltpu
from jax.sharding import PartitionSpec as P

MESH = pl.DeviceIdType.MESH
F32 = jnp.float32
BF16 = jnp.bfloat16

spread_coef = 0.15
level_eps = 1e-05

LEVELS = 100
ROWS = 8
LANES = 128
HIDDEN = 512
COLS = ROWS * LANES
PAD = 104
LAT = 8
LON = 32
SIDE = 4
CHIPS = SIDE * SIDE
PLANE = 2 * CHIPS
DEPTH = 8
HALF = HIDDEN // 2


def ring(d, n):
    return min(d, n - d)


CHIP_STEPS = sorted(
    ((dx, dy) for dx in range(SIDE) for dy in range(SIDE)),
    key=lambda s: -(ring(s[0], SIDE) + ring(s[1], SIDE)),
)
Z_STEPS = sorted(range(1, DEPTH), key=lambda d: -ring(d, DEPTH))


def kernel(
    tracer_hbm, cot_hbm, land_hbm, bottom_hbm, kappa_hbm, w_in_hbm, b_in_hbm, w_out_hbm, b_out_hbm,
    out_ref, gw_in_ref, gb_in_ref, gw_out_ref, gb_out_ref,
    tr_v, cot_v, land_v, bottom_v, kappa_s, w_in_v, b_in_v, w_out_v, b_out_s,
    slabs, adj_slabs, edge_hi, edge_lo, edge2_hi, edge2_lo, halo, halo2, near_depth,
    small_src, small_r1, small_mid, small_r2,
    small2_src, small2_r1, small2_mid, small2_r2,
    wi_f, wo_f, wi_b, w1t, wot, wo_b,
    inp, hid, slope, dpre, dlog, din,
    logit, mixed, val_x, val_y, mul_x, mul_y, gate, adj, dlev,
    grad, from_core, half, from_plane, mid, from_z, chunk, full,
    load_sems, small_send, small_recv, core_send, core_recv, plane_send, plane_recv,
    z_send, z_recv, gather_send, gather_recv, fwd_send, fwd_recv, halo_send, halo_recv,
):
    lat = lax.axis_index("lat")
    lon = lax.axis_index("lon")
    y_me = lat % SIDE
    x_me = (lat // SIDE) * 2 + lon // 16
    z_me = (lon // 2) % DEPTH
    core = lon % 2
    p_me = x_me * SIDE + y_me
    q_me = p_me * 2 + core
    lon_z = z_me * 2

    loads = []
    for n, (src, dst) in enumerate(
        (
            (tracer_hbm, tr_v), (land_hbm, land_v), (bottom_hbm, bottom_v), (w_in_hbm, w_in_v),
            (b_in_hbm, b_in_v), (w_out_hbm, w_out_v), (cot_hbm, cot_v), (kappa_hbm, kappa_s),
            (b_out_hbm, b_out_s),
        )
    ):
        load = pltpu.make_async_copy(src, dst, load_sems.at[n])
        load.start()
        loads.append(load)

    xs = [(x_me + d) % SIDE for d in range(SIDE)]
    ys = [(y_me + d) % SIDE for d in range(SIDE)]

    def chip_peer(dx, dy, dc):
        to_core = core if dc == 0 else 1 - core
        dev = ((xs[dx] // 2) * SIDE + ys[dy], (xs[dx] % 2) * 16 + lon_z + to_core)
        return xs[dx] * SIDE + ys[dy], dev

    def z_peer(d):
        return (lat, (lon // 16) * 16 + ((z_me + d) % DEPTH) * 2 + core)

    everyone = [(dx, dy, dc) for dx, dy in CHIP_STEPS for dc in (0, 1) if dx or dy or dc]
    same_core = [(dx, dy) for dx, dy in CHIP_STEPS if dx or dy]
    partner = (lat, lon + 1 - 2 * core)

    barrier = pltpu.get_barrier_semaphore()

    def greet(dev):
        pl.semaphore_signal(barrier, inc=1, device_id=dev, device_id_type=MESH)

    for step in everyone:
        greet(chip_peer(*step)[1])
    for d in Z_STEPS:
        greet(z_peer(d))
    greet((lat, (lon + 2 * core - 1 + LON) % LON))

    row_id = lax.broadcasted_iota(jnp.int32, (PAD, LANES), 0)
    lane_id = lax.broadcasted_iota(jnp.int32, (PAD, LANES), 1)
    row_f = row_id.astype(F32)
    diag = row_id == lane_id

    def as_row(column):
        return jnp.sum(jnp.where(diag, column, 0.0), axis=0, keepdims=True)

    def as_column(row):
        return jnp.sum(jnp.where(diag, row, 0.0), axis=1, keepdims=True)

    for n in range(3):
        loads[n].wait()
    depth_all = (land_v[...] * bottom_v[...]).astype(F32)
    energy = jnp.zeros((PAD, LANES), F32)
    hi = jnp.zeros((PAD, LANES), F32)
    lo = jnp.zeros((PAD, LANES), F32)
    for i in range(ROWS):
        slabs[i, 0:LEVELS, :] = tr_v[:, i, :]
        slabs[i, LEVELS:PAD, :] = jnp.broadcast_to(depth_all[i : i + 1, :], (PAD - LEVELS, LANES))
        x = slabs[i]
        wet_x = jnp.where(row_f < depth_all[i : i + 1, :], x, 0.0)
        energy = energy + wet_x * wet_x
        hi = jnp.where(lane_id == i, pltpu.roll(x, i + 1, 1), hi)
        lo = jnp.where(lane_id == i, pltpu.roll(x, i, 1) if i else x, lo)
    small_src[...] = as_row(jnp.sum(energy, axis=1, keepdims=True))
    small_r1[q_me] = small_src[...]
    edge_hi[...] = hi
    edge_lo[...] = lo

    pl.semaphore_wait(barrier, PLANE - 1 + DEPTH - 1 + 1)

    def post(src, dst, dev, send, recv):
        pltpu.make_async_remote_copy(
            src, dst, send, recv, device_id=dev, device_id_type=MESH
        ).start()

    def small_plane(src, dst, which):
        for step in everyone:
            post(src, dst.at[q_me], chip_peer(*step)[1], small_send.at[which], small_recv.at[which])

    def send_z(src, dst, send, recv):
        for d in Z_STEPS:
            post(src, dst.at[z_me], z_peer(d), send, recv)

    def drain(ref, sem):
        pltpu.make_async_copy(ref, ref, sem).wait()

    def send_halo(k, pieces, dst):
        up = (lat + 1) % LAT
        down = (lat + LAT - 1) % LAT
        right = (lon + 1) % LON
        left = (lon + LON - 1) % LON
        targets = ((up, lon), (down, lon), (lat, right), (lat, left))
        copies = []
        for n, (src, dev) in enumerate(zip(pieces, targets)):
            copy = pltpu.make_async_remote_copy(
                src, dst.at[n], halo_send.at[4 * k + n], halo_recv.at[4 * k + n],
                device_id=dev, device_id_type=MESH,
            )
            copy.start()
            copies.append(copy)
        return copies

    small_plane(small_src, small_r1, 0)
    halo_copies = send_halo(0, (slabs.at[ROWS - 1], slabs.at[0], edge_hi, edge_lo), halo)

    for n in range(3, 6):
        loads[n].wait()
    bias = b_in_v[...].reshape(1, HIDDEN)
    bias_hi = bias.astype(BF16).astype(F32)
    bias_mid = (bias - bias_hi).astype(BF16).astype(F32)
    bias_lo = bias - bias_hi - bias_mid
    wi_f[LEVELS:LANES, :] = jnp.zeros((LANES - LEVELS, HIDDEN), F32)
    wi_f[0:LEVELS, :] = w_in_v[...].astype(F32)
    wi_f[LEVELS : LEVELS + 1, :] = bias_hi
    wi_f[LEVELS + 1 : LEVELS + 2, :] = bias_mid
    wi_f[LEVELS + 2 : LEVELS + 3, :] = bias_lo
    wi_b[...] = wi_f[...].astype(BF16)
    w1t[...] = wi_f[...].T.astype(BF16)
    wo_f[LEVELS:LANES, :] = jnp.zeros((LANES - LEVELS, HIDDEN), F32)
    wo_f[0:LEVELS, :] = w_out_v[...].astype(F32)
    wot[...] = wo_f[...].astype(BF16)
    wo_b[...] = wo_f[...].T.astype(BF16)
    dlev[LEVELS:LANES] = jnp.zeros((LANES - LEVELS, ROWS, LANES), F32)
    for i in range(ROWS):
        adj_slabs[i, LEVELS:PAD, :] = jnp.zeros((PAD - LEVELS, LANES), F32)
    edge2_hi[LEVELS:PAD, :] = jnp.zeros((PAD - LEVELS, LANES), F32)
    edge2_lo[LEVELS:PAD, :] = jnp.zeros((PAD - LEVELS, LANES), F32)
    inp[PAD - 8 : LANES, :] = jnp.zeros((LANES - PAD + 8, COLS), BF16)
    for n in range(6, 9):
        loads[n].wait()

    drain(small_r1.at[pl.ds(0, PLANE - 1)], small_recv.at[0])
    small_mid[...] = jnp.sum(small_r1[...], axis=0)
    small_r2[z_me] = small_mid[...]
    send_z(small_mid, small_r2, small_send.at[1], small_recv.at[1])

    for copy in halo_copies:
        copy.wait_recv()

    def neighbours(field, edges, i):
        centre = field[i]
        below = field[i + 1] if i + 1 < ROWS else edges[1]
        above = field[i - 1] if i else edges[0]
        from_left = pltpu.roll(edges[2], LANES - i, 1) if i else edges[2]
        left = jnp.where(lane_id == 0, from_left, pltpu.roll(centre, 1, 1))
        right = jnp.where(
            lane_id == LANES - 1, pltpu.roll(edges[3], LANES - 1 - i, 1), pltpu.roll(centre, LANES - 1, 1)
        )
        return centre, (below, above, left, right)

    def flux(centre, near, i):
        total = jnp.zeros((PAD, LANES), F32)
        for n in range(4):
            total = total + jnp.where(
                row_f < near_depth[n * ROWS + i : n * ROWS + i + 1, :], near[n] - centre, 0.0
            )
        return centre + spread_coef * total

    has_above = jnp.where(lat > 0, 1.0, 0.0)
    has_below = jnp.where(lat < LAT - 1, 1.0, 0.0)
    for i in range(ROWS):
        centre, near = neighbours(slabs, halo, i)
        own = centre[LEVELS : LEVELS + 1, :]
        for n in range(4):
            other = near[n][LEVELS : LEVELS + 1, :]
            if n == 0 and i == ROWS - 1:
                other = other * has_below
            if n == 1 and i == 0:
                other = other * has_above
            near_depth[n * ROWS + i : n * ROWS + i + 1, :] = jnp.minimum(own, other)
        mixed[:, i, :] = flux(centre, near, i)[0:LEVELS]

    drain(small_r2.at[pl.ds(0, DEPTH - 1)], small_recv.at[1])
    energy_all = as_column(jnp.sum(small_r2[...], axis=0))
    count = float(LAT * LON * COLS)
    radius = jnp.sqrt(energy_all / count + level_eps)
    inv_radius = 1.0 / radius

    def wet_slab(i):
        x = slabs[i]
        return jnp.where(row_f < x[LEVELS : LEVELS + 1, :], x, 0.0)

    one_rows = jnp.where(row_id < LEVELS + 3, 1.0, 0.0)
    for i in range(ROWS):
        scaled = jnp.where(row_id < LEVELS, wet_slab(i) * inv_radius, one_rows)
        scaled = jnp.concatenate([scaled, jnp.zeros((LANES - PAD, LANES), F32)], axis=0)
        inp[:, i * LANES : (i + 1) * LANES] = scaled.astype(BF16)

    width = 256
    for j in range(COLS // width):
        cols = slice(j * width, (j + 1) * width)
        pre = jnp.dot(w1t[...], inp[:, cols], preferred_element_type=F32)
        sig = 1.0 / (1.0 + jnp.exp(-pre))
        act = pre * sig
        hid[:, cols] = act.astype(BF16)
        slope[:, cols] = sig * (1.0 + pre * (1.0 - sig))
        out = jnp.dot(wot[...], hid[:, cols], preferred_element_type=F32)
        for s in range(width // LANES):
            logit[:, j * (width // LANES) + s, :] = out[0:LEVELS, s * LANES : (s + 1) * LANES]

    depth = depth_all
    middle = LEVELS // 2

    def level_terms(k):
        x = logit[k] + b_out_s[k]
        ex = jnp.exp(-jnp.abs(x))
        soft = jnp.maximum(x, 0.0) + jnp.log1p(ex)
        sig = jnp.where(x >= 0.0, 1.0, ex) / (1.0 + ex)
        kf = (k + 1).astype(F32)
        open_face = kf < depth
        kap = kappa_s[k]
        down = jnp.where(open_face, kap + soft, 0.0)
        up = jnp.where(open_face, kap, 0.0)
        gate[k] = jnp.where(open_face, sig, 0.0)
        return down, up

    def eliminate(s, carry):
        down_p, up_p, r_p, v_p, w_p, sb_n, u_n, z_n = carry
        k = s
        down, up = level_terms(k)
        pivot = 1.0 + down + up_p - down_p * up_p * r_p
        r = 1.0 / pivot
        v = (mixed[k] + down_p * v_p) * r
        w = (cot_v[k] + up_p * w_p) * r
        val_x[k] = v
        val_y[k] = w
        mul_x[k] = up * r
        mul_y[k] = down * r
        b = LEVELS - 1 - s
        down_b, up_b = level_terms(b)
        up_above = jnp.where(b.astype(F32) < depth, kappa_s[b - 1], 0.0)
        pivot_b = 1.0 + down_b + up_above - down_b * up_b * sb_n
        sb = 1.0 / pivot_b
        u = (mixed[b] + up_b * u_n) * sb
        zz = (cot_v[b] + down_b * z_n) * sb
        val_x[b] = u
        val_y[b] = zz
        mul_y[b] = up_above * sb
        mul_x[b + 1] = down_b * sb_n
        return down, up, r, v, w, sb, u, zz

    zero = jnp.zeros((ROWS, LANES), F32)
    down_m, up_m, r_m, v_m, w_m, sb_m, u_m, z_m = lax.fori_loop(
        0, middle, eliminate, (zero,) * 8, unroll=5
    )
    ratio_x = up_m * r_m
    ratio_y = down_m * r_m
    back_x = down_m * sb_m
    back_y = up_m * sb_m
    inv_det = 1.0 / (1.0 - ratio_x * back_x)
    x_top = (v_m + ratio_x * u_m) * inv_det
    x_bot = u_m + back_x * x_top
    y_top = (w_m + ratio_y * z_m) * inv_det
    y_bot = z_m + back_y * y_top
    adj[middle - 1] = y_top
    adj[middle] = y_bot
    dlev[middle - 1] = gate[middle - 1] * x_top * (y_bot - y_top)

    def substitute(s, carry):
        x_t, y_t, x_b, y_b = carry
        k = middle - 1 - s
        x_n = val_x[k] + mul_x[k] * x_t
        y_n = val_y[k] + mul_y[k] * y_t
        adj[k] = y_n
        dlev[k] = gate[k] * x_n * (y_t - y_n)
        b = middle + s
        x_c = val_x[b] + mul_x[b] * x_b
        y_c = val_y[b] + mul_y[b] * y_b
        adj[b] = y_c
        dlev[b - 1] = gate[b - 1] * x_b * (y_c - y_b)
        return x_n, y_n, x_c, y_c

    lax.fori_loop(1, middle, substitute, (x_top, y_top, x_bot, y_bot), unroll=7)
    dlev[LEVELS - 1] = zero

    for i in range(ROWS):
        dlog[:, i * LANES : (i + 1) * LANES] = dlev[:, i, :].astype(BF16)
    contract_last = (((1,), (1,)), ((), ()))

    def share(m, value):
        for p in range(CHIPS):
            for c in range(2):
                grad[m, c, p] = value[8 * p : 8 * p + 8, c * HALF : (c + 1) * HALF]
        post(grad.at[m, 1 - core], from_core.at[m], partner, core_send.at[m], core_recv.at[m])

    share(0, lax.dot_general(dlog[...], hid[...], contract_last, preferred_element_type=F32))

    hi = jnp.zeros((LEVELS, LANES), F32)
    lo = jnp.zeros((LEVELS, LANES), F32)
    lane_l = lane_id[0:LEVELS]
    for i in range(ROWS):
        x = adj[:, i, :]
        adj_slabs[i, 0:LEVELS, :] = x
        hi = jnp.where(lane_l == i, pltpu.roll(x, i + 1, 1), hi)
        lo = jnp.where(lane_l == i, pltpu.roll(x, i, 1) if i else x, lo)
    edge2_hi[0:LEVELS, :] = hi
    edge2_lo[0:LEVELS, :] = lo

    for j in range(COLS // width):
        cols = slice(j * width, (j + 1) * width)
        back = jnp.dot(wo_b[...], dlog[:, cols], preferred_element_type=F32)
        dpre[:, cols] = (back * slope[:, cols]).astype(BF16)
    share(1, lax.dot_general(inp[...], dpre[...], contract_last, preferred_element_type=F32))

    def scatter(m):
        drain(from_core.at[m], core_recv.at[m])
        half[m] = grad[m, core] + from_core[m]
        from_plane[m, p_me] = half[m, p_me]
        for dx, dy in same_core:
            p, dev = chip_peer(dx, dy, 0)
            post(half.at[m, p], from_plane.at[m, p_me], dev, plane_send.at[m], plane_recv.at[m])

    scatter(0)
    bout_row = lax.dot_general(
        jnp.ones((16, COLS), BF16), dlog[...], contract_last, preferred_element_type=F32
    )[0:1]
    level = jnp.zeros((PAD, LANES), F32)
    for j in range(COLS // width):
        cols = slice(j * width, (j + 1) * width)
        out = jnp.dot(wi_b[...], dpre[:, cols], preferred_element_type=F32)
        for s in range(width // LANES):
            i = j * (width // LANES) + s
            part = out[0:PAD, s * LANES : (s + 1) * LANES]
            din[i] = part
            level = level + part * wet_slab(i)
    small2_src[:, 0:LANES] = as_row(jnp.sum(level, axis=1, keepdims=True))
    small2_src[:, LANES : 2 * LANES] = bout_row
    small2_r1[q_me] = small2_src[...]
    scatter(1)
    small_plane(small2_src, small2_r1, 2)
    halo2_copies = send_halo(
        1, (adj_slabs.at[ROWS - 1], adj_slabs.at[0], edge2_hi, edge2_lo), halo2
    )

    def through_z(m):
        drain(from_plane.at[m, pl.ds(0, CHIPS - 1)], plane_recv.at[m])
        mid[m] = jnp.sum(from_plane[m], axis=0)
        from_z[m, z_me] = mid[m]
        send_z(mid.at[m], from_z.at[m], z_send.at[m], z_recv.at[m])

    scale = 1.0 / math.sqrt(count)

    def gather(m):
        drain(from_z.at[m, pl.ds(0, DEPTH - 1)], z_recv.at[m])
        chunk[m] = jnp.sum(from_z[m], axis=0) * scale
        full[m, core, p_me] = chunk[m]
        for dx, dy in same_core:
            _, dev = chip_peer(dx, dy, 0)
            post(chunk.at[m], full.at[m, core, p_me], dev, gather_send.at[m], gather_recv.at[m])

    def forward(m):
        drain(full.at[m, core, pl.ds(0, CHIPS - 1)], gather_recv.at[m])
        post(full.at[m, core], full.at[m, core], partner, fwd_send.at[m], fwd_recv.at[m])

    through_z(0)
    through_z(1)
    drain(small2_r1.at[pl.ds(0, PLANE - 1)], small_recv.at[2])
    small2_mid[...] = jnp.sum(small2_r1[...], axis=0)
    small2_r2[z_me] = small2_mid[...]
    send_z(small2_mid, small2_r2, small_send.at[3], small_recv.at[3])
    for copy in halo2_copies:
        copy.wait_recv()
    for i in range(ROWS):
        centre, near = neighbours(adj_slabs, halo2, i)
        mix = flux(centre, near, i)
        wet = row_f < slabs[i, LEVELS : LEVELS + 1, :]
        din[i] = mix + jnp.where(wet, din[i] * inv_radius, 0.0)
    gather(0)
    gather(1)

    drain(small2_r2.at[pl.ds(0, DEPTH - 1)], small_recv.at[3])
    small2 = jnp.sum(small2_r2[...], axis=0)
    level_sum = as_column(small2[:, 0:LANES])
    gb_out_ref[...] = small2[:, LANES : 2 * LANES] * scale
    level_scale = level_sum / (count * radius * radius * radius)
    for i in range(ROWS):
        out_ref[:, i, :] = (din[i] - wet_slab(i) * level_scale)[0:LEVELS]

    forward(0)
    forward(1)

    def deliver(m, ref):
        drain(full.at[m, 1 - core], fwd_recv.at[m])
        for p in range(LEVELS // 8 + 1):
            rows = min(8, LEVELS - 8 * p)
            for c in range(2):
                ref[8 * p : 8 * p + rows, c * HALF : (c + 1) * HALF] = full[m, c, p, 0:rows, :]

    deliver(0, gw_out_ref)
    deliver(1, gw_in_ref)
    bias_tile, bias_row = LEVELS // 8, LEVELS % 8
    for c in range(2):
        gb_in_ref[:, c * HALF : (c + 1) * HALF] = full[1, c, bias_tile, bias_row : bias_row + 1, :]

    for copy in halo_copies + halo2_copies:
        copy.wait_send()
    for k, ref in enumerate((small_r1, small_r2, small2_r1, small2_r2)):
        drain(ref.at[pl.ds(0, ref.shape[0] - 1)], small_send.at[k])
    for m in range(2):
        drain(from_core.at[m], core_send.at[m])
        drain(from_plane.at[m, pl.ds(0, CHIPS - 1)], plane_send.at[m])
        drain(from_z.at[m, pl.ds(0, DEPTH - 1)], z_send.at[m])
        drain(full.at[m, core, pl.ds(0, CHIPS - 1)], gather_send.at[m])
        drain(full.at[m, core], fwd_send.at[m])


def store_results(out_v, gw_in_v, gb_in_v, gw_out_v, gb_out_v, out_h, gw_in_h, gb_in_ref, gw_out_h, gb_out_ref, sems):
    copies = []
    for n, (src, dst) in enumerate(((out_v, out_h), (gw_in_v, gw_in_h), (gw_out_v, gw_out_h))):
        copy = pltpu.make_async_copy(src, dst, sems.at[n])
        copy.start()
        copies.append(copy)
    gb_in_ref[...] = gb_in_v[...].reshape(HIDDEN)
    gb_out_ref[...] = gb_out_v[...].reshape(LANES)[0:LEVELS]
    for copy in copies:
        copy.wait()


def shards(tracer, cotangent, land_mask, bottom, kappa, w_in, b_in, w_out, b_out):
    vmem = pl.BlockSpec(memory_space=pltpu.VMEM)
    hbm = pl.BlockSpec(memory_space=pltpu.HBM)
    slab = (ROWS, PAD, LANES)
    levels = (LEVELS, ROWS, LANES)
    edge = (PAD, LANES)
    pieces = (CHIPS, 8, HALF)

    def v(*shape, dtype=F32):
        return pltpu.VMEM(shape, dtype)

    def sems(n):
        return pltpu.SemaphoreType.DMA((n,))

    scratch = [
        v(*levels), v(*levels), v(ROWS, LANES, dtype=jnp.int32), v(ROWS, LANES, dtype=jnp.int32),
        pltpu.SMEM((LEVELS,), F32), v(LEVELS, HIDDEN, dtype=BF16), v(HIDDEN),
        v(LEVELS, HIDDEN, dtype=BF16), pltpu.SMEM((LEVELS,), F32),
        v(*slab), v(*slab), v(*edge), v(*edge), v(*edge), v(*edge),
        v(4, *edge), v(4, *edge), v(4 * ROWS, LANES),
        v(1, LANES), v(PLANE, 1, LANES), v(1, LANES), v(DEPTH, 1, LANES),
        v(1, 2 * LANES), v(PLANE, 1, 2 * LANES), v(1, 2 * LANES), v(DEPTH, 1, 2 * LANES),
        v(LANES, HIDDEN), v(LANES, HIDDEN), v(LANES, HIDDEN, dtype=BF16),
        v(HIDDEN, LANES, dtype=BF16), v(LANES, HIDDEN, dtype=BF16), v(HIDDEN, LANES, dtype=BF16),
        v(LANES, COLS, dtype=BF16), v(HIDDEN, COLS, dtype=BF16), v(HIDDEN, COLS),
        v(HIDDEN, COLS, dtype=BF16), v(LANES, COLS, dtype=BF16), v(*slab),
        v(*levels), v(*levels), v(*levels), v(*levels), v(LEVELS + 1, ROWS, LANES),
        v(*levels), v(*levels), v(*levels), v(LANES, ROWS, LANES),
        v(2, 2, *pieces), v(2, *pieces), v(2, *pieces), v(2, *pieces), v(2, 8, HALF),
        v(2, DEPTH, 8, HALF), v(2, 8, HALF), v(2, 2, *pieces),
        sems(9), sems(4), sems(4), sems(2), sems(2), sems(2), sems(2),
        sems(2), sems(2), sems(2), sems(2), sems(2), sems(2), sems(8), sems(8),
    ]
    shapes = (
        jax.ShapeDtypeStruct(tracer.shape, F32),
        jax.ShapeDtypeStruct((LEVELS, HIDDEN), F32),
        jax.ShapeDtypeStruct((1, HIDDEN), F32),
        jax.ShapeDtypeStruct((LEVELS, HIDDEN), F32),
        jax.ShapeDtypeStruct((1, LANES), F32),
    )
    operands = (tracer, cotangent, land_mask, bottom, kappa, w_in, b_in, w_out.T, b_out)
    results = pl.pallas_call(
        kernel,
        out_shape=shapes,
        in_specs=[hbm] * 9,
        out_specs=(vmem,) * 5,
        scratch_shapes=scratch,
        compiler_params=pltpu.CompilerParams(
            collective_id=0, has_side_effects=True, vmem_limit_bytes=40 * 1024 * 1024
        ),
        name="step_adjoint",
    )(*(pltpu.with_memory_space_constraint(a, pltpu.HBM) for a in operands))
    out, gw_in, gb_in, gw_out, gb_out = pl.pallas_call(
        store_results,
        out_shape=shapes[:2]
        + (jax.ShapeDtypeStruct((HIDDEN,), F32), shapes[3], jax.ShapeDtypeStruct((LEVELS,), F32)),
        in_specs=[vmem] * 5,
        out_specs=(hbm, hbm, vmem, hbm, vmem),
        scratch_shapes=[sems(3)],
        compiler_params=pltpu.CompilerParams(vmem_limit_bytes=1024 * 1024),
        name="store_results",
    )(*results)
    return out, gw_in, gb_in, gw_out.T, gb_out


def solution(mesh):
    placed = (
        P(None, "lat", "lon"),
        P(None, "lat", "lon"),
        P("lat", "lon"),
        P("lat", "lon"),
        P(),
        P(),
        P(),
        P(),
        P(),
    )
    return jax.shard_map(
        shards,
        mesh=mesh,
        in_specs=placed,
        out_specs=(P(None, "lat", "lon"), P(), P(), P(), P()),
        check_vma=False,
    )
```

```python
import functools
import math

import jax
import jax.numpy as jnp
from jax import lax
from jax.experimental import pallas as pl
from jax.experimental.pallas import tpu as pltpu
from jax.sharding import PartitionSpec as P

MESH = pl.DeviceIdType.MESH
F32 = jnp.float32
BF16 = jnp.bfloat16

spread_coef = 0.15
level_eps = 1e-05

LEVELS = 100
ROWS = 8
LANES = 128
HIDDEN = 512
COLS = ROWS * LANES
PAD = 104
LAT = 8
LON = 32
SIDE = 4
CHIPS = SIDE * SIDE
PLANE = 2 * CHIPS
DEPTH = 8
HALF = HIDDEN // 2


def ring(d, n):
    return min(d, n - d)


CHIP_STEPS = sorted(
    ((dx, dy) for dx in range(SIDE) for dy in range(SIDE)),
    key=lambda s: -(ring(s[0], SIDE) + ring(s[1], SIDE)),
)
Z_STEPS = sorted(range(1, DEPTH), key=lambda d: -ring(d, DEPTH))


def kernel(
    tracer_hbm, cot_hbm, land_hbm, bottom_hbm, kappa_hbm, w_in_hbm, b_in_hbm, w_out_hbm, b_out_hbm,
    out_ref, gw_in_ref, gb_in_ref, gw_out_ref, gb_out_ref,
    tr_v, cot_v, land_v, bottom_v, kappa_s, w_in_v, b_in_v, w_out_v, b_out_s,
    slabs, adj_slabs, edge_hi, edge_lo, edge2_hi, edge2_lo, halo, halo2, near_depth,
    small_src, small_r1, small_mid, small_r2,
    rows_src, rows_in,
    wi_f, wo_f, wi_b, w1t, wot, wo_b,
    inp, hid, slope, dpre, dlog, din,
    logit, mixed, val_x, val_y, mul_x, mul_y, gate, adj, dlev,
    grad, from_core, half, from_plane, mid, from_z, chunk, full,
    load_sems, small_send, small_recv, core_send, core_recv, plane_send, plane_recv,
    z_send, z_recv, gather_send, gather_recv, fwd_send, fwd_recv, halo_send, halo_recv,
):
    lat = lax.axis_index("lat")
    lon = lax.axis_index("lon")
    y_me = lat % SIDE
    x_me = (lat // SIDE) * 2 + lon // 16
    z_me = (lon // 2) % DEPTH
    core = lon % 2
    p_me = x_me * SIDE + y_me
    q_me = p_me * 2 + core
    lon_z = z_me * 2

    loads = []
    for n, (src, dst) in enumerate(
        (
            (tracer_hbm, tr_v), (land_hbm, land_v), (bottom_hbm, bottom_v), (w_in_hbm, w_in_v),
            (b_in_hbm, b_in_v), (w_out_hbm, w_out_v), (cot_hbm, cot_v), (kappa_hbm, kappa_s),
            (b_out_hbm, b_out_s),
        )
    ):
        loads.append(pltpu.make_async_copy(src, dst, load_sems.at[n]))
    for load in loads[:3]:
        load.start()

    xs = [(x_me + d) % SIDE for d in range(SIDE)]
    ys = [(y_me + d) % SIDE for d in range(SIDE)]

    def chip_peer(dx, dy, dc):
        to_core = core if dc == 0 else 1 - core
        dev = ((xs[dx] // 2) * SIDE + ys[dy], (xs[dx] % 2) * 16 + lon_z + to_core)
        return xs[dx] * SIDE + ys[dy], dev

    def z_peer(d):
        return (lat, (lon // 16) * 16 + ((z_me + d) % DEPTH) * 2 + core)

    everyone = [(dx, dy, dc) for dx, dy in CHIP_STEPS for dc in (0, 1) if dx or dy or dc]
    same_core = [(dx, dy) for dx, dy in CHIP_STEPS if dx or dy]
    partner = (lat, lon + 1 - 2 * core)

    barrier = pltpu.get_barrier_semaphore()

    def greet(dev):
        pl.semaphore_signal(barrier, inc=1, device_id=dev, device_id_type=MESH)

    greet(z_peer(Z_STEPS[0]))
    for step in everyone:
        greet(chip_peer(*step)[1])
    for d in Z_STEPS[1:]:
        greet(z_peer(d))
    greet((lat, (lon + 2 * core - 1 + LON) % LON))
    for load in loads[3:]:
        load.start()

    row_id = lax.broadcasted_iota(jnp.int32, (PAD, LANES), 0)
    lane_id = lax.broadcasted_iota(jnp.int32, (PAD, LANES), 1)
    row_f = row_id.astype(F32)
    diag = row_id == lane_id

    def as_row(column):
        return jnp.sum(jnp.where(diag, column, 0.0), axis=0, keepdims=True)

    def as_column(row):
        return jnp.sum(jnp.where(diag, row, 0.0), axis=1, keepdims=True)

    for n in range(3):
        loads[n].wait()
    depth_all = (land_v[...] * bottom_v[...]).astype(F32)
    energy = jnp.zeros((PAD, LANES), F32)
    for i in range(ROWS):
        slabs[i, 0:LEVELS, :] = tr_v[:, i, :]
        slabs[i, LEVELS:PAD, :] = jnp.broadcast_to(depth_all[i : i + 1, :], (PAD - LEVELS, LANES))
        wet_x = jnp.where(row_f < depth_all[i : i + 1, :], slabs[i], 0.0)
        energy = energy + wet_x * wet_x
    small_src[...] = as_row(jnp.sum(energy, axis=1, keepdims=True))
    small_r1[q_me] = small_src[...]

    pl.semaphore_wait(barrier, PLANE - 1 + DEPTH - 1 + 1)

    def post(src, dst, dev, send, recv):
        pltpu.make_async_remote_copy(
            src, dst, send, recv, device_id=dev, device_id_type=MESH
        ).start()

    def send_z(src, dst, send, recv):
        for d in Z_STEPS:
            post(src, dst.at[z_me], z_peer(d), send, recv)

    def drain(ref, sem):
        pltpu.make_async_copy(ref, ref, sem).wait()

    def send_halo(k, pieces, dst):
        up = (lat + 1) % LAT
        down = (lat + LAT - 1) % LAT
        right = (lon + 1) % LON
        left = (lon + LON - 1) % LON
        targets = ((up, lon), (down, lon), (lat, right), (lat, left))
        copies = []
        for n, (src, dev) in enumerate(zip(pieces, targets)):
            copy = pltpu.make_async_remote_copy(
                src, dst.at[n], halo_send.at[4 * k + n], halo_recv.at[4 * k + n],
                device_id=dev, device_id_type=MESH,
            )
            copy.start()
            copies.append(copy)
        return copies

    for step in everyone:
        post(small_src, small_r1.at[q_me], chip_peer(*step)[1], small_send.at[0], small_recv.at[0])
    hi = jnp.zeros((PAD, LANES), F32)
    lo = jnp.zeros((PAD, LANES), F32)
    for i in range(ROWS):
        x = slabs[i]
        hi = jnp.where(lane_id == i, pltpu.roll(x, i + 1, 1), hi)
        lo = jnp.where(lane_id == i, pltpu.roll(x, i, 1) if i else x, lo)
    edge_hi[...] = hi
    edge_lo[...] = lo
    halo_copies = send_halo(0, (slabs.at[ROWS - 1], slabs.at[0], edge_hi, edge_lo), halo)

    for n in range(3, 6):
        loads[n].wait()
    bias = b_in_v[...].reshape(1, HIDDEN)
    bias_hi = bias.astype(BF16).astype(F32)
    bias_mid = (bias - bias_hi).astype(BF16).astype(F32)
    bias_lo = bias - bias_hi - bias_mid
    wi_f[LEVELS:LANES, :] = jnp.zeros((LANES - LEVELS, HIDDEN), F32)
    wi_f[0:LEVELS, :] = w_in_v[...].astype(F32)
    wi_f[LEVELS : LEVELS + 1, :] = bias_hi
    wi_f[LEVELS + 1 : LEVELS + 2, :] = bias_mid
    wi_f[LEVELS + 2 : LEVELS + 3, :] = bias_lo
    wi_b[...] = wi_f[...].astype(BF16)
    w1t[...] = wi_f[...].T.astype(BF16)
    wo_f[LEVELS:LANES, :] = jnp.zeros((LANES - LEVELS, HIDDEN), F32)
    wo_f[0:LEVELS, :] = w_out_v[...].astype(F32)
    wot[...] = wo_f[...].astype(BF16)
    wo_b[...] = wo_f[...].T.astype(BF16)
    dlev[LEVELS:LANES] = jnp.zeros((LANES - LEVELS, ROWS, LANES), F32)
    for i in range(ROWS):
        adj_slabs[i, LEVELS:PAD, :] = jnp.zeros((PAD - LEVELS, LANES), F32)
    edge2_hi[LEVELS:PAD, :] = jnp.zeros((PAD - LEVELS, LANES), F32)
    edge2_lo[LEVELS:PAD, :] = jnp.zeros((PAD - LEVELS, LANES), F32)
    inp[PAD - 8 : LANES, :] = jnp.zeros((LANES - PAD + 8, COLS), BF16)
    for n in range(6, 9):
        loads[n].wait()

    drain(small_r1.at[pl.ds(0, PLANE - 1)], small_recv.at[0])
    small_mid[...] = jnp.sum(small_r1[...], axis=0)
    small_r2[z_me] = small_mid[...]
    send_z(small_mid, small_r2, small_send.at[1], small_recv.at[1])

    for copy in halo_copies:
        copy.wait_recv()

    def neighbours(field, edges, i):
        centre = field[i]
        below = field[i + 1] if i + 1 < ROWS else edges[1]
        above = field[i - 1] if i else edges[0]
        from_left = pltpu.roll(edges[2], LANES - i, 1) if i else edges[2]
        left = jnp.where(lane_id == 0, from_left, pltpu.roll(centre, 1, 1))
        right = jnp.where(
            lane_id == LANES - 1, pltpu.roll(edges[3], LANES - 1 - i, 1), pltpu.roll(centre, LANES - 1, 1)
        )
        return centre, (below, above, left, right)

    def flux(centre, near, i):
        total = jnp.zeros((PAD, LANES), F32)
        for n in range(4):
            total = total + jnp.where(
                row_f < near_depth[n * ROWS + i : n * ROWS + i + 1, :], near[n] - centre, 0.0
            )
        return centre + spread_coef * total

    has_above = jnp.where(lat > 0, 1.0, 0.0)
    has_below = jnp.where(lat < LAT - 1, 1.0, 0.0)
    for i in range(ROWS):
        centre, near = neighbours(slabs, halo, i)
        own = centre[LEVELS : LEVELS + 1, :]
        for n in range(4):
            other = near[n][LEVELS : LEVELS + 1, :]
            if n == 0 and i == ROWS - 1:
                other = other * has_below
            if n == 1 and i == 0:
                other = other * has_above
            near_depth[n * ROWS + i : n * ROWS + i + 1, :] = jnp.minimum(own, other)
        mixed[:, i, :] = flux(centre, near, i)[0:LEVELS]

    drain(small_r2.at[pl.ds(0, DEPTH - 1)], small_recv.at[1])
    energy_all = as_column(jnp.sum(small_r2[...], axis=0))
    count = float(LAT * LON * COLS)
    radius = jnp.sqrt(energy_all / count + level_eps)
    inv_radius = 1.0 / radius

    def wet_slab(i):
        x = slabs[i]
        return jnp.where(row_f < x[LEVELS : LEVELS + 1, :], x, 0.0)

    one_rows = jnp.where(row_id < LEVELS + 3, 1.0, 0.0)
    for i in range(ROWS):
        scaled = jnp.where(row_id < LEVELS, wet_slab(i) * inv_radius, one_rows)
        scaled = jnp.concatenate([scaled, jnp.zeros((LANES - PAD, LANES), F32)], axis=0)
        inp[:, i * LANES : (i + 1) * LANES] = scaled.astype(BF16)

    width = 256
    for j in range(COLS // width):
        cols = slice(j * width, (j + 1) * width)
        pre = jnp.dot(w1t[...], inp[:, cols], preferred_element_type=F32)
        sig = 1.0 / (1.0 + jnp.exp(-pre))
        act = pre * sig
        hid[:, cols] = act.astype(BF16)
        slope[:, cols] = sig * (1.0 + pre * (1.0 - sig))
        out = jnp.dot(wot[...], hid[:, cols], preferred_element_type=F32)
        for s in range(width // LANES):
            logit[:, j * (width // LANES) + s, :] = out[0:LEVELS, s * LANES : (s + 1) * LANES]

    depth = depth_all
    middle = LEVELS // 2

    def level_terms(k):
        x = logit[k] + b_out_s[k]
        ex = jnp.exp(-jnp.abs(x))
        soft = jnp.maximum(x, 0.0) + jnp.log1p(ex)
        sig = jnp.where(x >= 0.0, 1.0, ex) / (1.0 + ex)
        kf = (k + 1).astype(F32)
        open_face = kf < depth
        kap = kappa_s[k]
        down = jnp.where(open_face, kap + soft, 0.0)
        up = jnp.where(open_face, kap, 0.0)
        gate[k] = jnp.where(open_face, sig, 0.0)
        return down, up

    def eliminate(s, carry):
        down_p, up_p, r_p, v_p, w_p, sb_n, u_n, z_n = carry
        k = s
        down, up = level_terms(k)
        pivot = 1.0 + down + up_p - down_p * up_p * r_p
        r = 1.0 / pivot
        v = (mixed[k] + down_p * v_p) * r
        w = (cot_v[k] + up_p * w_p) * r
        val_x[k] = v
        val_y[k] = w
        mul_x[k] = up * r
        mul_y[k] = down * r
        b = LEVELS - 1 - s
        down_b, up_b = level_terms(b)
        up_above = jnp.where(b.astype(F32) < depth, kappa_s[b - 1], 0.0)
        pivot_b = 1.0 + down_b + up_above - down_b * up_b * sb_n
        sb = 1.0 / pivot_b
        u = (mixed[b] + up_b * u_n) * sb
        zz = (cot_v[b] + down_b * z_n) * sb
        val_x[b] = u
        val_y[b] = zz
        mul_y[b] = up_above * sb
        mul_x[b + 1] = down_b * sb_n
        return down, up, r, v, w, sb, u, zz

    zero = jnp.zeros((ROWS, LANES), F32)
    down_m, up_m, r_m, v_m, w_m, sb_m, u_m, z_m = lax.fori_loop(
        0, middle, eliminate, (zero,) * 8, unroll=5
    )
    ratio_x = up_m * r_m
    ratio_y = down_m * r_m
    back_x = down_m * sb_m
    back_y = up_m * sb_m
    inv_det = 1.0 / (1.0 - ratio_x * back_x)
    x_top = (v_m + ratio_x * u_m) * inv_det
    x_bot = u_m + back_x * x_top
    y_top = (w_m + ratio_y * z_m) * inv_det
    y_bot = z_m + back_y * y_top
    adj[middle - 1] = y_top
    adj[middle] = y_bot
    dlev[middle - 1] = gate[middle - 1] * x_top * (y_bot - y_top)

    def substitute(s, carry):
        x_t, y_t, x_b, y_b = carry
        k = middle - 1 - s
        x_n = val_x[k] + mul_x[k] * x_t
        y_n = val_y[k] + mul_y[k] * y_t
        adj[k] = y_n
        dlev[k] = gate[k] * x_n * (y_t - y_n)
        b = middle + s
        x_c = val_x[b] + mul_x[b] * x_b
        y_c = val_y[b] + mul_y[b] * y_b
        adj[b] = y_c
        dlev[b - 1] = gate[b - 1] * x_b * (y_c - y_b)
        return x_n, y_n, x_c, y_c

    lax.fori_loop(1, middle, substitute, (x_top, y_top, x_bot, y_bot), unroll=7)
    dlev[LEVELS - 1] = zero

    for i in range(ROWS):
        dlog[:, i * LANES : (i + 1) * LANES] = dlev[:, i, :].astype(BF16)
    contract_last = (((1,), (1,)), ((), ()))

    def share(m, value):
        for p in range(CHIPS):
            for c in range(2):
                grad[m, c, p] = value[8 * p : 8 * p + 8, c * HALF : (c + 1) * HALF]
        post(grad.at[m, 1 - core], from_core.at[m], partner, core_send.at[m], core_recv.at[m])

    share(0, lax.dot_general(dlog[...], hid[...], contract_last, preferred_element_type=F32))

    hi = jnp.zeros((LEVELS, LANES), F32)
    lo = jnp.zeros((LEVELS, LANES), F32)
    lane_l = lane_id[0:LEVELS]
    for i in range(ROWS):
        x = adj[:, i, :]
        adj_slabs[i, 0:LEVELS, :] = x
        hi = jnp.where(lane_l == i, pltpu.roll(x, i + 1, 1), hi)
        lo = jnp.where(lane_l == i, pltpu.roll(x, i, 1) if i else x, lo)
    edge2_hi[0:LEVELS, :] = hi
    edge2_lo[0:LEVELS, :] = lo
    halo2_copies = send_halo(
        1, (adj_slabs.at[ROWS - 1], adj_slabs.at[0], edge2_hi, edge2_lo), halo2
    )

    for j in range(COLS // width):
        cols = slice(j * width, (j + 1) * width)
        back = jnp.dot(wo_b[...], dlog[:, cols], preferred_element_type=F32)
        dpre[:, cols] = (back * slope[:, cols]).astype(BF16)
    share(1, lax.dot_general(inp[...], dpre[...], contract_last, preferred_element_type=F32))

    bout_row = lax.dot_general(
        jnp.ones((16, COLS), BF16), dlog[...], contract_last, preferred_element_type=F32
    )[0:1]
    level = jnp.zeros((PAD, LANES), F32)
    for j in range(COLS // width):
        cols = slice(j * width, (j + 1) * width)
        out = jnp.dot(wi_b[...], dpre[:, cols], preferred_element_type=F32)
        for s in range(width // LANES):
            i = j * (width // LANES) + s
            part = out[0:PAD, s * LANES : (s + 1) * LANES]
            din[i] = part
            level = level + part * wet_slab(i)
    rows_src[:, 0:LANES] = as_row(jnp.sum(level, axis=1, keepdims=True))
    rows_src[:, LANES : 2 * LANES] = bout_row
    post(rows_src, rows_in, partner, core_send.at[2], core_recv.at[2])
    for m in range(2):
        drain(from_core.at[m], core_recv.at[m])
        half[:, m] = grad[m, core] + from_core[m]
    drain(rows_in, core_recv.at[2])
    both_rows = rows_src[...] + rows_in[...]
    tile, first = LEVELS // 8, LEVELS % 8
    half[tile, 1, first + 1 : first + 2, 0:LANES] = both_rows[:, 0:LANES]
    half[tile, 1, first + 2 : first + 3, 0:LANES] = both_rows[:, LANES : 2 * LANES]
    from_plane[p_me] = half[p_me]
    for dx, dy in same_core:
        p, dev = chip_peer(dx, dy, 0)
        post(half.at[p], from_plane.at[p_me], dev, plane_send.at[0], plane_recv.at[0])

    for copy in halo2_copies:
        copy.wait_recv()
    for i in range(ROWS):
        centre, near = neighbours(adj_slabs, halo2, i)
        mix = flux(centre, near, i)
        wet = row_f < slabs[i, LEVELS : LEVELS + 1, :]
        din[i] = mix + jnp.where(wet, din[i] * inv_radius, 0.0)

    drain(from_plane.at[pl.ds(0, CHIPS - 1)], plane_recv.at[0])
    mid[...] = jnp.sum(from_plane[...], axis=0)
    from_z[z_me] = mid[...]
    send_z(mid, from_z, z_send.at[0], z_recv.at[0])
    scale = 1.0 / math.sqrt(count)
    drain(from_z.at[pl.ds(0, DEPTH - 1)], z_recv.at[0])
    chunk[...] = jnp.sum(from_z[...], axis=0) * scale
    full[core, p_me] = chunk[...]
    for dx, dy in same_core:
        _, dev = chip_peer(dx, dy, 0)
        post(chunk, full.at[core, p_me], dev, gather_send.at[0], gather_recv.at[0])
    drain(full.at[core, pl.ds(0, CHIPS - 1)], gather_recv.at[0])
    post(full.at[core], full.at[core], partner, fwd_send.at[0], fwd_recv.at[0])

    level_sum = as_column(full[core, tile, 1, first + 1 : first + 2, 0:LANES]) * math.sqrt(count)
    gb_out_ref[...] = full[core, tile, 1, first + 2 : first + 3, 0:LANES]
    level_scale = level_sum / (count * radius * radius * radius)
    for i in range(ROWS):
        out_ref[:, i, :] = (din[i] - wet_slab(i) * level_scale)[0:LEVELS]

    drain(full.at[1 - core], fwd_recv.at[0])
    for m, ref in enumerate((gw_out_ref, gw_in_ref)):
        for p in range(LEVELS // 8 + 1):
            rows = min(8, LEVELS - 8 * p)
            for c in range(2):
                ref[8 * p : 8 * p + rows, c * HALF : (c + 1) * HALF] = full[c, p, m, 0:rows, :]
    for c in range(2):
        gb_in_ref[:, c * HALF : (c + 1) * HALF] = full[c, tile, 1, first : first + 1, :]

    for copy in halo_copies + halo2_copies:
        copy.wait_send()
    drain(small_r1.at[pl.ds(0, PLANE - 1)], small_send.at[0])
    drain(small_r2.at[pl.ds(0, DEPTH - 1)], small_send.at[1])
    for m in range(2):
        drain(from_core.at[m], core_send.at[m])
    drain(rows_in, core_send.at[2])
    drain(from_plane.at[pl.ds(0, CHIPS - 1)], plane_send.at[0])
    drain(from_z.at[pl.ds(0, DEPTH - 1)], z_send.at[0])
    drain(full.at[core, pl.ds(0, CHIPS - 1)], gather_send.at[0])
    drain(full.at[core], fwd_send.at[0])


def store_results(out_v, gw_in_v, gb_in_v, gw_out_v, gb_out_v, out_h, gw_in_h, gb_in_ref, gw_out_h, gb_out_ref, sems):
    copies = []
    for n, (src, dst) in enumerate(((out_v, out_h), (gw_in_v, gw_in_h), (gw_out_v, gw_out_h))):
        copy = pltpu.make_async_copy(src, dst, sems.at[n])
        copy.start()
        copies.append(copy)
    gb_in_ref[...] = gb_in_v[...].reshape(HIDDEN)
    gb_out_ref[...] = gb_out_v[...].reshape(LANES)[0:LEVELS]
    for copy in copies:
        copy.wait()


def shards(tracer, cotangent, land_mask, bottom, kappa, w_in, b_in, w_out, b_out):
    vmem = pl.BlockSpec(memory_space=pltpu.VMEM)
    hbm = pl.BlockSpec(memory_space=pltpu.HBM)
    slab = (ROWS, PAD, LANES)
    levels = (LEVELS, ROWS, LANES)
    edge = (PAD, LANES)
    pieces = (CHIPS, 8, HALF)
    pair = (2, 8, HALF)

    def v(*shape, dtype=F32):
        return pltpu.VMEM(shape, dtype)

    def sems(n):
        return pltpu.SemaphoreType.DMA((n,))

    scratch = [
        v(*levels), v(*levels), v(ROWS, LANES, dtype=jnp.int32), v(ROWS, LANES, dtype=jnp.int32),
        pltpu.SMEM((LEVELS,), F32), v(LEVELS, HIDDEN, dtype=BF16), v(HIDDEN),
        v(LEVELS, HIDDEN, dtype=BF16), pltpu.SMEM((LEVELS,), F32),
        v(*slab), v(*slab), v(*edge), v(*edge), v(*edge), v(*edge),
        v(4, *edge), v(4, *edge), v(4 * ROWS, LANES),
        v(1, LANES), v(PLANE, 1, LANES), v(1, LANES), v(DEPTH, 1, LANES),
        v(1, 2 * LANES), v(1, 2 * LANES),
        v(LANES, HIDDEN), v(LANES, HIDDEN), v(LANES, HIDDEN, dtype=BF16),
        v(HIDDEN, LANES, dtype=BF16), v(LANES, HIDDEN, dtype=BF16), v(HIDDEN, LANES, dtype=BF16),
        v(LANES, COLS, dtype=BF16), v(HIDDEN, COLS, dtype=BF16), v(HIDDEN, COLS),
        v(HIDDEN, COLS, dtype=BF16), v(LANES, COLS, dtype=BF16), v(*slab),
        v(*levels), v(*levels), v(*levels), v(*levels), v(LEVELS + 1, ROWS, LANES),
        v(*levels), v(*levels), v(*levels), v(LANES, ROWS, LANES),
        v(2, 2, *pieces), v(2, *pieces), v(CHIPS, *pair), v(CHIPS, *pair), v(*pair),
        v(DEPTH, *pair), v(*pair), v(2, CHIPS, *pair),
        sems(9), sems(2), sems(2), sems(3), sems(3), sems(1), sems(1),
        sems(1), sems(1), sems(1), sems(1), sems(1), sems(1), sems(8), sems(8),
    ]
    shapes = (
        jax.ShapeDtypeStruct(tracer.shape, F32),
        jax.ShapeDtypeStruct((LEVELS, HIDDEN), F32),
        jax.ShapeDtypeStruct((1, HIDDEN), F32),
        jax.ShapeDtypeStruct((LEVELS, HIDDEN), F32),
        jax.ShapeDtypeStruct((1, LANES), F32),
    )
    operands = (tracer, cotangent, land_mask, bottom, kappa, w_in, b_in, w_out.T, b_out)
    results = pl.pallas_call(
        kernel,
        out_shape=shapes,
        in_specs=[hbm] * 9,
        out_specs=(vmem,) * 5,
        scratch_shapes=scratch,
        compiler_params=pltpu.CompilerParams(
            collective_id=0, has_side_effects=True, vmem_limit_bytes=40 * 1024 * 1024
        ),
        name="step_adjoint",
    )(*(pltpu.with_memory_space_constraint(a, pltpu.HBM) for a in operands))
    out, gw_in, gb_in, gw_out, gb_out = pl.pallas_call(
        store_results,
        out_shape=shapes[:2]
        + (jax.ShapeDtypeStruct((HIDDEN,), F32), shapes[3], jax.ShapeDtypeStruct((LEVELS,), F32)),
        in_specs=[vmem] * 5,
        out_specs=(hbm, hbm, vmem, hbm, vmem),
        scratch_shapes=[sems(3)],
        compiler_params=pltpu.CompilerParams(vmem_limit_bytes=1024 * 1024),
        name="store_results",
    )(*results)
    return out, gw_in, gb_in, gw_out.T, gb_out


def solution(mesh):
    placed = (
        P(None, "lat", "lon"),
        P(None, "lat", "lon"),
        P("lat", "lon"),
        P("lat", "lon"),
        P(),
        P(),
        P(),
        P(),
        P(),
    )
    return jax.shard_map(
        shards,
        mesh=mesh,
        in_specs=placed,
        out_specs=(P(None, "lat", "lon"), P(), P(), P(), P()),
        check_vma=False,
    )
```

```python
import functools
import math

import jax
import jax.numpy as jnp
from jax import lax
from jax.experimental import pallas as pl
from jax.experimental.pallas import tpu as pltpu
from jax.sharding import PartitionSpec as P

MESH = pl.DeviceIdType.MESH
F32 = jnp.float32
BF16 = jnp.bfloat16

spread_coef = 0.15
level_eps = 1e-05

LEVELS = 100
ROWS = 8
LANES = 128
HIDDEN = 512
COLS = ROWS * LANES
PAD = 104
LAT = 8
LON = 32
SIDE = 4
CHIPS = SIDE * SIDE
PLANE = 2 * CHIPS
DEPTH = 8
HALF = HIDDEN // 2


def ring(d, n):
    return min(d, n - d)


CHIP_STEPS = sorted(
    ((dx, dy) for dx in range(SIDE) for dy in range(SIDE)),
    key=lambda s: -(ring(s[0], SIDE) + ring(s[1], SIDE)),
)
Z_STEPS = sorted(range(1, DEPTH), key=lambda d: -ring(d, DEPTH))


def kernel(
    tracer_hbm, cot_hbm, land_hbm, bottom_hbm, kappa_hbm, w_in_hbm, b_in_hbm, w_out_hbm, b_out_hbm,
    out_ref, gw_in_ref, gb_in_ref, gw_out_ref, gb_out_ref,
    tr_v, cot_v, land_v, bottom_v, kappa_s, w_in_v, b_in_v, w_out_v, b_out_s,
    slabs, adj_slabs, edge_hi, edge_lo, edge2_hi, edge2_lo, halo, halo2, near_depth,
    small_src, small_r1, small_mid, small_r2,
    rows_in,
    wi_f, wo_f, wi_b, w1t, wot, wo_b,
    inp, hid, slope, dpre, dlog, din,
    logit, mixed, val_x, val_y, mul_x, mul_y, gate, adj, dlev,
    grad, from_core, half, from_plane, mid, from_z, chunk, full,
    load_sems, small_send, small_recv, core_send, core_recv, plane_send, plane_recv,
    z_send, z_recv, gather_send, gather_recv, fwd_send, fwd_recv, halo_send, halo_recv,
):
    lat = lax.axis_index("lat")
    lon = lax.axis_index("lon")
    y_me = lat % SIDE
    x_me = (lat // SIDE) * 2 + lon // 16
    z_me = (lon // 2) % DEPTH
    core = lon % 2
    p_me = x_me * SIDE + y_me
    q_me = p_me * 2 + core
    lon_z = z_me * 2

    loads = []
    for n, (src, dst) in enumerate(
        (
            (tracer_hbm, tr_v), (land_hbm, land_v), (bottom_hbm, bottom_v), (w_in_hbm, w_in_v),
            (b_in_hbm, b_in_v), (w_out_hbm, w_out_v), (cot_hbm, cot_v), (kappa_hbm, kappa_s),
            (b_out_hbm, b_out_s),
        )
    ):
        loads.append(pltpu.make_async_copy(src, dst, load_sems.at[n]))
    for load in loads[:3]:
        load.start()

    xs = [(x_me + d) % SIDE for d in range(SIDE)]
    ys = [(y_me + d) % SIDE for d in range(SIDE)]

    def chip_peer(dx, dy, dc):
        to_core = core if dc == 0 else 1 - core
        dev = ((xs[dx] // 2) * SIDE + ys[dy], (xs[dx] % 2) * 16 + lon_z + to_core)
        return xs[dx] * SIDE + ys[dy], dev

    def z_peer(d):
        return (lat, (lon // 16) * 16 + ((z_me + d) % DEPTH) * 2 + core)

    everyone = [(dx, dy, dc) for dx, dy in CHIP_STEPS for dc in (0, 1) if dx or dy or dc]
    same_core = [(dx, dy) for dx, dy in CHIP_STEPS if dx or dy]
    partner = (lat, lon + 1 - 2 * core)

    barrier = pltpu.get_barrier_semaphore()

    def greet(dev):
        pl.semaphore_signal(barrier, inc=1, device_id=dev, device_id_type=MESH)

    greet(z_peer(Z_STEPS[0]))
    for step in everyone:
        greet(chip_peer(*step)[1])
    for d in Z_STEPS[1:]:
        greet(z_peer(d))
    greet((lat, (lon + 2 * core - 1 + LON) % LON))
    for load in loads[3:]:
        load.start()

    row_id = lax.broadcasted_iota(jnp.int32, (PAD, LANES), 0)
    lane_id = lax.broadcasted_iota(jnp.int32, (PAD, LANES), 1)
    row_f = row_id.astype(F32)
    diag = row_id == lane_id

    def as_row(column):
        return jnp.sum(jnp.where(diag, column, 0.0), axis=0, keepdims=True)

    def as_column(row):
        return jnp.sum(jnp.where(diag, row, 0.0), axis=1, keepdims=True)

    for n in range(3):
        loads[n].wait()
    depth_all = (land_v[...] * bottom_v[...]).astype(F32)
    energy = jnp.zeros((PAD, LANES), F32)
    for i in range(ROWS):
        slabs[i, 0:LEVELS, :] = tr_v[:, i, :]
        slabs[i, LEVELS:PAD, :] = jnp.broadcast_to(depth_all[i : i + 1, :], (PAD - LEVELS, LANES))
        wet_x = jnp.where(row_f < depth_all[i : i + 1, :], slabs[i], 0.0)
        energy = energy + wet_x * wet_x
    small_src[...] = as_row(jnp.sum(energy, axis=1, keepdims=True))
    small_r1[q_me] = small_src[...]

    pl.semaphore_wait(barrier, PLANE - 1 + DEPTH - 1 + 1)

    def post(src, dst, dev, send, recv):
        pltpu.make_async_remote_copy(
            src, dst, send, recv, device_id=dev, device_id_type=MESH
        ).start()

    def send_z(src, dst, send, recv):
        for d in Z_STEPS:
            post(src, dst.at[z_me], z_peer(d), send, recv)

    def drain(ref, sem):
        pltpu.make_async_copy(ref, ref, sem).wait()

    def send_halo(k, pieces, dst):
        up = (lat + 1) % LAT
        down = (lat + LAT - 1) % LAT
        right = (lon + 1) % LON
        left = (lon + LON - 1) % LON
        targets = ((up, lon), (down, lon), (lat, right), (lat, left))
        copies = []
        for n, (src, dev) in enumerate(zip(pieces, targets)):
            copy = pltpu.make_async_remote_copy(
                src, dst.at[n], halo_send.at[4 * k + n], halo_recv.at[4 * k + n],
                device_id=dev, device_id_type=MESH,
            )
            copy.start()
            copies.append(copy)
        return copies

    for step in everyone:
        post(small_src, small_r1.at[q_me], chip_peer(*step)[1], small_send.at[0], small_recv.at[0])
    hi = jnp.zeros((PAD, LANES), F32)
    lo = jnp.zeros((PAD, LANES), F32)
    for i in range(ROWS):
        x = slabs[i]
        hi = jnp.where(lane_id == i, pltpu.roll(x, i + 1, 1), hi)
        lo = jnp.where(lane_id == i, pltpu.roll(x, i, 1) if i else x, lo)
    edge_hi[...] = hi
    edge_lo[...] = lo
    halo_copies = send_halo(0, (slabs.at[ROWS - 1], slabs.at[0], edge_hi, edge_lo), halo)

    for n in range(3, 6):
        loads[n].wait()
    bias = b_in_v[...].reshape(1, HIDDEN)
    bias_hi = bias.astype(BF16).astype(F32)
    bias_mid = (bias - bias_hi).astype(BF16).astype(F32)
    bias_lo = bias - bias_hi - bias_mid
    wi_f[LEVELS:LANES, :] = jnp.zeros((LANES - LEVELS, HIDDEN), F32)
    wi_f[0:LEVELS, :] = w_in_v[...].astype(F32)
    wi_f[LEVELS : LEVELS + 1, :] = bias_hi
    wi_f[LEVELS + 1 : LEVELS + 2, :] = bias_mid
    wi_f[LEVELS + 2 : LEVELS + 3, :] = bias_lo
    wi_b[...] = wi_f[...].astype(BF16)
    w1t[...] = wi_f[...].T.astype(BF16)
    wo_f[LEVELS:LANES, :] = jnp.zeros((LANES - LEVELS, HIDDEN), F32)
    wo_f[0:LEVELS, :] = w_out_v[...].astype(F32)
    wot[...] = wo_f[...].astype(BF16)
    wo_b[...] = wo_f[...].T.astype(BF16)
    dlev[LEVELS:LANES] = jnp.zeros((LANES - LEVELS, ROWS, LANES), F32)
    for i in range(ROWS):
        adj_slabs[i, LEVELS:PAD, :] = jnp.zeros((PAD - LEVELS, LANES), F32)
    edge2_hi[LEVELS:PAD, :] = jnp.zeros((PAD - LEVELS, LANES), F32)
    edge2_lo[LEVELS:PAD, :] = jnp.zeros((PAD - LEVELS, LANES), F32)
    inp[PAD - 8 : LANES, :] = jnp.zeros((LANES - PAD + 8, COLS), BF16)
    for n in range(6, 9):
        loads[n].wait()

    drain(small_r1.at[pl.ds(0, PLANE - 1)], small_recv.at[0])
    small_mid[...] = jnp.sum(small_r1[...], axis=0)
    small_r2[z_me] = small_mid[...]
    send_z(small_mid, small_r2, small_send.at[1], small_recv.at[1])

    for copy in halo_copies:
        copy.wait_recv()

    def neighbours(field, edges, i):
        centre = field[i]
        below = field[i + 1] if i + 1 < ROWS else edges[1]
        above = field[i - 1] if i else edges[0]
        from_left = pltpu.roll(edges[2], LANES - i, 1) if i else edges[2]
        left = jnp.where(lane_id == 0, from_left, pltpu.roll(centre, 1, 1))
        right = jnp.where(
            lane_id == LANES - 1, pltpu.roll(edges[3], LANES - 1 - i, 1), pltpu.roll(centre, LANES - 1, 1)
        )
        return centre, (below, above, left, right)

    def flux(centre, near, i):
        total = jnp.zeros((PAD, LANES), F32)
        for n in range(4):
            total = total + jnp.where(
                row_f < near_depth[n * ROWS + i : n * ROWS + i + 1, :], near[n] - centre, 0.0
            )
        return centre + spread_coef * total

    has_above = jnp.where(lat > 0, 1.0, 0.0)
    has_below = jnp.where(lat < LAT - 1, 1.0, 0.0)
    for i in range(ROWS):
        centre, near = neighbours(slabs, halo, i)
        own = centre[LEVELS : LEVELS + 1, :]
        for n in range(4):
            other = near[n][LEVELS : LEVELS + 1, :]
            if n == 0 and i == ROWS - 1:
                other = other * has_below
            if n == 1 and i == 0:
                other = other * has_above
            near_depth[n * ROWS + i : n * ROWS + i + 1, :] = jnp.minimum(own, other)
        mixed[:, i, :] = flux(centre, near, i)[0:LEVELS]

    drain(small_r2.at[pl.ds(0, DEPTH - 1)], small_recv.at[1])
    energy_all = as_column(jnp.sum(small_r2[...], axis=0))
    count = float(LAT * LON * COLS)
    radius = jnp.sqrt(energy_all / count + level_eps)
    inv_radius = 1.0 / radius

    def wet_slab(i):
        x = slabs[i]
        return jnp.where(row_f < x[LEVELS : LEVELS + 1, :], x, 0.0)

    one_rows = jnp.where(row_id < LEVELS + 3, 1.0, 0.0)
    for i in range(ROWS):
        scaled = jnp.where(row_id < LEVELS, wet_slab(i) * inv_radius, one_rows)
        scaled = jnp.concatenate([scaled, jnp.zeros((LANES - PAD, LANES), F32)], axis=0)
        inp[:, i * LANES : (i + 1) * LANES] = scaled.astype(BF16)

    width = 256
    for j in range(COLS // width):
        cols = slice(j * width, (j + 1) * width)
        pre = jnp.dot(w1t[...], inp[:, cols], preferred_element_type=F32)
        sig = 1.0 / (1.0 + jnp.exp(-pre))
        act = pre * sig
        hid[:, cols] = act.astype(BF16)
        slope[:, cols] = sig * (1.0 + pre * (1.0 - sig))
        out = jnp.dot(wot[...], hid[:, cols], preferred_element_type=F32)
        for s in range(width // LANES):
            logit[:, j * (width // LANES) + s, :] = out[0:LEVELS, s * LANES : (s + 1) * LANES]

    depth = depth_all
    middle = LEVELS // 2

    def level_terms(k):
        x = logit[k] + b_out_s[k]
        ex = jnp.exp(-jnp.abs(x))
        soft = jnp.maximum(x, 0.0) + jnp.log1p(ex)
        sig = jnp.where(x >= 0.0, 1.0, ex) / (1.0 + ex)
        kf = (k + 1).astype(F32)
        open_face = kf < depth
        kap = kappa_s[k]
        down = jnp.where(open_face, kap + soft, 0.0)
        up = jnp.where(open_face, kap, 0.0)
        gate[k] = jnp.where(open_face, sig, 0.0)
        return down, up

    def eliminate(s, carry):
        down_p, up_p, r_p, v_p, w_p, sb_n, u_n, z_n = carry
        k = s
        down, up = level_terms(k)
        pivot = 1.0 + down + up_p - down_p * up_p * r_p
        r = 1.0 / pivot
        v = (mixed[k] + down_p * v_p) * r
        w = (cot_v[k] + up_p * w_p) * r
        val_x[k] = v
        val_y[k] = w
        mul_x[k] = up * r
        mul_y[k] = down * r
        b = LEVELS - 1 - s
        down_b, up_b = level_terms(b)
        up_above = jnp.where(b.astype(F32) < depth, kappa_s[b - 1], 0.0)
        pivot_b = 1.0 + down_b + up_above - down_b * up_b * sb_n
        sb = 1.0 / pivot_b
        u = (mixed[b] + up_b * u_n) * sb
        zz = (cot_v[b] + down_b * z_n) * sb
        val_x[b] = u
        val_y[b] = zz
        mul_y[b] = up_above * sb
        mul_x[b + 1] = down_b * sb_n
        return down, up, r, v, w, sb, u, zz

    zero = jnp.zeros((ROWS, LANES), F32)
    down_m, up_m, r_m, v_m, w_m, sb_m, u_m, z_m = lax.fori_loop(
        0, middle, eliminate, (zero,) * 8, unroll=5
    )
    ratio_x = up_m * r_m
    ratio_y = down_m * r_m
    back_x = down_m * sb_m
    back_y = up_m * sb_m
    inv_det = 1.0 / (1.0 - ratio_x * back_x)
    x_top = (v_m + ratio_x * u_m) * inv_det
    x_bot = u_m + back_x * x_top
    y_top = (w_m + ratio_y * z_m) * inv_det
    y_bot = z_m + back_y * y_top
    adj[middle - 1] = y_top
    adj[middle] = y_bot
    dlev[middle - 1] = gate[middle - 1] * x_top * (y_bot - y_top)

    def substitute(s, carry):
        x_t, y_t, x_b, y_b = carry
        k = middle - 1 - s
        x_n = val_x[k] + mul_x[k] * x_t
        y_n = val_y[k] + mul_y[k] * y_t
        adj[k] = y_n
        dlev[k] = gate[k] * x_n * (y_t - y_n)
        b = middle + s
        x_c = val_x[b] + mul_x[b] * x_b
        y_c = val_y[b] + mul_y[b] * y_b
        adj[b] = y_c
        dlev[b - 1] = gate[b - 1] * x_b * (y_c - y_b)
        return x_n, y_n, x_c, y_c

    lax.fori_loop(1, middle, substitute, (x_top, y_top, x_bot, y_bot), unroll=7)
    dlev[LEVELS - 1] = zero

    for i in range(ROWS):
        dlog[:, i * LANES : (i + 1) * LANES] = dlev[:, i, :].astype(BF16)
    contract_last = (((1,), (1,)), ((), ()))

    def share(m, value):
        for p in range(CHIPS):
            for c in range(2):
                grad[m, c, p] = value[8 * p : 8 * p + 8, c * HALF : (c + 1) * HALF]
        post(grad.at[m, 1 - core], from_core.at[m], partner, core_send.at[m], core_recv.at[m])

    share(0, lax.dot_general(dlog[...], hid[...], contract_last, preferred_element_type=F32))

    for j in range(COLS // width):
        cols = slice(j * width, (j + 1) * width)
        back = jnp.dot(wo_b[...], dlog[:, cols], preferred_element_type=F32)
        dpre[:, cols] = (back * slope[:, cols]).astype(BF16)
    share(1, lax.dot_general(inp[...], dpre[...], contract_last, preferred_element_type=F32))

    def scatter(m):
        for dx, dy in same_core:
            p, dev = chip_peer(dx, dy, 0)
            post(half.at[m, p], from_plane.at[m, p_me], dev, plane_send.at[m], plane_recv.at[m])

    tile, first = LEVELS // 8, LEVELS % 8
    drain(from_core.at[0], core_recv.at[0])
    half[0] = grad[0, core] + from_core[0]
    from_plane[0, p_me] = half[0, p_me]
    scatter(0)
    bout_row = lax.dot_general(
        jnp.ones((16, COLS), BF16), dlog[...], contract_last, preferred_element_type=F32
    )[0:1]
    level = jnp.zeros((PAD, LANES), F32)
    for j in range(COLS // width):
        cols = slice(j * width, (j + 1) * width)
        out = jnp.dot(wi_b[...], dpre[:, cols], preferred_element_type=F32)
        for s in range(width // LANES):
            i = j * (width // LANES) + s
            part = out[0:PAD, s * LANES : (s + 1) * LANES]
            din[i] = part
            level = level + part * wet_slab(i)
    level_row = as_row(jnp.sum(level, axis=1, keepdims=True))
    drain(from_core.at[1], core_recv.at[1])
    half[1] = grad[1, core] + from_core[1]
    half[1, tile, first + 1 : first + 2, 0:LANES] = level_row
    half[1, tile, first + 2 : first + 3, 0:LANES] = bout_row
    from_plane[1, p_me] = half[1, p_me]
    scatter(1)

    hi = jnp.zeros((LEVELS, LANES), F32)
    lo = jnp.zeros((LEVELS, LANES), F32)
    lane_l = lane_id[0:LEVELS]
    for i in range(ROWS):
        x = adj[:, i, :]
        adj_slabs[i, 0:LEVELS, :] = x
        hi = jnp.where(lane_l == i, pltpu.roll(x, i + 1, 1), hi)
        lo = jnp.where(lane_l == i, pltpu.roll(x, i, 1) if i else x, lo)
    edge2_hi[0:LEVELS, :] = hi
    edge2_lo[0:LEVELS, :] = lo

    def through_z(m):
        drain(from_plane.at[m, pl.ds(0, CHIPS - 1)], plane_recv.at[m])
        mid[m] = jnp.sum(from_plane[m], axis=0)
        from_z[m, z_me] = mid[m]
        send_z(mid.at[m], from_z.at[m], z_send.at[m], z_recv.at[m])

    scale = 1.0 / math.sqrt(count)

    def gather(m):
        drain(from_z.at[m, pl.ds(0, DEPTH - 1)], z_recv.at[m])
        chunk[m] = jnp.sum(from_z[m], axis=0) * scale
        full[m, core, p_me] = chunk[m]
        for dx, dy in same_core:
            _, dev = chip_peer(dx, dy, 0)
            post(chunk.at[m], full.at[m, core, p_me], dev, gather_send.at[m], gather_recv.at[m])

    through_z(0)
    through_z(1)
    halo2_copies = send_halo(
        1, (adj_slabs.at[ROWS - 1], adj_slabs.at[0], edge2_hi, edge2_lo), halo2
    )
    gather(0)
    gather(1)

    for copy in halo2_copies:
        copy.wait_recv()
    for i in range(ROWS):
        centre, near = neighbours(adj_slabs, halo2, i)
        mix = flux(centre, near, i)
        wet = row_f < slabs[i, LEVELS : LEVELS + 1, :]
        din[i] = mix + jnp.where(wet, din[i] * inv_radius, 0.0)

    def forward(m):
        drain(full.at[m, core, pl.ds(0, CHIPS - 1)], gather_recv.at[m])
        if m:
            post(full.at[m, core, tile], rows_in, partner, core_send.at[2], core_recv.at[2])
        post(full.at[m, core], full.at[m, core], partner, fwd_send.at[m], fwd_recv.at[m])

    def deliver(m, ref):
        drain(full.at[m, 1 - core], fwd_recv.at[m])
        for p in range(LEVELS // 8 + 1):
            rows = min(8, LEVELS - 8 * p)
            for c in range(2):
                ref[8 * p : 8 * p + rows, c * HALF : (c + 1) * HALF] = full[m, c, p, 0:rows, :]

    forward(0)
    forward(1)
    deliver(0, gw_out_ref)
    drain(rows_in, core_recv.at[2])
    both_rows = full[1, core, tile, first + 1 : first + 3, 0:LANES] + rows_in[first + 1 : first + 3, 0:LANES]
    level_sum = as_column(both_rows[0:1]) * math.sqrt(count)
    gb_out_ref[...] = both_rows[1:2]
    level_scale = level_sum / (count * radius * radius * radius)
    for i in range(ROWS):
        out_ref[:, i, :] = (din[i] - wet_slab(i) * level_scale)[0:LEVELS]
    deliver(1, gw_in_ref)
    for c in range(2):
        gb_in_ref[:, c * HALF : (c + 1) * HALF] = full[1, c, tile, first : first + 1, :]

    for copy in halo_copies + halo2_copies:
        copy.wait_send()
    drain(small_r1.at[pl.ds(0, PLANE - 1)], small_send.at[0])
    drain(small_r2.at[pl.ds(0, DEPTH - 1)], small_send.at[1])
    for m in range(2):
        drain(from_core.at[m], core_send.at[m])
        drain(from_plane.at[m, pl.ds(0, CHIPS - 1)], plane_send.at[m])
        drain(from_z.at[m, pl.ds(0, DEPTH - 1)], z_send.at[m])
        drain(full.at[m, core, pl.ds(0, CHIPS - 1)], gather_send.at[m])
        drain(full.at[m, core], fwd_send.at[m])
    drain(rows_in, core_send.at[2])


def store_results(out_v, gw_in_v, gb_in_v, gw_out_v, gb_out_v, out_h, gw_in_h, gb_in_ref, gw_out_h, gb_out_ref, sems):
    copies = []
    for n, (src, dst) in enumerate(((out_v, out_h), (gw_in_v, gw_in_h), (gw_out_v, gw_out_h))):
        copy = pltpu.make_async_copy(src, dst, sems.at[n])
        copy.start()
        copies.append(copy)
    gb_in_ref[...] = gb_in_v[...].reshape(HIDDEN)
    gb_out_ref[...] = gb_out_v[...].reshape(LANES)[0:LEVELS]
    for copy in copies:
        copy.wait()


def shards(tracer, cotangent, land_mask, bottom, kappa, w_in, b_in, w_out, b_out):
    vmem = pl.BlockSpec(memory_space=pltpu.VMEM)
    hbm = pl.BlockSpec(memory_space=pltpu.HBM)
    slab = (ROWS, PAD, LANES)
    levels = (LEVELS, ROWS, LANES)
    edge = (PAD, LANES)
    pieces = (CHIPS, 8, HALF)

    def v(*shape, dtype=F32):
        return pltpu.VMEM(shape, dtype)

    def sems(n):
        return pltpu.SemaphoreType.DMA((n,))

    scratch = [
        v(*levels), v(*levels), v(ROWS, LANES, dtype=jnp.int32), v(ROWS, LANES, dtype=jnp.int32),
        pltpu.SMEM((LEVELS,), F32), v(LEVELS, HIDDEN, dtype=BF16), v(HIDDEN),
        v(LEVELS, HIDDEN, dtype=BF16), pltpu.SMEM((LEVELS,), F32),
        v(*slab), v(*slab), v(*edge), v(*edge), v(*edge), v(*edge),
        v(4, *edge), v(4, *edge), v(4 * ROWS, LANES),
        v(1, LANES), v(PLANE, 1, LANES), v(1, LANES), v(DEPTH, 1, LANES),
        v(8, HALF),
        v(LANES, HIDDEN), v(LANES, HIDDEN), v(LANES, HIDDEN, dtype=BF16),
        v(HIDDEN, LANES, dtype=BF16), v(LANES, HIDDEN, dtype=BF16), v(HIDDEN, LANES, dtype=BF16),
        v(LANES, COLS, dtype=BF16), v(HIDDEN, COLS, dtype=BF16), v(HIDDEN, COLS),
        v(HIDDEN, COLS, dtype=BF16), v(LANES, COLS, dtype=BF16), v(*slab),
        v(*levels), v(*levels), v(*levels), v(*levels), v(LEVELS + 1, ROWS, LANES),
        v(*levels), v(*levels), v(*levels), v(LANES, ROWS, LANES),
        v(2, 2, *pieces), v(2, *pieces), v(2, *pieces), v(2, *pieces), v(2, 8, HALF),
        v(2, DEPTH, 8, HALF), v(2, 8, HALF), v(2, 2, *pieces),
        sems(9), sems(2), sems(2), sems(3), sems(3), sems(2), sems(2),
        sems(2), sems(2), sems(2), sems(2), sems(2), sems(2), sems(8), sems(8),
    ]
    shapes = (
        jax.ShapeDtypeStruct(tracer.shape, F32),
        jax.ShapeDtypeStruct((LEVELS, HIDDEN), F32),
        jax.ShapeDtypeStruct((1, HIDDEN), F32),
        jax.ShapeDtypeStruct((LEVELS, HIDDEN), F32),
        jax.ShapeDtypeStruct((1, LANES), F32),
    )
    operands = (tracer, cotangent, land_mask, bottom, kappa, w_in, b_in, w_out.T, b_out)
    results = pl.pallas_call(
        kernel,
        out_shape=shapes,
        in_specs=[hbm] * 9,
        out_specs=(vmem,) * 5,
        scratch_shapes=scratch,
        compiler_params=pltpu.CompilerParams(
            collective_id=0, has_side_effects=True, vmem_limit_bytes=40 * 1024 * 1024
        ),
        name="step_adjoint",
    )(*(pltpu.with_memory_space_constraint(a, pltpu.HBM) for a in operands))
    out, gw_in, gb_in, gw_out, gb_out = pl.pallas_call(
        store_results,
        out_shape=shapes[:2]
        + (jax.ShapeDtypeStruct((HIDDEN,), F32), shapes[3], jax.ShapeDtypeStruct((LEVELS,), F32)),
        in_specs=[vmem] * 5,
        out_specs=(hbm, hbm, vmem, hbm, vmem),
        scratch_shapes=[sems(3)],
        compiler_params=pltpu.CompilerParams(vmem_limit_bytes=1024 * 1024),
        name="store_results",
    )(*results)
    return out, gw_in, gb_in, gw_out.T, gb_out


def solution(mesh):
    placed = (
        P(None, "lat", "lon"),
        P(None, "lat", "lon"),
        P("lat", "lon"),
        P("lat", "lon"),
        P(),
        P(),
        P(),
        P(),
        P(),
    )
    return jax.shard_map(
        shards,
        mesh=mesh,
        in_specs=placed,
        out_specs=(P(None, "lat", "lon"), P(), P(), P(), P()),
        check_vma=False,
    )
```

```python
import functools
import math

import jax
import jax.numpy as jnp
from jax import lax
from jax.experimental import pallas as pl
from jax.experimental.pallas import tpu as pltpu
from jax.sharding import PartitionSpec as P

MESH = pl.DeviceIdType.MESH
F32 = jnp.float32
BF16 = jnp.bfloat16

spread_coef = 0.15
level_eps = 1e-05

LEVELS = 100
ROWS = 8
LANES = 128
HIDDEN = 512
COLS = ROWS * LANES
PAD = 104
LAT = 8
LON = 32
SIDE = 4
CHIPS = SIDE * SIDE
PLANE = 2 * CHIPS
DEPTH = 8
HALF = HIDDEN // 2
REDUCERS = PAD // 8


def ring(d, n):
    return min(d, n - d)


CHIP_STEPS = sorted(
    ((dx, dy) for dx in range(SIDE) for dy in range(SIDE)),
    key=lambda s: -(ring(s[0], SIDE) + ring(s[1], SIDE)),
)
Z_STEPS = sorted(range(1, DEPTH), key=lambda d: -ring(d, DEPTH))


def kernel(
    tracer_hbm, cot_hbm, land_hbm, bottom_hbm, kappa_hbm, w_in_hbm, b_in_hbm, w_out_hbm, b_out_hbm,
    out_ref, gw_in_ref, gb_in_ref, gw_out_ref, gb_out_ref,
    tr_v, cot_v, land_v, bottom_v, kappa_s, w_in_v, b_in_v, w_out_v, b_out_s,
    slabs, adj_slabs, edge_hi, edge_lo, edge2_hi, edge2_lo, halo, halo2, near_depth,
    small_src, small_r1, small_mid, small_r2,
    wi_f, wi_half, wo_f, wi_b, w1t, wot, wo_b,
    inp, hid, slope, dpre, dlog, din,
    logit, mixed, val_x, val_y, mul_x, mul_y, gate, adj, dlev,
    given, kept, from_core, half, from_plane, mid, from_z, chunk, full,
    load_sems, small_send, small_recv, core_send, core_recv, plane_send, plane_recv,
    z_send, z_recv, gather_send, gather_recv, fwd_send, fwd_recv, halo_send, halo_recv,
):
    lat = lax.axis_index("lat")
    lon = lax.axis_index("lon")
    y_me = lat % SIDE
    x_me = (lat // SIDE) * 2 + lon // 16
    z_me = (lon // 2) % DEPTH
    core = lon % 2
    p_me = x_me * SIDE + y_me
    q_me = p_me * 2 + core
    reducer = p_me < REDUCERS
    idle = p_me >= REDUCERS
    lon_z = z_me * 2

    loads = []
    for n, (src, dst) in enumerate(
        (
            (tracer_hbm, tr_v), (land_hbm, land_v), (bottom_hbm, bottom_v), (w_in_hbm, w_in_v),
            (b_in_hbm, b_in_v), (w_out_hbm, w_out_v), (cot_hbm, cot_v), (kappa_hbm, kappa_s),
            (b_out_hbm, b_out_s),
        )
    ):
        loads.append(pltpu.make_async_copy(src, dst, load_sems.at[n]))
    for load in loads[:3]:
        load.start()

    xs = [(x_me + d) % SIDE for d in range(SIDE)]
    ys = [(y_me + d) % SIDE for d in range(SIDE)]

    def chip_peer(dx, dy, dc):
        to_core = core if dc == 0 else 1 - core
        dev = ((xs[dx] // 2) * SIDE + ys[dy], (xs[dx] % 2) * 16 + lon_z + to_core)
        return xs[dx] * SIDE + ys[dy], dev

    def z_peer(d):
        return (lat, (lon // 16) * 16 + ((z_me + d) % DEPTH) * 2 + core)

    everyone = [(dx, dy, dc) for dx, dy in CHIP_STEPS for dc in (0, 1) if dx or dy or dc]
    same_core = [(dx, dy) for dx, dy in CHIP_STEPS if dx or dy]
    partner = (lat, lon + 1 - 2 * core)

    barrier = pltpu.get_barrier_semaphore()

    def greet(dev):
        pl.semaphore_signal(barrier, inc=1, device_id=dev, device_id_type=MESH)

    greet(z_peer(Z_STEPS[0]))
    for step in everyone:
        greet(chip_peer(*step)[1])
    for d in Z_STEPS[1:]:
        greet(z_peer(d))
    greet((lat, (lon + 2 * core - 1 + LON) % LON))
    for load in loads[3:]:
        load.start()

    row_id = lax.broadcasted_iota(jnp.int32, (PAD, LANES), 0)
    lane_id = lax.broadcasted_iota(jnp.int32, (PAD, LANES), 1)
    row_f = row_id.astype(F32)
    diag = row_id == lane_id

    def as_row(column):
        return jnp.sum(jnp.where(diag, column, 0.0), axis=0, keepdims=True)

    def as_column(row):
        return jnp.sum(jnp.where(diag, row, 0.0), axis=1, keepdims=True)

    for n in range(3):
        loads[n].wait()
    depth_all = (land_v[...] * bottom_v[...]).astype(F32)
    energy = jnp.zeros((PAD, LANES), F32)
    for i in range(ROWS):
        slabs[i, 0:LEVELS, :] = tr_v[:, i, :]
        slabs[i, LEVELS:PAD, :] = jnp.broadcast_to(depth_all[i : i + 1, :], (PAD - LEVELS, LANES))
        wet_x = jnp.where(row_f < depth_all[i : i + 1, :], slabs[i], 0.0)
        energy = energy + wet_x * wet_x
    small_src[...] = as_row(jnp.sum(energy, axis=1, keepdims=True))
    small_r1[q_me] = small_src[...]

    pl.semaphore_wait(barrier, PLANE - 1 + DEPTH - 1 + 1)

    def post(src, dst, dev, send, recv):
        pltpu.make_async_remote_copy(
            src, dst, send, recv, device_id=dev, device_id_type=MESH
        ).start()

    def send_z(src, dst, send, recv):
        for d in Z_STEPS:
            post(src, dst.at[z_me], z_peer(d), send, recv)

    def drain(ref, sem):
        pltpu.make_async_copy(ref, ref, sem).wait()

    def send_halo(k, pieces, dst):
        up = (lat + 1) % LAT
        down = (lat + LAT - 1) % LAT
        right = (lon + 1) % LON
        left = (lon + LON - 1) % LON
        targets = ((up, lon), (down, lon), (lat, right), (lat, left))
        copies = []
        for n, (src, dev) in enumerate(zip(pieces, targets)):
            copy = pltpu.make_async_remote_copy(
                src, dst.at[n], halo_send.at[4 * k + n], halo_recv.at[4 * k + n],
                device_id=dev, device_id_type=MESH,
            )
            copy.start()
            copies.append(copy)
        return copies

    for step in everyone:
        post(small_src, small_r1.at[q_me], chip_peer(*step)[1], small_send.at[0], small_recv.at[0])
    hi = jnp.zeros((PAD, LANES), F32)
    lo = jnp.zeros((PAD, LANES), F32)
    for i in range(ROWS):
        x = slabs[i]
        hi = jnp.where(lane_id == i, pltpu.roll(x, i + 1, 1), hi)
        lo = jnp.where(lane_id == i, pltpu.roll(x, i, 1) if i else x, lo)
    edge_hi[...] = hi
    edge_lo[...] = lo
    halo_copies = send_halo(0, (slabs.at[ROWS - 1], slabs.at[0], edge_hi, edge_lo), halo)

    for n in range(3, 6):
        loads[n].wait()
    bias = b_in_v[...].reshape(1, HIDDEN)
    bias_hi = bias.astype(BF16).astype(F32)
    bias_mid = (bias - bias_hi).astype(BF16).astype(F32)
    bias_lo = bias - bias_hi - bias_mid
    wi_f[LEVELS:LANES, :] = jnp.zeros((LANES - LEVELS, HIDDEN), F32)
    wi_f[0:LEVELS, :] = w_in_v[...].astype(F32)
    wi_f[LEVELS : LEVELS + 1, :] = bias_hi
    wi_f[LEVELS + 1 : LEVELS + 2, :] = bias_mid
    wi_f[LEVELS + 2 : LEVELS + 3, :] = bias_lo
    wi_b[...] = wi_f[...].astype(BF16)
    for c in range(2):
        wi_half[c] = wi_f[0:PAD, c * HALF : (c + 1) * HALF]
    w1t[...] = wi_f[...].T.astype(BF16)
    wo_f[LEVELS:LANES, :] = jnp.zeros((LANES - LEVELS, HIDDEN), F32)
    wo_f[0:LEVELS, :] = w_out_v[...].astype(F32)
    wot[...] = wo_f[...].astype(BF16)
    wo_b[...] = wo_f[...].T.astype(BF16)
    dlev[LEVELS:LANES] = jnp.zeros((LANES - LEVELS, ROWS, LANES), F32)
    for i in range(ROWS):
        adj_slabs[i, LEVELS:PAD, :] = jnp.zeros((PAD - LEVELS, LANES), F32)
    edge2_hi[LEVELS:PAD, :] = jnp.zeros((PAD - LEVELS, LANES), F32)
    edge2_lo[LEVELS:PAD, :] = jnp.zeros((PAD - LEVELS, LANES), F32)
    inp[PAD - 8 : LANES, :] = jnp.zeros((LANES - PAD + 8, COLS), BF16)
    for n in range(6, 9):
        loads[n].wait()

    drain(small_r1.at[pl.ds(0, PLANE - 1)], small_recv.at[0])
    small_mid[...] = jnp.sum(small_r1[...], axis=0)
    small_r2[z_me] = small_mid[...]
    send_z(small_mid, small_r2, small_send.at[1], small_recv.at[1])

    for copy in halo_copies:
        copy.wait_recv()

    def neighbours(field, edges, i):
        centre = field[i]
        below = field[i + 1] if i + 1 < ROWS else edges[1]
        above = field[i - 1] if i else edges[0]
        from_left = pltpu.roll(edges[2], LANES - i, 1) if i else edges[2]
        left = jnp.where(lane_id == 0, from_left, pltpu.roll(centre, 1, 1))
        right = jnp.where(
            lane_id == LANES - 1, pltpu.roll(edges[3], LANES - 1 - i, 1), pltpu.roll(centre, LANES - 1, 1)
        )
        return centre, (below, above, left, right)

    def flux(centre, near, i):
        total = jnp.zeros((PAD, LANES), F32)
        for n in range(4):
            total = total + jnp.where(
                row_f < near_depth[n * ROWS + i : n * ROWS + i + 1, :], near[n] - centre, 0.0
            )
        return centre + spread_coef * total

    has_above = jnp.where(lat > 0, 1.0, 0.0)
    has_below = jnp.where(lat < LAT - 1, 1.0, 0.0)
    for i in range(ROWS):
        centre, near = neighbours(slabs, halo, i)
        own = centre[LEVELS : LEVELS + 1, :]
        for n in range(4):
            other = near[n][LEVELS : LEVELS + 1, :]
            if n == 0 and i == ROWS - 1:
                other = other * has_below
            if n == 1 and i == 0:
                other = other * has_above
            near_depth[n * ROWS + i : n * ROWS + i + 1, :] = jnp.minimum(own, other)
        mixed[:, i, :] = flux(centre, near, i)[0:LEVELS]

    drain(small_r2.at[pl.ds(0, DEPTH - 1)], small_recv.at[1])
    energy_all = as_column(jnp.sum(small_r2[...], axis=0))
    count = float(LAT * LON * COLS)
    radius = jnp.sqrt(energy_all / count + level_eps)
    inv_radius = 1.0 / radius

    def wet_slab(i):
        x = slabs[i]
        return jnp.where(row_f < x[LEVELS : LEVELS + 1, :], x, 0.0)

    one_rows = jnp.where(row_id < LEVELS + 3, 1.0, 0.0)
    for i in range(ROWS):
        scaled = jnp.where(row_id < LEVELS, wet_slab(i) * inv_radius, one_rows)
        scaled = jnp.concatenate([scaled, jnp.zeros((LANES - PAD, LANES), F32)], axis=0)
        inp[:, i * LANES : (i + 1) * LANES] = scaled.astype(BF16)

    width = 256
    for j in range(COLS // width):
        cols = slice(j * width, (j + 1) * width)
        pre = jnp.dot(w1t[...], inp[:, cols], preferred_element_type=F32)
        sig = 1.0 / (1.0 + jnp.exp(-pre))
        act = pre * sig
        hid[:, cols] = act.astype(BF16)
        slope[:, cols] = sig * (1.0 + pre * (1.0 - sig))
        out = jnp.dot(wot[...], hid[:, cols], preferred_element_type=F32)
        for s in range(width // LANES):
            logit[:, j * (width // LANES) + s, :] = out[0:LEVELS, s * LANES : (s + 1) * LANES]

    depth = depth_all
    middle = LEVELS // 2

    def level_terms(k):
        x = logit[k] + b_out_s[k]
        ex = jnp.exp(-jnp.abs(x))
        soft = jnp.maximum(x, 0.0) + jnp.log1p(ex)
        sig = jnp.where(x >= 0.0, 1.0, ex) / (1.0 + ex)
        kf = (k + 1).astype(F32)
        open_face = kf < depth
        kap = kappa_s[k]
        down = jnp.where(open_face, kap + soft, 0.0)
        up = jnp.where(open_face, kap, 0.0)
        gate[k] = jnp.where(open_face, sig, 0.0)
        return down, up

    def eliminate(s, carry):
        down_p, up_p, r_p, v_p, w_p, sb_n, u_n, z_n = carry
        k = s
        down, up = level_terms(k)
        pivot = 1.0 + down + up_p - down_p * up_p * r_p
        r = 1.0 / pivot
        v = (mixed[k] + down_p * v_p) * r
        w = (cot_v[k] + up_p * w_p) * r
        val_x[k] = v
        val_y[k] = w
        mul_x[k] = up * r
        mul_y[k] = down * r
        b = LEVELS - 1 - s
        down_b, up_b = level_terms(b)
        up_above = jnp.where(b.astype(F32) < depth, kappa_s[b - 1], 0.0)
        pivot_b = 1.0 + down_b + up_above - down_b * up_b * sb_n
        sb = 1.0 / pivot_b
        u = (mixed[b] + up_b * u_n) * sb
        zz = (cot_v[b] + down_b * z_n) * sb
        val_x[b] = u
        val_y[b] = zz
        mul_y[b] = up_above * sb
        mul_x[b + 1] = down_b * sb_n
        return down, up, r, v, w, sb, u, zz

    zero = jnp.zeros((ROWS, LANES), F32)
    down_m, up_m, r_m, v_m, w_m, sb_m, u_m, z_m = lax.fori_loop(
        0, middle, eliminate, (zero,) * 8, unroll=5
    )
    ratio_x = up_m * r_m
    ratio_y = down_m * r_m
    back_x = down_m * sb_m
    back_y = up_m * sb_m
    inv_det = 1.0 / (1.0 - ratio_x * back_x)
    x_top = (v_m + ratio_x * u_m) * inv_det
    x_bot = u_m + back_x * x_top
    y_top = (w_m + ratio_y * z_m) * inv_det
    y_bot = z_m + back_y * y_top
    adj[middle - 1] = y_top
    adj[middle] = y_bot
    dlev[middle - 1] = gate[middle - 1] * x_top * (y_bot - y_top)

    def substitute(s, carry):
        x_t, y_t, x_b, y_b = carry
        k = middle - 1 - s
        x_n = val_x[k] + mul_x[k] * x_t
        y_n = val_y[k] + mul_y[k] * y_t
        adj[k] = y_n
        dlev[k] = gate[k] * x_n * (y_t - y_n)
        b = middle + s
        x_c = val_x[b] + mul_x[b] * x_b
        y_c = val_y[b] + mul_y[b] * y_b
        adj[b] = y_c
        dlev[b - 1] = gate[b - 1] * x_b * (y_c - y_b)
        return x_n, y_n, x_c, y_c

    lax.fori_loop(1, middle, substitute, (x_top, y_top, x_bot, y_bot), unroll=7)
    dlev[LEVELS - 1] = zero

    for i in range(ROWS):
        dlog[:, i * LANES : (i + 1) * LANES] = dlev[:, i, :].astype(BF16)
    for j in range(COLS // width):
        cols = slice(j * width, (j + 1) * width)
        back = jnp.dot(wo_b[...], dlog[:, cols], preferred_element_type=F32)
        dpre[:, cols] = (back * slope[:, cols]).astype(BF16)
    contract_last = (((1,), (1,)), ((), ()))
    sources = ((inp, dpre), (dlog, hid))

    def half_of(m, c):
        small, big = sources[m]
        rows = big[pl.ds(pl.multiple_of(c * HALF, HALF), HALF), :]
        value = lax.dot_general(small[...], rows, contract_last, preferred_element_type=F32)
        return value[0:PAD].reshape(REDUCERS, 8, HALF)

    for m in range(2):
        given[m] = half_of(m, 1 - core)
        post(given.at[m], from_core.at[m], partner, core_send.at[m], core_recv.at[m])
    for m in range(2):
        kept[m] = half_of(m, core)
    bout_row = lax.dot_general(
        jnp.ones((16, COLS), BF16), dlog[...], contract_last, preferred_element_type=F32
    )[0:1]
    tile, first = LEVELS // 8, LEVELS % 8

    for m in range(2):
        drain(from_core.at[m], core_recv.at[m])
        half[m] = kept[m] + from_core[m]
        if m:
            half[1, tile, first : first + 1, 0:LANES] = bout_row
        for dx, dy in same_core:
            p, dev = chip_peer(dx, dy, 0)

            @pl.when(p < REDUCERS)
            def _(m=m, p=p, dev=dev):
                post(half.at[m, p], from_plane.at[m, p_me], dev, plane_send.at[m], plane_recv.at[m])

    hi = jnp.zeros((LEVELS, LANES), F32)
    lo = jnp.zeros((LEVELS, LANES), F32)
    lane_l = lane_id[0:LEVELS]
    for i in range(ROWS):
        x = adj[:, i, :]
        adj_slabs[i, 0:LEVELS, :] = x
        hi = jnp.where(lane_l == i, pltpu.roll(x, i + 1, 1), hi)
        lo = jnp.where(lane_l == i, pltpu.roll(x, i, 1) if i else x, lo)
    edge2_hi[0:LEVELS, :] = hi
    edge2_lo[0:LEVELS, :] = lo
    for j in range(COLS // width):
        cols = slice(j * width, (j + 1) * width)
        out = jnp.dot(wi_b[...], dpre[:, cols], preferred_element_type=F32)
        for s in range(width // LANES):
            i = j * (width // LANES) + s
            din[i] = out[0:PAD, s * LANES : (s + 1) * LANES] * inv_radius

    scale = 1.0 / math.sqrt(count)
    for m in range(2):

        @pl.when(reducer)
        def _(m=m):
            from_plane[m, p_me] = half[m, p_me]
            drain(from_plane.at[m, pl.ds(0, CHIPS - 1)], plane_recv.at[m])
            mid[m] = jnp.sum(from_plane[m], axis=0)
            from_z[m, z_me] = mid[m]
            send_z(mid.at[m], from_z.at[m], z_send.at[m], z_recv.at[m])

    halo2_copies = send_halo(
        1, (adj_slabs.at[ROWS - 1], adj_slabs.at[0], edge2_hi, edge2_lo), halo2
    )
    for m in range(2):

        @pl.when(reducer)
        def _(m=m):
            drain(from_z.at[m, pl.ds(0, DEPTH - 1)], z_recv.at[m])
            chunk[m] = jnp.sum(from_z[m], axis=0) * scale
            full[m, core, p_me] = chunk[m]
            for dx, dy in same_core:
                _, dev = chip_peer(dx, dy, 0)
                post(chunk.at[m], full.at[m, core, p_me], dev, gather_send.at[m], gather_recv.at[m])

    for copy in halo2_copies:
        copy.wait_recv()
    for i in range(ROWS):
        centre, near = neighbours(adj_slabs, halo2, i)
        wet = row_f < slabs[i, LEVELS : LEVELS + 1, :]
        din[i] = flux(centre, near, i) + jnp.where(wet, din[i], 0.0)

    def drain_peers(ref, sem):
        @pl.when(reducer)
        def _():
            drain(ref.at[pl.ds(0, REDUCERS - 1)], sem)

        @pl.when(idle)
        def _():
            drain(ref, sem)

    for m in range(2):
        drain_peers(full.at[m, core], gather_recv.at[m])
        post(full.at[m, core], full.at[m, core], partner, fwd_send.at[m], fwd_recv.at[m])

    def deliver(m, ref):
        for p in range(REDUCERS):
            rows = min(8, LEVELS - 8 * p)
            for c in range(2):
                ref[8 * p : 8 * p + rows, c * HALF : (c + 1) * HALF] = full[m, c, p, 0:rows, :]

    drain(full.at[0, 1 - core], fwd_recv.at[0])
    weighted = jnp.zeros((PAD, HALF), F32)
    for c in range(2):
        weighted = weighted + wi_half[c] * full[0, c].reshape(PAD, HALF)
    level_sum = radius * jnp.sum(weighted, axis=1, keepdims=True) * math.sqrt(count)
    level_scale = level_sum / (count * radius * radius * radius)
    for i in range(ROWS):
        out_ref[:, i, :] = (din[i] - wet_slab(i) * level_scale)[0:LEVELS]
    deliver(0, gw_in_ref)
    for c in range(2):
        gb_in_ref[:, c * HALF : (c + 1) * HALF] = full[0, c, tile, first : first + 1, :]
    drain(full.at[1, 1 - core], fwd_recv.at[1])
    deliver(1, gw_out_ref)
    gb_out_ref[...] = (
        full[1, 0, tile, first : first + 1, 0:LANES] + full[1, 1, tile, first : first + 1, 0:LANES]
    )

    for copy in halo_copies + halo2_copies:
        copy.wait_send()
    drain(small_r1.at[pl.ds(0, PLANE - 1)], small_send.at[0])
    drain(small_r2.at[pl.ds(0, DEPTH - 1)], small_send.at[1])
    for m in range(2):
        drain(from_core.at[m], core_send.at[m])
        drain_peers(half.at[m], plane_send.at[m])

        @pl.when(reducer)
        def _(m=m):
            drain(from_z.at[m, pl.ds(0, DEPTH - 1)], z_send.at[m])
            drain(from_plane.at[m, pl.ds(0, CHIPS - 1)], gather_send.at[m])

        drain(full.at[m, core], fwd_send.at[m])


def store_results(out_v, gw_in_v, gb_in_v, gw_out_v, gb_out_v, out_h, gw_in_h, gb_in_ref, gw_out_h, gb_out_ref, sems):
    copies = []
    for n, (src, dst) in enumerate(((out_v, out_h), (gw_in_v, gw_in_h), (gw_out_v, gw_out_h))):
        copy = pltpu.make_async_copy(src, dst, sems.at[n])
        copy.start()
        copies.append(copy)
    gb_in_ref[...] = gb_in_v[...].reshape(HIDDEN)
    gb_out_ref[...] = gb_out_v[...].reshape(LANES)[0:LEVELS]
    for copy in copies:
        copy.wait()


def shards(tracer, cotangent, land_mask, bottom, kappa, w_in, b_in, w_out, b_out):
    vmem = pl.BlockSpec(memory_space=pltpu.VMEM)
    hbm = pl.BlockSpec(memory_space=pltpu.HBM)
    slab = (ROWS, PAD, LANES)
    levels = (LEVELS, ROWS, LANES)
    edge = (PAD, LANES)
    pieces = (REDUCERS, 8, HALF)

    def v(*shape, dtype=F32):
        return pltpu.VMEM(shape, dtype)

    def sems(n):
        return pltpu.SemaphoreType.DMA((n,))

    scratch = [
        v(*levels), v(*levels), v(ROWS, LANES, dtype=jnp.int32), v(ROWS, LANES, dtype=jnp.int32),
        pltpu.SMEM((LEVELS,), F32), v(LEVELS, HIDDEN, dtype=BF16), v(HIDDEN),
        v(LEVELS, HIDDEN, dtype=BF16), pltpu.SMEM((LEVELS,), F32),
        v(*slab), v(*slab), v(*edge), v(*edge), v(*edge), v(*edge),
        v(4, *edge), v(4, *edge), v(4 * ROWS, LANES),
        v(1, LANES), v(PLANE, 1, LANES), v(1, LANES), v(DEPTH, 1, LANES),
        v(LANES, HIDDEN), v(2, PAD, HALF), v(LANES, HIDDEN), v(LANES, HIDDEN, dtype=BF16),
        v(HIDDEN, LANES, dtype=BF16), v(LANES, HIDDEN, dtype=BF16), v(HIDDEN, LANES, dtype=BF16),
        v(LANES, COLS, dtype=BF16), v(HIDDEN, COLS, dtype=BF16), v(HIDDEN, COLS),
        v(HIDDEN, COLS, dtype=BF16), v(LANES, COLS, dtype=BF16), v(*slab),
        v(*levels), v(*levels), v(*levels), v(*levels), v(LEVELS + 1, ROWS, LANES),
        v(*levels), v(*levels), v(*levels), v(LANES, ROWS, LANES),
        v(2, *pieces), v(2, *pieces), v(2, *pieces), v(2, *pieces), v(2, CHIPS, 8, HALF),
        v(2, 8, HALF), v(2, DEPTH, 8, HALF), v(2, 8, HALF), v(2, 2, *pieces),
        sems(9), sems(2), sems(2), sems(2), sems(2), sems(2), sems(2),
        sems(2), sems(2), sems(2), sems(2), sems(2), sems(2), sems(8), sems(8),
    ]
    shapes = (
        jax.ShapeDtypeStruct(tracer.shape, F32),
        jax.ShapeDtypeStruct((LEVELS, HIDDEN), F32),
        jax.ShapeDtypeStruct((1, HIDDEN), F32),
        jax.ShapeDtypeStruct((LEVELS, HIDDEN), F32),
        jax.ShapeDtypeStruct((1, LANES), F32),
    )
    operands = (tracer, cotangent, land_mask, bottom, kappa, w_in, b_in, w_out.T, b_out)
    results = pl.pallas_call(
        kernel,
        out_shape=shapes,
        in_specs=[hbm] * 9,
        out_specs=(vmem,) * 5,
        scratch_shapes=scratch,
        compiler_params=pltpu.CompilerParams(
            collective_id=0, has_side_effects=True, vmem_limit_bytes=40 * 1024 * 1024
        ),
        name="step_adjoint",
    )(*(pltpu.with_memory_space_constraint(a, pltpu.HBM) for a in operands))
    out, gw_in, gb_in, gw_out, gb_out = pl.pallas_call(
        store_results,
        out_shape=shapes[:2]
        + (jax.ShapeDtypeStruct((HIDDEN,), F32), shapes[3], jax.ShapeDtypeStruct((LEVELS,), F32)),
        in_specs=[vmem] * 5,
        out_specs=(hbm, hbm, vmem, hbm, vmem),
        scratch_shapes=[sems(3)],
        compiler_params=pltpu.CompilerParams(vmem_limit_bytes=1024 * 1024),
        name="store_results",
    )(*results)
    return out, gw_in, gb_in, gw_out.T, gb_out


def solution(mesh):
    placed = (
        P(None, "lat", "lon"),
        P(None, "lat", "lon"),
        P("lat", "lon"),
        P("lat", "lon"),
        P(),
        P(),
        P(),
        P(),
        P(),
    )
    return jax.shard_map(
        shards,
        mesh=mesh,
        in_specs=placed,
        out_specs=(P(None, "lat", "lon"), P(), P(), P(), P()),
        check_vma=False,
    )
```

```python
import functools
import math

import jax
import jax.numpy as jnp
from jax import lax
from jax.experimental import pallas as pl
from jax.experimental.pallas import tpu as pltpu
from jax.sharding import PartitionSpec as P

MESH = pl.DeviceIdType.MESH
F32 = jnp.float32
BF16 = jnp.bfloat16

spread_coef = 0.15
level_eps = 1e-05

LEVELS = 100
ROWS = 8
LANES = 128
HIDDEN = 512
COLS = ROWS * LANES
PAD = 104
LAT = 8
LON = 32
SIDE = 4
CHIPS = SIDE * SIDE
PLANE = 2 * CHIPS
DEPTH = 8
HALF = HIDDEN // 2
ROWS_EACH = 2 * PAD // CHIPS


def ring(d, n):
    return min(d, n - d)


CHIP_STEPS = sorted(
    ((dx, dy) for dx in range(SIDE) for dy in range(SIDE)),
    key=lambda s: -(ring(s[0], SIDE) + ring(s[1], SIDE)),
)
Z_STEPS = sorted(range(1, DEPTH), key=lambda d: -ring(d, DEPTH))


def kernel(
    tracer_hbm, cot_hbm, land_hbm, bottom_hbm, kappa_hbm, w_in_hbm, b_in_hbm, w_out_hbm, b_out_hbm,
    out_ref, gw_in_ref, gb_in_ref, gw_out_ref, gb_out_ref,
    tr_v, cot_v, land_v, bottom_v, kappa_s, w_in_v, b_in_v, w_out_v, b_out_s,
    slabs, adj_slabs, edge_hi, edge_lo, edge2_hi, edge2_lo, halo, halo2, near_depth,
    small_src, small_r1, small_mid, small_r2,
    wi_f, wo_f, wi_b, w1t, wot, wo_b,
    inp, hid, slope, dpre, dlog, din,
    logit, mixed, val_x, val_y, mul_x, mul_y, gate, adj, dlev,
    given, kept, from_core, half, from_plane, mid, from_z, chunk, full,
    load_sems, small_send, small_recv, core_send, core_recv, plane_send, plane_recv,
    z_send, z_recv, gather_send, gather_recv, fwd_send, fwd_recv, halo_send, halo_recv,
):
    lat = lax.axis_index("lat")
    lon = lax.axis_index("lon")
    y_me = lat % SIDE
    x_me = (lat // SIDE) * 2 + lon // 16
    z_me = (lon // 2) % DEPTH
    core = lon % 2
    p_me = x_me * SIDE + y_me
    q_me = p_me * 2 + core
    mine = pl.ds(p_me * ROWS_EACH, ROWS_EACH)
    lon_z = z_me * 2

    loads = []
    for n, (src, dst) in enumerate(
        (
            (tracer_hbm, tr_v), (land_hbm, land_v), (bottom_hbm, bottom_v), (w_in_hbm, w_in_v),
            (b_in_hbm, b_in_v), (w_out_hbm, w_out_v), (cot_hbm, cot_v), (kappa_hbm, kappa_s),
            (b_out_hbm, b_out_s),
        )
    ):
        loads.append(pltpu.make_async_copy(src, dst, load_sems.at[n]))
    for load in loads[:3]:
        load.start()

    xs = [(x_me + d) % SIDE for d in range(SIDE)]
    ys = [(y_me + d) % SIDE for d in range(SIDE)]

    def chip_peer(dx, dy, dc):
        to_core = core if dc == 0 else 1 - core
        dev = ((xs[dx] // 2) * SIDE + ys[dy], (xs[dx] % 2) * 16 + lon_z + to_core)
        return xs[dx] * SIDE + ys[dy], dev

    def z_peer(d):
        return (lat, (lon // 16) * 16 + ((z_me + d) % DEPTH) * 2 + core)

    everyone = [(dx, dy, dc) for dx, dy in CHIP_STEPS for dc in (0, 1) if dx or dy or dc]
    same_core = [(dx, dy) for dx, dy in CHIP_STEPS if dx or dy]
    partner = (lat, lon + 1 - 2 * core)

    barrier = pltpu.get_barrier_semaphore()

    def greet(dev):
        pl.semaphore_signal(barrier, inc=1, device_id=dev, device_id_type=MESH)

    greet(z_peer(Z_STEPS[0]))
    for step in everyone:
        greet(chip_peer(*step)[1])
    for d in Z_STEPS[1:]:
        greet(z_peer(d))
    greet((lat, (lon + 2 * core - 1 + LON) % LON))
    for load in loads[3:]:
        load.start()

    row_id = lax.broadcasted_iota(jnp.int32, (PAD, LANES), 0)
    lane_id = lax.broadcasted_iota(jnp.int32, (PAD, LANES), 1)
    row_f = row_id.astype(F32)
    diag = row_id == lane_id

    def as_row(column):
        return jnp.sum(jnp.where(diag, column, 0.0), axis=0, keepdims=True)

    def as_column(row):
        return jnp.sum(jnp.where(diag, row, 0.0), axis=1, keepdims=True)

    for n in range(3):
        loads[n].wait()
    depth_all = (land_v[...] * bottom_v[...]).astype(F32)
    energy = jnp.zeros((PAD, LANES), F32)
    for i in range(ROWS):
        slabs[i, 0:LEVELS, :] = tr_v[:, i, :]
        slabs[i, LEVELS:PAD, :] = jnp.broadcast_to(depth_all[i : i + 1, :], (PAD - LEVELS, LANES))
        wet_x = jnp.where(row_f < depth_all[i : i + 1, :], slabs[i], 0.0)
        energy = energy + wet_x * wet_x
    small_src[...] = as_row(jnp.sum(energy, axis=1, keepdims=True))
    small_r1[q_me] = small_src[...]

    pl.semaphore_wait(barrier, PLANE - 1 + DEPTH - 1 + 1)

    def post(src, dst, dev, send, recv):
        pltpu.make_async_remote_copy(
            src, dst, send, recv, device_id=dev, device_id_type=MESH
        ).start()

    def send_z(src, dst, send, recv):
        for d in Z_STEPS:
            post(src, dst.at[z_me], z_peer(d), send, recv)

    def drain(ref, sem):
        pltpu.make_async_copy(ref, ref, sem).wait()

    def send_halo(k, pieces, dst):
        up = (lat + 1) % LAT
        down = (lat + LAT - 1) % LAT
        right = (lon + 1) % LON
        left = (lon + LON - 1) % LON
        targets = ((up, lon), (down, lon), (lat, right), (lat, left))
        copies = []
        for n, (src, dev) in enumerate(zip(pieces, targets)):
            copy = pltpu.make_async_remote_copy(
                src, dst.at[n], halo_send.at[4 * k + n], halo_recv.at[4 * k + n],
                device_id=dev, device_id_type=MESH,
            )
            copy.start()
            copies.append(copy)
        return copies

    for step in everyone:
        post(small_src, small_r1.at[q_me], chip_peer(*step)[1], small_send.at[0], small_recv.at[0])
    hi = jnp.zeros((PAD, LANES), F32)
    lo = jnp.zeros((PAD, LANES), F32)
    for i in range(ROWS):
        x = slabs[i]
        hi = jnp.where(lane_id == i, pltpu.roll(x, i + 1, 1), hi)
        lo = jnp.where(lane_id == i, pltpu.roll(x, i, 1) if i else x, lo)
    edge_hi[...] = hi
    edge_lo[...] = lo
    halo_copies = send_halo(0, (slabs.at[ROWS - 1], slabs.at[0], edge_hi, edge_lo), halo)

    for n in range(3, 6):
        loads[n].wait()
    bias = b_in_v[...].reshape(1, HIDDEN)
    bias_hi = bias.astype(BF16).astype(F32)
    bias_mid = (bias - bias_hi).astype(BF16).astype(F32)
    bias_lo = bias - bias_hi - bias_mid
    wi_f[LEVELS:LANES, :] = jnp.zeros((LANES - LEVELS, HIDDEN), F32)
    wi_f[0:LEVELS, :] = w_in_v[...].astype(F32)
    wi_f[LEVELS : LEVELS + 1, :] = bias_hi
    wi_f[LEVELS + 1 : LEVELS + 2, :] = bias_mid
    wi_f[LEVELS + 2 : LEVELS + 3, :] = bias_lo
    wi_b[...] = wi_f[...].astype(BF16)
    w1t[...] = wi_f[...].T.astype(BF16)
    wo_f[LEVELS:LANES, :] = jnp.zeros((LANES - LEVELS, HIDDEN), F32)
    wo_f[0:LEVELS, :] = w_out_v[...].astype(F32)
    wot[...] = wo_f[...].astype(BF16)
    wo_b[...] = wo_f[...].T.astype(BF16)
    dlev[LEVELS:LANES] = jnp.zeros((LANES - LEVELS, ROWS, LANES), F32)
    for i in range(ROWS):
        adj_slabs[i, LEVELS:PAD, :] = jnp.zeros((PAD - LEVELS, LANES), F32)
    edge2_hi[LEVELS:PAD, :] = jnp.zeros((PAD - LEVELS, LANES), F32)
    edge2_lo[LEVELS:PAD, :] = jnp.zeros((PAD - LEVELS, LANES), F32)
    inp[PAD - 8 : LANES, :] = jnp.zeros((LANES - PAD + 8, COLS), BF16)
    for n in range(6, 9):
        loads[n].wait()

    drain(small_r1.at[pl.ds(0, PLANE - 1)], small_recv.at[0])
    small_mid[...] = jnp.sum(small_r1[...], axis=0)
    small_r2[z_me] = small_mid[...]
    send_z(small_mid, small_r2, small_send.at[1], small_recv.at[1])

    for copy in halo_copies:
        copy.wait_recv()

    def neighbours(field, edges, i):
        centre = field[i]
        below = field[i + 1] if i + 1 < ROWS else edges[1]
        above = field[i - 1] if i else edges[0]
        from_left = pltpu.roll(edges[2], LANES - i, 1) if i else edges[2]
        left = jnp.where(lane_id == 0, from_left, pltpu.roll(centre, 1, 1))
        right = jnp.where(
            lane_id == LANES - 1, pltpu.roll(edges[3], LANES - 1 - i, 1), pltpu.roll(centre, LANES - 1, 1)
        )
        return centre, (below, above, left, right)

    def flux(centre, near, i):
        total = jnp.zeros((PAD, LANES), F32)
        for n in range(4):
            total = total + jnp.where(
                row_f < near_depth[n * ROWS + i : n * ROWS + i + 1, :], near[n] - centre, 0.0
            )
        return centre + spread_coef * total

    has_above = jnp.where(lat > 0, 1.0, 0.0)
    has_below = jnp.where(lat < LAT - 1, 1.0, 0.0)
    for i in range(ROWS):
        centre, near = neighbours(slabs, halo, i)
        own = centre[LEVELS : LEVELS + 1, :]
        for n in range(4):
            other = near[n][LEVELS : LEVELS + 1, :]
            if n == 0 and i == ROWS - 1:
                other = other * has_below
            if n == 1 and i == 0:
                other = other * has_above
            near_depth[n * ROWS + i : n * ROWS + i + 1, :] = jnp.minimum(own, other)
        mixed[:, i, :] = flux(centre, near, i)[0:LEVELS]

    drain(small_r2.at[pl.ds(0, DEPTH - 1)], small_recv.at[1])
    energy_all = as_column(jnp.sum(small_r2[...], axis=0))
    count = float(LAT * LON * COLS)
    radius = jnp.sqrt(energy_all / count + level_eps)
    inv_radius = 1.0 / radius

    def wet_slab(i):
        x = slabs[i]
        return jnp.where(row_f < x[LEVELS : LEVELS + 1, :], x, 0.0)

    one_rows = jnp.where(row_id < LEVELS + 3, 1.0, 0.0)
    for i in range(ROWS):
        scaled = jnp.where(row_id < LEVELS, wet_slab(i) * inv_radius, one_rows)
        scaled = jnp.concatenate([scaled, jnp.zeros((LANES - PAD, LANES), F32)], axis=0)
        inp[:, i * LANES : (i + 1) * LANES] = scaled.astype(BF16)

    width = 256
    for j in range(COLS // width):
        cols = slice(j * width, (j + 1) * width)
        pre = jnp.dot(w1t[...], inp[:, cols], preferred_element_type=F32)
        sig = 1.0 / (1.0 + jnp.exp(-pre))
        act = pre * sig
        hid[:, cols] = act.astype(BF16)
        slope[:, cols] = sig * (1.0 + pre * (1.0 - sig))
        out = jnp.dot(wot[...], hid[:, cols], preferred_element_type=F32)
        for s in range(width // LANES):
            logit[:, j * (width // LANES) + s, :] = out[0:LEVELS, s * LANES : (s + 1) * LANES]

    depth = depth_all
    middle = LEVELS // 2

    def level_terms(k):
        x = logit[k] + b_out_s[k]
        ex = jnp.exp(-jnp.abs(x))
        soft = jnp.maximum(x, 0.0) + jnp.log1p(ex)
        sig = jnp.where(x >= 0.0, 1.0, ex) / (1.0 + ex)
        kf = (k + 1).astype(F32)
        open_face = kf < depth
        kap = kappa_s[k]
        down = jnp.where(open_face, kap + soft, 0.0)
        up = jnp.where(open_face, kap, 0.0)
        gate[k] = jnp.where(open_face, sig, 0.0)
        return down, up

    def eliminate(s, carry):
        down_p, up_p, r_p, v_p, w_p, sb_n, u_n, z_n = carry
        k = s
        down, up = level_terms(k)
        pivot = 1.0 + down + up_p - down_p * up_p * r_p
        r = 1.0 / pivot
        v = (mixed[k] + down_p * v_p) * r
        w = (cot_v[k] + up_p * w_p) * r
        val_x[k] = v
        val_y[k] = w
        mul_x[k] = up * r
        mul_y[k] = down * r
        b = LEVELS - 1 - s
        down_b, up_b = level_terms(b)
        up_above = jnp.where(b.astype(F32) < depth, kappa_s[b - 1], 0.0)
        pivot_b = 1.0 + down_b + up_above - down_b * up_b * sb_n
        sb = 1.0 / pivot_b
        u = (mixed[b] + up_b * u_n) * sb
        zz = (cot_v[b] + down_b * z_n) * sb
        val_x[b] = u
        val_y[b] = zz
        mul_y[b] = up_above * sb
        mul_x[b + 1] = down_b * sb_n
        return down, up, r, v, w, sb, u, zz

    zero = jnp.zeros((ROWS, LANES), F32)
    down_m, up_m, r_m, v_m, w_m, sb_m, u_m, z_m = lax.fori_loop(
        0, middle, eliminate, (zero,) * 8, unroll=5
    )
    ratio_x = up_m * r_m
    ratio_y = down_m * r_m
    back_x = down_m * sb_m
    back_y = up_m * sb_m
    inv_det = 1.0 / (1.0 - ratio_x * back_x)
    x_top = (v_m + ratio_x * u_m) * inv_det
    x_bot = u_m + back_x * x_top
    y_top = (w_m + ratio_y * z_m) * inv_det
    y_bot = z_m + back_y * y_top
    adj[middle - 1] = y_top
    adj[middle] = y_bot
    dlev[middle - 1] = gate[middle - 1] * x_top * (y_bot - y_top)

    def substitute(s, carry):
        x_t, y_t, x_b, y_b = carry
        k = middle - 1 - s
        x_n = val_x[k] + mul_x[k] * x_t
        y_n = val_y[k] + mul_y[k] * y_t
        adj[k] = y_n
        dlev[k] = gate[k] * x_n * (y_t - y_n)
        b = middle + s
        x_c = val_x[b] + mul_x[b] * x_b
        y_c = val_y[b] + mul_y[b] * y_b
        adj[b] = y_c
        dlev[b - 1] = gate[b - 1] * x_b * (y_c - y_b)
        return x_n, y_n, x_c, y_c

    lax.fori_loop(1, middle, substitute, (x_top, y_top, x_bot, y_bot), unroll=7)
    dlev[LEVELS - 1] = zero

    for i in range(ROWS):
        dlog[:, i * LANES : (i + 1) * LANES] = dlev[:, i, :].astype(BF16)
    for j in range(COLS // width):
        cols = slice(j * width, (j + 1) * width)
        back = jnp.dot(wo_b[...], dlog[:, cols], preferred_element_type=F32)
        dpre[:, cols] = (back * slope[:, cols]).astype(BF16)
    contract_last = (((1,), (1,)), ((), ()))
    sources = ((inp, dpre), (dlog, hid))

    def half_into(ref, m, c):
        small, big = sources[m]
        rows = big[pl.ds(pl.multiple_of(c * HALF, HALF), HALF), :]
        value = lax.dot_general(small[...], rows, contract_last, preferred_element_type=F32)
        ref[m, 0:PAD, :] = value[0:PAD, 0:LANES]
        ref[m, PAD : 2 * PAD, :] = value[0:PAD, LANES:HALF]

    for m in range(2):
        half_into(given, m, 1 - core)
        post(given.at[m], from_core.at[m], partner, core_send.at[m], core_recv.at[m])
    for m in range(2):
        half_into(kept, m, core)

    for m in range(2):
        drain(from_core.at[m], core_recv.at[m])
        half[m] = kept[m] + from_core[m]
        if m:
            half[1, LEVELS : LEVELS + 1, :] = lax.dot_general(
                jnp.ones((16, COLS), BF16), dlog[...], contract_last, preferred_element_type=F32
            )[0:1]
        for dx, dy in same_core:
            p, dev = chip_peer(dx, dy, 0)
            post(
                half.at[m, pl.ds(p * ROWS_EACH, ROWS_EACH)], from_plane.at[m, p_me], dev,
                plane_send.at[m], plane_recv.at[m],
            )
        from_plane[m, p_me] = half[m, mine, :]

    hi = jnp.zeros((LEVELS, LANES), F32)
    lo = jnp.zeros((LEVELS, LANES), F32)
    lane_l = lane_id[0:LEVELS]
    for i in range(ROWS):
        x = adj[:, i, :]
        adj_slabs[i, 0:LEVELS, :] = x
        hi = jnp.where(lane_l == i, pltpu.roll(x, i + 1, 1), hi)
        lo = jnp.where(lane_l == i, pltpu.roll(x, i, 1) if i else x, lo)
    edge2_hi[0:LEVELS, :] = hi
    edge2_lo[0:LEVELS, :] = lo
    for j in range(COLS // width):
        cols = slice(j * width, (j + 1) * width)
        out = jnp.dot(wi_b[...], dpre[:, cols], preferred_element_type=F32)
        for s in range(width // LANES):
            i = j * (width // LANES) + s
            din[i] = out[0:PAD, s * LANES : (s + 1) * LANES] * inv_radius

    scale = 1.0 / math.sqrt(count)
    for m in range(2):
        drain(from_plane.at[m, pl.ds(0, CHIPS - 1)], plane_recv.at[m])
        mid[m] = jnp.sum(from_plane[m], axis=0)
        from_z[m, z_me] = mid[m]
        send_z(mid.at[m], from_z.at[m], z_send.at[m], z_recv.at[m])

    halo2_copies = send_halo(
        1, (adj_slabs.at[ROWS - 1], adj_slabs.at[0], edge2_hi, edge2_lo), halo2
    )
    for m in range(2):
        drain(from_z.at[m, pl.ds(0, DEPTH - 1)], z_recv.at[m])
        chunk[m] = jnp.sum(from_z[m], axis=0) * scale
        for dx, dy in same_core:
            _, dev = chip_peer(dx, dy, 0)
            post(chunk.at[m], full.at[m, core, mine], dev, gather_send.at[m], gather_recv.at[m])
        full[m, core, mine, :] = chunk[m]

    for copy in halo2_copies:
        copy.wait_recv()
    for i in range(ROWS):
        centre, near = neighbours(adj_slabs, halo2, i)
        wet = row_f < slabs[i, LEVELS : LEVELS + 1, :]
        din[i] = flux(centre, near, i) + jnp.where(wet, din[i], 0.0)

    peers_rows = pl.ds(0, (CHIPS - 1) * ROWS_EACH)
    for m in range(2):
        drain(full.at[m, core, peers_rows], gather_recv.at[m])
        post(full.at[m, core], full.at[m, core], partner, fwd_send.at[m], fwd_recv.at[m])

    def deliver(m, ref):
        for c in range(2):
            for h in range(2):
                n = 2 * c + h
                ref[:, n * LANES : (n + 1) * LANES] = full[m, c, h * PAD : h * PAD + LEVELS, :]

    drain(full.at[0, 1 - core], fwd_recv.at[0])
    weighted = jnp.zeros((PAD, LANES), F32)
    for c in range(2):
        for h in range(2):
            n = 2 * c + h
            part = full[0, c, h * PAD : (h + 1) * PAD, :]
            weighted = weighted + wi_f[0:PAD, n * LANES : (n + 1) * LANES] * part
            gb_in_ref[:, n * LANES : (n + 1) * LANES] = part[LEVELS : LEVELS + 1, :]
    level_sum = radius * jnp.sum(weighted, axis=1, keepdims=True) * math.sqrt(count)
    level_scale = level_sum / (count * radius * radius * radius)
    for i in range(ROWS):
        out_ref[:, i, :] = (din[i] - wet_slab(i) * level_scale)[0:LEVELS]
    deliver(0, gw_in_ref)
    drain(full.at[1, 1 - core], fwd_recv.at[1])
    deliver(1, gw_out_ref)
    gb_out_ref[...] = full[1, 0, LEVELS : LEVELS + 1, :] + full[1, 1, LEVELS : LEVELS + 1, :]

    for copy in halo_copies + halo2_copies:
        copy.wait_send()
    drain(small_r1.at[pl.ds(0, PLANE - 1)], small_send.at[0])
    drain(small_r2.at[pl.ds(0, DEPTH - 1)], small_send.at[1])
    for m in range(2):
        drain(from_core.at[m], core_send.at[m])
        drain(from_plane.at[m, pl.ds(0, CHIPS - 1)], plane_send.at[m])
        drain(from_z.at[m, pl.ds(0, DEPTH - 1)], z_send.at[m])
        drain(full.at[m, core, peers_rows], gather_send.at[m])
        drain(full.at[m, core], fwd_send.at[m])


def store_results(out_v, gw_in_v, gb_in_v, gw_out_v, gb_out_v, out_h, gw_in_h, gb_in_ref, gw_out_h, gb_out_ref, sems):
    copies = []
    for n, (src, dst) in enumerate(((out_v, out_h), (gw_in_v, gw_in_h), (gw_out_v, gw_out_h))):
        copy = pltpu.make_async_copy(src, dst, sems.at[n])
        copy.start()
        copies.append(copy)
    gb_in_ref[...] = gb_in_v[...].reshape(HIDDEN)
    gb_out_ref[...] = gb_out_v[...].reshape(LANES)[0:LEVELS]
    for copy in copies:
        copy.wait()


def shards(tracer, cotangent, land_mask, bottom, kappa, w_in, b_in, w_out, b_out):
    vmem = pl.BlockSpec(memory_space=pltpu.VMEM)
    hbm = pl.BlockSpec(memory_space=pltpu.HBM)
    slab = (ROWS, PAD, LANES)
    levels = (LEVELS, ROWS, LANES)
    edge = (PAD, LANES)
    flat = (2 * PAD, LANES)
    piece = (ROWS_EACH, LANES)

    def v(*shape, dtype=F32):
        return pltpu.VMEM(shape, dtype)

    def sems(n):
        return pltpu.SemaphoreType.DMA((n,))

    scratch = [
        v(*levels), v(*levels), v(ROWS, LANES, dtype=jnp.int32), v(ROWS, LANES, dtype=jnp.int32),
        pltpu.SMEM((LEVELS,), F32), v(LEVELS, HIDDEN, dtype=BF16), v(HIDDEN),
        v(LEVELS, HIDDEN, dtype=BF16), pltpu.SMEM((LEVELS,), F32),
        v(*slab), v(*slab), v(*edge), v(*edge), v(*edge), v(*edge),
        v(4, *edge), v(4, *edge), v(4 * ROWS, LANES),
        v(1, LANES), v(PLANE, 1, LANES), v(1, LANES), v(DEPTH, 1, LANES),
        v(LANES, HIDDEN), v(LANES, HIDDEN), v(LANES, HIDDEN, dtype=BF16),
        v(HIDDEN, LANES, dtype=BF16), v(LANES, HIDDEN, dtype=BF16), v(HIDDEN, LANES, dtype=BF16),
        v(LANES, COLS, dtype=BF16), v(HIDDEN, COLS, dtype=BF16), v(HIDDEN, COLS),
        v(HIDDEN, COLS, dtype=BF16), v(LANES, COLS, dtype=BF16), v(*slab),
        v(*levels), v(*levels), v(*levels), v(*levels), v(LEVELS + 1, ROWS, LANES),
        v(*levels), v(*levels), v(*levels), v(LANES, ROWS, LANES),
        v(2, *flat), v(2, *flat), v(2, *flat), v(2, *flat), v(2, CHIPS, *piece),
        v(2, *piece), v(2, DEPTH, *piece), v(2, *piece), v(2, 2, *flat),
        sems(9), sems(2), sems(2), sems(2), sems(2), sems(2), sems(2),
        sems(2), sems(2), sems(2), sems(2), sems(2), sems(2), sems(8), sems(8),
    ]
    shapes = (
        jax.ShapeDtypeStruct(tracer.shape, F32),
        jax.ShapeDtypeStruct((LEVELS, HIDDEN), F32),
        jax.ShapeDtypeStruct((1, HIDDEN), F32),
        jax.ShapeDtypeStruct((LEVELS, HIDDEN), F32),
        jax.ShapeDtypeStruct((1, LANES), F32),
    )
    operands = (tracer, cotangent, land_mask, bottom, kappa, w_in, b_in, w_out.T, b_out)
    results = pl.pallas_call(
        kernel,
        out_shape=shapes,
        in_specs=[hbm] * 9,
        out_specs=(vmem,) * 5,
        scratch_shapes=scratch,
        compiler_params=pltpu.CompilerParams(
            collective_id=0, has_side_effects=True, vmem_limit_bytes=40 * 1024 * 1024
        ),
        name="step_adjoint",
    )(*(pltpu.with_memory_space_constraint(a, pltpu.HBM) for a in operands))
    out, gw_in, gb_in, gw_out, gb_out = pl.pallas_call(
        store_results,
        out_shape=shapes[:2]
        + (jax.ShapeDtypeStruct((HIDDEN,), F32), shapes[3], jax.ShapeDtypeStruct((LEVELS,), F32)),
        in_specs=[vmem] * 5,
        out_specs=(hbm, hbm, vmem, hbm, vmem),
        scratch_shapes=[sems(3)],
        compiler_params=pltpu.CompilerParams(vmem_limit_bytes=1024 * 1024),
        name="store_results",
    )(*results)
    return out, gw_in, gb_in, gw_out.T, gb_out


def solution(mesh):
    placed = (
        P(None, "lat", "lon"),
        P(None, "lat", "lon"),
        P("lat", "lon"),
        P("lat", "lon"),
        P(),
        P(),
        P(),
        P(),
        P(),
    )
    return jax.shard_map(
        shards,
        mesh=mesh,
        in_specs=placed,
        out_specs=(P(None, "lat", "lon"), P(), P(), P(), P()),
        check_vma=False,
    )
```

```python
import functools
import math

import jax
import jax.numpy as jnp
from jax import lax
from jax.experimental import pallas as pl
from jax.experimental.pallas import tpu as pltpu
from jax.sharding import PartitionSpec as P

MESH = pl.DeviceIdType.MESH
F32 = jnp.float32
BF16 = jnp.bfloat16

spread_coef = 0.15
level_eps = 1e-05

LEVELS = 100
ROWS = 8
LANES = 128
HIDDEN = 512
COLS = ROWS * LANES
PAD = 104
LAT = 8
LON = 32
SIDE = 4
CHIPS = SIDE * SIDE
PLANE = 2 * CHIPS
DEPTH = 8
HALF = HIDDEN // 2
ROWS_EACH = 2 * PAD // CHIPS


def ring(d, n):
    return min(d, n - d)


CHIP_STEPS = sorted(
    ((dx, dy) for dx in range(SIDE) for dy in range(SIDE)),
    key=lambda s: -(ring(s[0], SIDE) + ring(s[1], SIDE)),
)
Z_STEPS = sorted(range(1, DEPTH), key=lambda d: -ring(d, DEPTH))


def kernel(
    tracer_hbm, cot_hbm, land_hbm, bottom_hbm, kappa_hbm, w_in_hbm, b_in_hbm, w_out_hbm, b_out_hbm,
    out_ref, gw_in_ref, gb_in_ref, gw_out_ref, gb_out_ref,
    tr_v, cot_v, land_v, bottom_v, kappa_s, w_in_v, b_in_v, w_out_v, b_out_s,
    slabs, adj_slabs, edge_hi, edge_lo, edge2_hi, edge2_lo, halo, halo2, near_depth,
    small_src, small_r1, small_mid, small_r2,
    wi_f, wo_f, wi_b, w1t, wot, wo_b,
    inp, hid, slope, dpre, dlog, din,
    logit, mixed, val_x, val_y, mul_x, mul_y, gate, adj, dlev,
    grad, from_core, half, from_plane, mid, from_z, chunk, full,
    load_sems, small_send, small_recv, core_send, core_recv, plane_send, plane_recv,
    z_send, z_recv, gather_send, gather_recv, fwd_send, fwd_recv, halo_send, halo_recv,
):
    lat = lax.axis_index("lat")
    lon = lax.axis_index("lon")
    y_me = lat % SIDE
    x_me = (lat // SIDE) * 2 + lon // 16
    z_me = (lon // 2) % DEPTH
    core = lon % 2
    p_me = x_me * SIDE + y_me
    q_me = p_me * 2 + core
    mine = pl.ds(p_me * ROWS_EACH, ROWS_EACH)
    lon_z = z_me * 2

    loads = []
    for n, (src, dst) in enumerate(
        (
            (tracer_hbm, tr_v), (land_hbm, land_v), (bottom_hbm, bottom_v), (w_in_hbm, w_in_v),
            (b_in_hbm, b_in_v), (w_out_hbm, w_out_v), (cot_hbm, cot_v), (kappa_hbm, kappa_s),
            (b_out_hbm, b_out_s),
        )
    ):
        loads.append(pltpu.make_async_copy(src, dst, load_sems.at[n]))
    for load in loads[:3]:
        load.start()

    xs = [(x_me + d) % SIDE for d in range(SIDE)]
    ys = [(y_me + d) % SIDE for d in range(SIDE)]

    def chip_peer(dx, dy, dc):
        to_core = core if dc == 0 else 1 - core
        dev = ((xs[dx] // 2) * SIDE + ys[dy], (xs[dx] % 2) * 16 + lon_z + to_core)
        return xs[dx] * SIDE + ys[dy], dev

    def z_peer(d):
        return (lat, (lon // 16) * 16 + ((z_me + d) % DEPTH) * 2 + core)

    everyone = [(dx, dy, dc) for dx, dy in CHIP_STEPS for dc in (0, 1) if dx or dy or dc]
    same_core = [(dx, dy) for dx, dy in CHIP_STEPS if dx or dy]
    partner = (lat, lon + 1 - 2 * core)

    barrier = pltpu.get_barrier_semaphore()

    def greet(dev):
        pl.semaphore_signal(barrier, inc=1, device_id=dev, device_id_type=MESH)

    greet(z_peer(Z_STEPS[0]))
    for step in everyone:
        greet(chip_peer(*step)[1])
    for d in Z_STEPS[1:]:
        greet(z_peer(d))
    greet((lat, (lon + 2 * core - 1 + LON) % LON))
    for load in loads[3:]:
        load.start()

    row_id = lax.broadcasted_iota(jnp.int32, (PAD, LANES), 0)
    lane_id = lax.broadcasted_iota(jnp.int32, (PAD, LANES), 1)
    row_f = row_id.astype(F32)
    diag = row_id == lane_id

    def as_row(column):
        return jnp.sum(jnp.where(diag, column, 0.0), axis=0, keepdims=True)

    def as_column(row):
        return jnp.sum(jnp.where(diag, row, 0.0), axis=1, keepdims=True)

    for n in range(3):
        loads[n].wait()
    depth_all = (land_v[...] * bottom_v[...]).astype(F32)
    energy = jnp.zeros((PAD, LANES), F32)
    for i in range(ROWS):
        slabs[i, 0:LEVELS, :] = tr_v[:, i, :]
        slabs[i, LEVELS:PAD, :] = jnp.broadcast_to(depth_all[i : i + 1, :], (PAD - LEVELS, LANES))
        wet_x = jnp.where(row_f < depth_all[i : i + 1, :], slabs[i], 0.0)
        energy = energy + wet_x * wet_x
    small_src[...] = as_row(jnp.sum(energy, axis=1, keepdims=True))
    small_r1[q_me] = small_src[...]

    pl.semaphore_wait(barrier, PLANE - 1 + DEPTH - 1 + 1)

    def post(src, dst, dev, send, recv):
        pltpu.make_async_remote_copy(
            src, dst, send, recv, device_id=dev, device_id_type=MESH
        ).start()

    def send_z(src, dst, send, recv):
        for d in Z_STEPS:
            post(src, dst.at[z_me], z_peer(d), send, recv)

    def drain(ref, sem):
        pltpu.make_async_copy(ref, ref, sem).wait()

    def send_halo(k, pieces, dst):
        up = (lat + 1) % LAT
        down = (lat + LAT - 1) % LAT
        right = (lon + 1) % LON
        left = (lon + LON - 1) % LON
        targets = ((up, lon), (down, lon), (lat, right), (lat, left))
        copies = []
        for n, (src, dev) in enumerate(zip(pieces, targets)):
            copy = pltpu.make_async_remote_copy(
                src, dst.at[n], halo_send.at[4 * k + n], halo_recv.at[4 * k + n],
                device_id=dev, device_id_type=MESH,
            )
            copy.start()
            copies.append(copy)
        return copies

    for step in everyone:
        post(small_src, small_r1.at[q_me], chip_peer(*step)[1], small_send.at[0], small_recv.at[0])
    hi = jnp.zeros((PAD, LANES), F32)
    lo = jnp.zeros((PAD, LANES), F32)
    for i in range(ROWS):
        x = slabs[i]
        hi = jnp.where(lane_id == i, pltpu.roll(x, i + 1, 1), hi)
        lo = jnp.where(lane_id == i, pltpu.roll(x, i, 1) if i else x, lo)
    edge_hi[...] = hi
    edge_lo[...] = lo
    halo_copies = send_halo(0, (slabs.at[ROWS - 1], slabs.at[0], edge_hi, edge_lo), halo)

    for n in range(3, 6):
        loads[n].wait()
    bias = b_in_v[...].reshape(1, HIDDEN)
    bias_hi = bias.astype(BF16).astype(F32)
    bias_mid = (bias - bias_hi).astype(BF16).astype(F32)
    bias_lo = bias - bias_hi - bias_mid
    wi_f[LEVELS:LANES, :] = jnp.zeros((LANES - LEVELS, HIDDEN), F32)
    wi_f[0:LEVELS, :] = w_in_v[...].astype(F32)
    wi_f[LEVELS : LEVELS + 1, :] = bias_hi
    wi_f[LEVELS + 1 : LEVELS + 2, :] = bias_mid
    wi_f[LEVELS + 2 : LEVELS + 3, :] = bias_lo
    wi_b[...] = wi_f[...].astype(BF16)
    w1t[...] = wi_f[...].T.astype(BF16)
    wo_f[LEVELS:LANES, :] = jnp.zeros((LANES - LEVELS, HIDDEN), F32)
    wo_f[0:LEVELS, :] = w_out_v[...].astype(F32)
    wot[...] = wo_f[...].astype(BF16)
    wo_b[...] = wo_f[...].T.astype(BF16)
    dlev[LEVELS:LANES] = jnp.zeros((LANES - LEVELS, ROWS, LANES), F32)
    for i in range(ROWS):
        adj_slabs[i, LEVELS:PAD, :] = jnp.zeros((PAD - LEVELS, LANES), F32)
    edge2_hi[LEVELS:PAD, :] = jnp.zeros((PAD - LEVELS, LANES), F32)
    edge2_lo[LEVELS:PAD, :] = jnp.zeros((PAD - LEVELS, LANES), F32)
    inp[PAD - 8 : LANES, :] = jnp.zeros((LANES - PAD + 8, COLS), BF16)
    for n in range(6, 9):
        loads[n].wait()

    drain(small_r1.at[pl.ds(0, PLANE - 1)], small_recv.at[0])
    small_mid[...] = jnp.sum(small_r1[...], axis=0)
    small_r2[z_me] = small_mid[...]
    send_z(small_mid, small_r2, small_send.at[1], small_recv.at[1])

    for copy in halo_copies:
        copy.wait_recv()

    def neighbours(field, edges, i):
        centre = field[i]
        below = field[i + 1] if i + 1 < ROWS else edges[1]
        above = field[i - 1] if i else edges[0]
        from_left = pltpu.roll(edges[2], LANES - i, 1) if i else edges[2]
        left = jnp.where(lane_id == 0, from_left, pltpu.roll(centre, 1, 1))
        right = jnp.where(
            lane_id == LANES - 1, pltpu.roll(edges[3], LANES - 1 - i, 1), pltpu.roll(centre, LANES - 1, 1)
        )
        return centre, (below, above, left, right)

    def flux(centre, near, i):
        total = jnp.zeros((PAD, LANES), F32)
        for n in range(4):
            total = total + jnp.where(
                row_f < near_depth[n * ROWS + i : n * ROWS + i + 1, :], near[n] - centre, 0.0
            )
        return centre + spread_coef * total

    has_above = jnp.where(lat > 0, 1.0, 0.0)
    has_below = jnp.where(lat < LAT - 1, 1.0, 0.0)
    for i in range(ROWS):
        centre, near = neighbours(slabs, halo, i)
        own = centre[LEVELS : LEVELS + 1, :]
        for n in range(4):
            other = near[n][LEVELS : LEVELS + 1, :]
            if n == 0 and i == ROWS - 1:
                other = other * has_below
            if n == 1 and i == 0:
                other = other * has_above
            near_depth[n * ROWS + i : n * ROWS + i + 1, :] = jnp.minimum(own, other)
        mixed[:, i, :] = flux(centre, near, i)[0:LEVELS]

    drain(small_r2.at[pl.ds(0, DEPTH - 1)], small_recv.at[1])
    energy_all = as_column(jnp.sum(small_r2[...], axis=0))
    count = float(LAT * LON * COLS)
    radius = jnp.sqrt(energy_all / count + level_eps)
    inv_radius = 1.0 / radius

    def wet_slab(i):
        x = slabs[i]
        return jnp.where(row_f < x[LEVELS : LEVELS + 1, :], x, 0.0)

    one_rows = jnp.where(row_id < LEVELS + 3, 1.0, 0.0)
    for i in range(ROWS):
        scaled = jnp.where(row_id < LEVELS, wet_slab(i) * inv_radius, one_rows)
        scaled = jnp.concatenate([scaled, jnp.zeros((LANES - PAD, LANES), F32)], axis=0)
        inp[:, i * LANES : (i + 1) * LANES] = scaled.astype(BF16)

    width = 256
    for j in range(COLS // width):
        cols = slice(j * width, (j + 1) * width)
        pre = jnp.dot(w1t[...], inp[:, cols], preferred_element_type=F32)
        sig = 1.0 / (1.0 + jnp.exp(-pre))
        act = pre * sig
        hid[:, cols] = act.astype(BF16)
        slope[:, cols] = sig * (1.0 + pre * (1.0 - sig))
        out = jnp.dot(wot[...], hid[:, cols], preferred_element_type=F32)
        for s in range(width // LANES):
            logit[:, j * (width // LANES) + s, :] = out[0:LEVELS, s * LANES : (s + 1) * LANES]

    depth = depth_all
    middle = LEVELS // 2

    def level_terms(k):
        x = logit[k] + b_out_s[k]
        ex = jnp.exp(-jnp.abs(x))
        soft = jnp.maximum(x, 0.0) + jnp.log1p(ex)
        sig = jnp.where(x >= 0.0, 1.0, ex) / (1.0 + ex)
        kf = (k + 1).astype(F32)
        open_face = kf < depth
        kap = kappa_s[k]
        down = jnp.where(open_face, kap + soft, 0.0)
        up = jnp.where(open_face, kap, 0.0)
        gate[k] = jnp.where(open_face, sig, 0.0)
        return down, up

    def eliminate(s, carry):
        down_p, up_p, r_p, v_p, w_p, sb_n, u_n, z_n = carry
        k = s
        down, up = level_terms(k)
        pivot = 1.0 + down + up_p - down_p * up_p * r_p
        r = 1.0 / pivot
        v = (mixed[k] + down_p * v_p) * r
        w = (cot_v[k] + up_p * w_p) * r
        val_x[k] = v
        val_y[k] = w
        mul_x[k] = up * r
        mul_y[k] = down * r
        b = LEVELS - 1 - s
        down_b, up_b = level_terms(b)
        up_above = jnp.where(b.astype(F32) < depth, kappa_s[b - 1], 0.0)
        pivot_b = 1.0 + down_b + up_above - down_b * up_b * sb_n
        sb = 1.0 / pivot_b
        u = (mixed[b] + up_b * u_n) * sb
        zz = (cot_v[b] + down_b * z_n) * sb
        val_x[b] = u
        val_y[b] = zz
        mul_y[b] = up_above * sb
        mul_x[b + 1] = down_b * sb_n
        return down, up, r, v, w, sb, u, zz

    zero = jnp.zeros((ROWS, LANES), F32)
    down_m, up_m, r_m, v_m, w_m, sb_m, u_m, z_m = lax.fori_loop(
        0, middle, eliminate, (zero,) * 8, unroll=5
    )
    ratio_x = up_m * r_m
    ratio_y = down_m * r_m
    back_x = down_m * sb_m
    back_y = up_m * sb_m
    inv_det = 1.0 / (1.0 - ratio_x * back_x)
    x_top = (v_m + ratio_x * u_m) * inv_det
    x_bot = u_m + back_x * x_top
    y_top = (w_m + ratio_y * z_m) * inv_det
    y_bot = z_m + back_y * y_top
    adj[middle - 1] = y_top
    adj[middle] = y_bot
    dlev[middle - 1] = gate[middle - 1] * x_top * (y_bot - y_top)

    def substitute(s, carry):
        x_t, y_t, x_b, y_b = carry
        k = middle - 1 - s
        x_n = val_x[k] + mul_x[k] * x_t
        y_n = val_y[k] + mul_y[k] * y_t
        adj[k] = y_n
        dlev[k] = gate[k] * x_n * (y_t - y_n)
        b = middle + s
        x_c = val_x[b] + mul_x[b] * x_b
        y_c = val_y[b] + mul_y[b] * y_b
        adj[b] = y_c
        dlev[b - 1] = gate[b - 1] * x_b * (y_c - y_b)
        return x_n, y_n, x_c, y_c

    lax.fori_loop(1, middle, substitute, (x_top, y_top, x_bot, y_bot), unroll=7)
    dlev[LEVELS - 1] = zero

    for i in range(ROWS):
        dlog[:, i * LANES : (i + 1) * LANES] = dlev[:, i, :].astype(BF16)
    for j in range(COLS // width):
        cols = slice(j * width, (j + 1) * width)
        back = jnp.dot(wo_b[...], dlog[:, cols], preferred_element_type=F32)
        dpre[:, cols] = (back * slope[:, cols]).astype(BF16)
    contract_last = (((1,), (1,)), ((), ()))
    sources = ((inp, dpre), (dlog, hid))

    for m, (small, big) in enumerate(sources):
        value = lax.dot_general(small[...], big[...], contract_last, preferred_element_type=F32)
        for n in range(4):
            grad[m, n // 2, (n % 2) * PAD : (n % 2 + 1) * PAD, :] = value[
                0:PAD, n * LANES : (n + 1) * LANES
            ]
        post(grad.at[m, 1 - core], from_core.at[m], partner, core_send.at[m], core_recv.at[m])

    for m in range(2):
        drain(from_core.at[m], core_recv.at[m])
        half[m] = grad[m, core] + from_core[m]
        if m:
            half[1, LEVELS : LEVELS + 1, :] = lax.dot_general(
                jnp.ones((16, COLS), BF16), dlog[...], contract_last, preferred_element_type=F32
            )[0:1]
        for dx, dy in same_core:
            p, dev = chip_peer(dx, dy, 0)
            post(
                half.at[m, pl.ds(p * ROWS_EACH, ROWS_EACH)], from_plane.at[m, p_me], dev,
                plane_send.at[m], plane_recv.at[m],
            )
        from_plane[m, p_me] = half[m, mine, :]

    hi = jnp.zeros((LEVELS, LANES), F32)
    lo = jnp.zeros((LEVELS, LANES), F32)
    lane_l = lane_id[0:LEVELS]
    for i in range(ROWS):
        x = adj[:, i, :]
        adj_slabs[i, 0:LEVELS, :] = x
        hi = jnp.where(lane_l == i, pltpu.roll(x, i + 1, 1), hi)
        lo = jnp.where(lane_l == i, pltpu.roll(x, i, 1) if i else x, lo)
    edge2_hi[0:LEVELS, :] = hi
    edge2_lo[0:LEVELS, :] = lo
    for j in range(COLS // width):
        cols = slice(j * width, (j + 1) * width)
        out = jnp.dot(wi_b[...], dpre[:, cols], preferred_element_type=F32)
        for s in range(width // LANES):
            i = j * (width // LANES) + s
            din[i] = out[0:PAD, s * LANES : (s + 1) * LANES] * inv_radius

    scale = 1.0 / math.sqrt(count)
    for m in range(2):
        drain(from_plane.at[m, pl.ds(0, CHIPS - 1)], plane_recv.at[m])
        mid[m] = jnp.sum(from_plane[m], axis=0)
        from_z[m, z_me] = mid[m]
        send_z(mid.at[m], from_z.at[m], z_send.at[m], z_recv.at[m])

    halo2_copies = send_halo(
        1, (adj_slabs.at[ROWS - 1], adj_slabs.at[0], edge2_hi, edge2_lo), halo2
    )
    for m in range(2):
        drain(from_z.at[m, pl.ds(0, DEPTH - 1)], z_recv.at[m])
        chunk[m] = jnp.sum(from_z[m], axis=0) * scale
        for dx, dy in same_core:
            _, dev = chip_peer(dx, dy, 0)
            post(chunk.at[m], full.at[m, core, mine], dev, gather_send.at[m], gather_recv.at[m])
        full[m, core, mine, :] = chunk[m]

    for copy in halo2_copies:
        copy.wait_recv()
    for i in range(ROWS):
        centre, near = neighbours(adj_slabs, halo2, i)
        wet = row_f < slabs[i, LEVELS : LEVELS + 1, :]
        din[i] = flux(centre, near, i) + jnp.where(wet, din[i], 0.0)

    peers_rows = pl.ds(0, (CHIPS - 1) * ROWS_EACH)
    for m in range(2):
        drain(full.at[m, core, peers_rows], gather_recv.at[m])
        post(full.at[m, core], full.at[m, core], partner, fwd_send.at[m], fwd_recv.at[m])

    def deliver(m, ref):
        for c in range(2):
            for h in range(2):
                n = 2 * c + h
                ref[:, n * LANES : (n + 1) * LANES] = full[m, c, h * PAD : h * PAD + LEVELS, :]

    drain(full.at[0, 1 - core], fwd_recv.at[0])
    weighted = jnp.zeros((PAD, LANES), F32)
    for c in range(2):
        for h in range(2):
            n = 2 * c + h
            part = full[0, c, h * PAD : (h + 1) * PAD, :]
            weighted = weighted + wi_f[0:PAD, n * LANES : (n + 1) * LANES] * part
            gb_in_ref[:, n * LANES : (n + 1) * LANES] = part[LEVELS : LEVELS + 1, :]
    level_sum = radius * jnp.sum(weighted, axis=1, keepdims=True) * math.sqrt(count)
    level_scale = level_sum / (count * radius * radius * radius)
    for i in range(ROWS):
        out_ref[:, i, :] = (din[i] - wet_slab(i) * level_scale)[0:LEVELS]
    deliver(0, gw_in_ref)
    drain(full.at[1, 1 - core], fwd_recv.at[1])
    deliver(1, gw_out_ref)
    gb_out_ref[...] = full[1, 0, LEVELS : LEVELS + 1, :] + full[1, 1, LEVELS : LEVELS + 1, :]

    for copy in halo_copies + halo2_copies:
        copy.wait_send()
    drain(small_r1.at[pl.ds(0, PLANE - 1)], small_send.at[0])
    drain(small_r2.at[pl.ds(0, DEPTH - 1)], small_send.at[1])
    for m in range(2):
        drain(from_core.at[m], core_send.at[m])
        drain(from_plane.at[m, pl.ds(0, CHIPS - 1)], plane_send.at[m])
        drain(from_z.at[m, pl.ds(0, DEPTH - 1)], z_send.at[m])
        drain(full.at[m, core, peers_rows], gather_send.at[m])
        drain(full.at[m, core], fwd_send.at[m])


def store_results(
    out_v, gw_in_v, gb_in_v, gw_out_v, gb_out_v, out_h, gw_in_h, gb_in_h, gw_out_h, gb_out_h,
    gb_in_flat, gb_out_flat, sems,
):
    pairs = (
        (out_v, out_h), (gw_in_v, gw_in_h), (gw_out_v, gw_out_h),
        (gb_in_flat, gb_in_h), (gb_out_flat, gb_out_h),
    )
    copies = [pltpu.make_async_copy(src, dst, sems.at[n]) for n, (src, dst) in enumerate(pairs)]
    for copy in copies[:3]:
        copy.start()
    gb_in_flat[...] = gb_in_v[...].reshape(HIDDEN)
    gb_out_flat[...] = gb_out_v[...].reshape(LANES)[0:LEVELS]
    for copy in copies[3:]:
        copy.start()
    for copy in copies:
        copy.wait()


def shards(tracer, cotangent, land_mask, bottom, kappa, w_in, b_in, w_out, b_out):
    vmem = pl.BlockSpec(memory_space=pltpu.VMEM)
    hbm = pl.BlockSpec(memory_space=pltpu.HBM)
    slab = (ROWS, PAD, LANES)
    levels = (LEVELS, ROWS, LANES)
    edge = (PAD, LANES)
    flat = (2 * PAD, LANES)
    piece = (ROWS_EACH, LANES)

    def v(*shape, dtype=F32):
        return pltpu.VMEM(shape, dtype)

    def sems(n):
        return pltpu.SemaphoreType.DMA((n,))

    scratch = [
        v(*levels), v(*levels), v(ROWS, LANES, dtype=jnp.int32), v(ROWS, LANES, dtype=jnp.int32),
        pltpu.SMEM((LEVELS,), F32), v(LEVELS, HIDDEN, dtype=BF16), v(HIDDEN),
        v(LEVELS, HIDDEN, dtype=BF16), pltpu.SMEM((LEVELS,), F32),
        v(*slab), v(*slab), v(*edge), v(*edge), v(*edge), v(*edge),
        v(4, *edge), v(4, *edge), v(4 * ROWS, LANES),
        v(1, LANES), v(PLANE, 1, LANES), v(1, LANES), v(DEPTH, 1, LANES),
        v(LANES, HIDDEN), v(LANES, HIDDEN), v(LANES, HIDDEN, dtype=BF16),
        v(HIDDEN, LANES, dtype=BF16), v(LANES, HIDDEN, dtype=BF16), v(HIDDEN, LANES, dtype=BF16),
        v(LANES, COLS, dtype=BF16), v(HIDDEN, COLS, dtype=BF16), v(HIDDEN, COLS),
        v(HIDDEN, COLS, dtype=BF16), v(LANES, COLS, dtype=BF16), v(*slab),
        v(*levels), v(*levels), v(*levels), v(*levels), v(LEVELS + 1, ROWS, LANES),
        v(*levels), v(*levels), v(*levels), v(LANES, ROWS, LANES),
        v(2, 2, *flat), v(2, *flat), v(2, *flat), v(2, CHIPS, *piece),
        v(2, *piece), v(2, DEPTH, *piece), v(2, *piece), v(2, 2, *flat),
        sems(9), sems(2), sems(2), sems(2), sems(2), sems(2), sems(2),
        sems(2), sems(2), sems(2), sems(2), sems(2), sems(2), sems(8), sems(8),
    ]
    shapes = (
        jax.ShapeDtypeStruct(tracer.shape, F32),
        jax.ShapeDtypeStruct((LEVELS, HIDDEN), F32),
        jax.ShapeDtypeStruct((1, HIDDEN), F32),
        jax.ShapeDtypeStruct((LEVELS, HIDDEN), F32),
        jax.ShapeDtypeStruct((1, LANES), F32),
    )
    operands = (tracer, cotangent, land_mask, bottom, kappa, w_in, b_in, w_out.T, b_out)
    results = pl.pallas_call(
        kernel,
        out_shape=shapes,
        in_specs=[hbm] * 9,
        out_specs=(vmem,) * 5,
        scratch_shapes=scratch,
        compiler_params=pltpu.CompilerParams(
            collective_id=0, has_side_effects=True, vmem_limit_bytes=40 * 1024 * 1024
        ),
        name="step_adjoint",
    )(*(pltpu.with_memory_space_constraint(a, pltpu.HBM) for a in operands))
    out, gw_in, gb_in, gw_out, gb_out = pl.pallas_call(
        store_results,
        out_shape=shapes[:2]
        + (jax.ShapeDtypeStruct((HIDDEN,), F32), shapes[3], jax.ShapeDtypeStruct((LEVELS,), F32)),
        in_specs=[vmem] * 5,
        out_specs=(hbm,) * 5,
        scratch_shapes=[v(HIDDEN), v(LEVELS), sems(5)],
        compiler_params=pltpu.CompilerParams(vmem_limit_bytes=1024 * 1024),
        name="store_results",
    )(*results)
    return out, gw_in, gb_in, gw_out.T, gb_out


def solution(mesh):
    placed = (
        P(None, "lat", "lon"),
        P(None, "lat", "lon"),
        P("lat", "lon"),
        P("lat", "lon"),
        P(),
        P(),
        P(),
        P(),
        P(),
    )
    return jax.shard_map(
        shards,
        mesh=mesh,
        in_specs=placed,
        out_specs=(P(None, "lat", "lon"), P(), P(), P(), P()),
        check_vma=False,
    )
```

```python
import functools
import math

import jax
import jax.numpy as jnp
from jax import lax
from jax.experimental import pallas as pl
from jax.experimental.pallas import tpu as pltpu
from jax.sharding import PartitionSpec as P

MESH = pl.DeviceIdType.MESH
F32 = jnp.float32
BF16 = jnp.bfloat16

spread_coef = 0.15
level_eps = 1e-05

LEVELS = 100
ROWS = 8
LANES = 128
HIDDEN = 512
COLS = ROWS * LANES
PAD = 104
LAT = 8
LON = 32
SIDE = 4
CHIPS = SIDE * SIDE
PLANE = 2 * CHIPS
DEPTH = 8
HALF = HIDDEN // 2
ROWS_EACH = 2 * PAD // CHIPS


def ring(d, n):
    return min(d, n - d)


CHIP_STEPS = sorted(
    ((dx, dy) for dx in range(SIDE) for dy in range(SIDE)),
    key=lambda s: -(ring(s[0], SIDE) + ring(s[1], SIDE)),
)
Z_STEPS = sorted(range(1, DEPTH), key=lambda d: -ring(d, DEPTH))


def kernel(
    tracer_hbm, cot_hbm, land_hbm, bottom_hbm, kappa_hbm, w_in_hbm, b_in_hbm, w_out_hbm, b_out_hbm,
    out_ref, gw_in_ref, gb_in_ref, gw_out_ref, gb_out_ref,
    tr_v, cot_v, land_v, bottom_v, kappa_s, w_in_v, b_in_v, w_out_v, b_out_s,
    slabs, adj_slabs, edge_hi, edge_lo, edge2_hi, edge2_lo, halo, halo2, near_depth,
    small_src, small_r1, small_mid, small_r2,
    wi_f, wo_f, wi_b, w1t, wot, wo_b,
    inp, hid, slope, dpre, dlog, din,
    logit, mixed, val_x, val_y, mul_x, mul_y, gate, adj, dlev,
    grad, from_core, half, from_plane, mid, from_z, chunk, full,
    load_sems, small_send, small_recv, core_send, core_recv, plane_send, plane_recv,
    z_send, z_recv, gather_send, gather_recv, far_recv, fwd_send, fwd_recv, halo_send, halo_recv,
):
    lat = lax.axis_index("lat")
    lon = lax.axis_index("lon")
    y_me = lat % SIDE
    x_me = (lat // SIDE) * 2 + lon // 16
    z_me = (lon // 2) % DEPTH
    core = lon % 2
    p_me = x_me * SIDE + y_me
    q_me = p_me * 2 + core
    mine = pl.ds(p_me * ROWS_EACH, ROWS_EACH)
    lon_z = z_me * 2

    loads = []
    for n, (src, dst) in enumerate(
        (
            (tracer_hbm, tr_v), (land_hbm, land_v), (bottom_hbm, bottom_v), (w_in_hbm, w_in_v),
            (b_in_hbm, b_in_v), (w_out_hbm, w_out_v), (cot_hbm, cot_v), (kappa_hbm, kappa_s),
            (b_out_hbm, b_out_s),
        )
    ):
        loads.append(pltpu.make_async_copy(src, dst, load_sems.at[n]))
    for load in loads[:3]:
        load.start()

    xs = [(x_me + d) % SIDE for d in range(SIDE)]
    ys = [(y_me + d) % SIDE for d in range(SIDE)]

    def chip_peer(dx, dy, dc):
        to_core = core if dc == 0 else 1 - core
        dev = ((xs[dx] // 2) * SIDE + ys[dy], (xs[dx] % 2) * 16 + lon_z + to_core)
        return xs[dx] * SIDE + ys[dy], dev

    def z_peer(d):
        return (lat, (lon // 16) * 16 + ((z_me + d) % DEPTH) * 2 + core)

    everyone = [(dx, dy, dc) for dx, dy in CHIP_STEPS for dc in (0, 1) if dx or dy or dc]
    same_core = [(dx, dy) for dx, dy in CHIP_STEPS if dx or dy]
    far_steps = [s for s in same_core if ring(s[0], SIDE) + ring(s[1], SIDE) > 2]
    near_steps = [s for s in same_core if s not in far_steps]
    partner = (lat, lon + 1 - 2 * core)

    barrier = pltpu.get_barrier_semaphore()

    def greet(dev):
        pl.semaphore_signal(barrier, inc=1, device_id=dev, device_id_type=MESH)

    greet(z_peer(Z_STEPS[0]))
    for step in everyone:
        greet(chip_peer(*step)[1])
    for d in Z_STEPS[1:]:
        greet(z_peer(d))
    greet((lat, (lon + 2 * core - 1 + LON) % LON))
    for load in loads[3:]:
        load.start()

    row_id = lax.broadcasted_iota(jnp.int32, (PAD, LANES), 0)
    lane_id = lax.broadcasted_iota(jnp.int32, (PAD, LANES), 1)
    row_f = row_id.astype(F32)
    diag = row_id == lane_id

    def as_row(column):
        return jnp.sum(jnp.where(diag, column, 0.0), axis=0, keepdims=True)

    def as_column(row):
        return jnp.sum(jnp.where(diag, row, 0.0), axis=1, keepdims=True)

    for n in range(3):
        loads[n].wait()
    depth_all = (land_v[...] * bottom_v[...]).astype(F32)
    energy = jnp.zeros((PAD, LANES), F32)
    for i in range(ROWS):
        slabs[i, 0:LEVELS, :] = tr_v[:, i, :]
        slabs[i, LEVELS:PAD, :] = jnp.broadcast_to(depth_all[i : i + 1, :], (PAD - LEVELS, LANES))
        wet_x = jnp.where(row_f < depth_all[i : i + 1, :], slabs[i], 0.0)
        energy = energy + wet_x * wet_x
    small_src[...] = as_row(jnp.sum(energy, axis=1, keepdims=True))
    small_r1[q_me] = small_src[...]

    pl.semaphore_wait(barrier, PLANE - 1 + DEPTH - 1 + 1)

    def post(src, dst, dev, send, recv):
        pltpu.make_async_remote_copy(
            src, dst, send, recv, device_id=dev, device_id_type=MESH
        ).start()

    def send_z(src, dst, send, recv):
        for d in Z_STEPS:
            post(src, dst.at[z_me], z_peer(d), send, recv)

    def drain(ref, sem):
        pltpu.make_async_copy(ref, ref, sem).wait()

    def send_halo(k, pieces, dst):
        up = (lat + 1) % LAT
        down = (lat + LAT - 1) % LAT
        right = (lon + 1) % LON
        left = (lon + LON - 1) % LON
        targets = ((up, lon), (down, lon), (lat, right), (lat, left))
        copies = []
        for n, (src, dev) in enumerate(zip(pieces, targets)):
            copy = pltpu.make_async_remote_copy(
                src, dst.at[n], halo_send.at[4 * k + n], halo_recv.at[4 * k + n],
                device_id=dev, device_id_type=MESH,
            )
            copy.start()
            copies.append(copy)
        return copies

    for step in everyone:
        post(small_src, small_r1.at[q_me], chip_peer(*step)[1], small_send.at[0], small_recv.at[0])
    hi = jnp.zeros((PAD, LANES), F32)
    lo = jnp.zeros((PAD, LANES), F32)
    for i in range(ROWS):
        x = slabs[i]
        hi = jnp.where(lane_id == i, pltpu.roll(x, i + 1, 1), hi)
        lo = jnp.where(lane_id == i, pltpu.roll(x, i, 1) if i else x, lo)
    edge_hi[...] = hi
    edge_lo[...] = lo
    halo_copies = send_halo(0, (slabs.at[ROWS - 1], slabs.at[0], edge_hi, edge_lo), halo)

    for n in range(3, 6):
        loads[n].wait()
    bias = b_in_v[...].reshape(1, HIDDEN)
    bias_hi = bias.astype(BF16).astype(F32)
    bias_mid = (bias - bias_hi).astype(BF16).astype(F32)
    bias_lo = bias - bias_hi - bias_mid
    wi_f[LEVELS:LANES, :] = jnp.zeros((LANES - LEVELS, HIDDEN), F32)
    wi_f[0:LEVELS, :] = w_in_v[...].astype(F32)
    wi_f[LEVELS : LEVELS + 1, :] = bias_hi
    wi_f[LEVELS + 1 : LEVELS + 2, :] = bias_mid
    wi_f[LEVELS + 2 : LEVELS + 3, :] = bias_lo
    wi_b[...] = wi_f[...].astype(BF16)
    w1t[...] = wi_f[...].T.astype(BF16)
    wo_f[LEVELS:LANES, :] = jnp.zeros((LANES - LEVELS, HIDDEN), F32)
    wo_f[0:LEVELS, :] = w_out_v[...].astype(F32)
    wot[...] = wo_f[...].astype(BF16)
    wo_b[...] = wo_f[...].T.astype(BF16)
    dlev[LEVELS:LANES] = jnp.zeros((LANES - LEVELS, ROWS, LANES), F32)
    for i in range(ROWS):
        adj_slabs[i, LEVELS:PAD, :] = jnp.zeros((PAD - LEVELS, LANES), F32)
    edge2_hi[LEVELS:PAD, :] = jnp.zeros((PAD - LEVELS, LANES), F32)
    edge2_lo[LEVELS:PAD, :] = jnp.zeros((PAD - LEVELS, LANES), F32)
    inp[PAD - 8 : LANES, :] = jnp.zeros((LANES - PAD + 8, COLS), BF16)
    for n in range(6, 9):
        loads[n].wait()

    drain(small_r1.at[pl.ds(0, PLANE - 1)], small_recv.at[0])
    small_mid[...] = jnp.sum(small_r1[...], axis=0)
    small_r2[z_me] = small_mid[...]
    send_z(small_mid, small_r2, small_send.at[1], small_recv.at[1])

    for copy in halo_copies:
        copy.wait_recv()

    def neighbours(field, edges, i):
        centre = field[i]
        below = field[i + 1] if i + 1 < ROWS else edges[1]
        above = field[i - 1] if i else edges[0]
        from_left = pltpu.roll(edges[2], LANES - i, 1) if i else edges[2]
        left = jnp.where(lane_id == 0, from_left, pltpu.roll(centre, 1, 1))
        right = jnp.where(
            lane_id == LANES - 1, pltpu.roll(edges[3], LANES - 1 - i, 1), pltpu.roll(centre, LANES - 1, 1)
        )
        return centre, (below, above, left, right)

    def flux(centre, near, i):
        total = jnp.zeros((PAD, LANES), F32)
        for n in range(4):
            total = total + jnp.where(
                row_f < near_depth[n * ROWS + i : n * ROWS + i + 1, :], near[n] - centre, 0.0
            )
        return centre + spread_coef * total

    has_above = jnp.where(lat > 0, 1.0, 0.0)
    has_below = jnp.where(lat < LAT - 1, 1.0, 0.0)
    for i in range(ROWS):
        centre, near = neighbours(slabs, halo, i)
        own = centre[LEVELS : LEVELS + 1, :]
        for n in range(4):
            other = near[n][LEVELS : LEVELS + 1, :]
            if n == 0 and i == ROWS - 1:
                other = other * has_below
            if n == 1 and i == 0:
                other = other * has_above
            near_depth[n * ROWS + i : n * ROWS + i + 1, :] = jnp.minimum(own, other)
        mixed[:, i, :] = flux(centre, near, i)[0:LEVELS]

    drain(small_r2.at[pl.ds(0, DEPTH - 1)], small_recv.at[1])
    energy_all = as_column(jnp.sum(small_r2[...], axis=0))
    count = float(LAT * LON * COLS)
    radius = jnp.sqrt(energy_all / count + level_eps)
    inv_radius = 1.0 / radius

    def wet_slab(i):
        x = slabs[i]
        return jnp.where(row_f < x[LEVELS : LEVELS + 1, :], x, 0.0)

    one_rows = jnp.where(row_id < LEVELS + 3, 1.0, 0.0)
    for i in range(ROWS):
        scaled = jnp.where(row_id < LEVELS, wet_slab(i) * inv_radius, one_rows)
        scaled = jnp.concatenate([scaled, jnp.zeros((LANES - PAD, LANES), F32)], axis=0)
        inp[:, i * LANES : (i + 1) * LANES] = scaled.astype(BF16)

    width = 256
    for j in range(COLS // width):
        cols = slice(j * width, (j + 1) * width)
        pre = jnp.dot(w1t[...], inp[:, cols], preferred_element_type=F32)
        sig = 1.0 / (1.0 + jnp.exp(-pre))
        act = pre * sig
        hid[:, cols] = act.astype(BF16)
        slope[:, cols] = sig * (1.0 + pre * (1.0 - sig))
        out = jnp.dot(wot[...], hid[:, cols], preferred_element_type=F32)
        for s in range(width // LANES):
            logit[:, j * (width // LANES) + s, :] = out[0:LEVELS, s * LANES : (s + 1) * LANES]

    depth = depth_all
    middle = LEVELS // 2

    def level_terms(k):
        x = logit[k] + b_out_s[k]
        ex = jnp.exp(-jnp.abs(x))
        soft = jnp.maximum(x, 0.0) + jnp.log1p(ex)
        sig = jnp.where(x >= 0.0, 1.0, ex) / (1.0 + ex)
        kf = (k + 1).astype(F32)
        open_face = kf < depth
        kap = kappa_s[k]
        down = jnp.where(open_face, kap + soft, 0.0)
        up = jnp.where(open_face, kap, 0.0)
        gate[k] = jnp.where(open_face, sig, 0.0)
        return down, up

    def eliminate(s, carry):
        down_p, up_p, r_p, v_p, w_p, sb_n, u_n, z_n = carry
        k = s
        down, up = level_terms(k)
        pivot = 1.0 + down + up_p - down_p * up_p * r_p
        r = 1.0 / pivot
        v = (mixed[k] + down_p * v_p) * r
        w = (cot_v[k] + up_p * w_p) * r
        val_x[k] = v
        val_y[k] = w
        mul_x[k] = up * r
        mul_y[k] = down * r
        b = LEVELS - 1 - s
        down_b, up_b = level_terms(b)
        up_above = jnp.where(b.astype(F32) < depth, kappa_s[b - 1], 0.0)
        pivot_b = 1.0 + down_b + up_above - down_b * up_b * sb_n
        sb = 1.0 / pivot_b
        u = (mixed[b] + up_b * u_n) * sb
        zz = (cot_v[b] + down_b * z_n) * sb
        val_x[b] = u
        val_y[b] = zz
        mul_y[b] = up_above * sb
        mul_x[b + 1] = down_b * sb_n
        return down, up, r, v, w, sb, u, zz

    zero = jnp.zeros((ROWS, LANES), F32)
    down_m, up_m, r_m, v_m, w_m, sb_m, u_m, z_m = lax.fori_loop(
        0, middle, eliminate, (zero,) * 8, unroll=5
    )
    ratio_x = up_m * r_m
    ratio_y = down_m * r_m
    back_x = down_m * sb_m
    back_y = up_m * sb_m
    inv_det = 1.0 / (1.0 - ratio_x * back_x)
    x_top = (v_m + ratio_x * u_m) * inv_det
    x_bot = u_m + back_x * x_top
    y_top = (w_m + ratio_y * z_m) * inv_det
    y_bot = z_m + back_y * y_top
    adj[middle - 1] = y_top
    adj[middle] = y_bot
    dlev[middle - 1] = gate[middle - 1] * x_top * (y_bot - y_top)

    def substitute(s, carry):
        x_t, y_t, x_b, y_b = carry
        k = middle - 1 - s
        x_n = val_x[k] + mul_x[k] * x_t
        y_n = val_y[k] + mul_y[k] * y_t
        adj[k] = y_n
        dlev[k] = gate[k] * x_n * (y_t - y_n)
        b = middle + s
        x_c = val_x[b] + mul_x[b] * x_b
        y_c = val_y[b] + mul_y[b] * y_b
        adj[b] = y_c
        dlev[b - 1] = gate[b - 1] * x_b * (y_c - y_b)
        return x_n, y_n, x_c, y_c

    lax.fori_loop(1, middle, substitute, (x_top, y_top, x_bot, y_bot), unroll=7)
    dlev[LEVELS - 1] = zero

    for i in range(ROWS):
        dlog[:, i * LANES : (i + 1) * LANES] = dlev[:, i, :].astype(BF16)
    for j in range(COLS // width):
        cols = slice(j * width, (j + 1) * width)
        back = jnp.dot(wo_b[...], dlog[:, cols], preferred_element_type=F32)
        dpre[:, cols] = (back * slope[:, cols]).astype(BF16)
    contract_last = (((1,), (1,)), ((), ()))
    sources = ((inp, dpre), (dlog, hid))

    for m, (small, big) in enumerate(sources):
        value = lax.dot_general(small[...], big[...], contract_last, preferred_element_type=F32)
        for n in range(4):
            grad[m, n // 2, (n % 2) * PAD : (n % 2 + 1) * PAD, :] = value[
                0:PAD, n * LANES : (n + 1) * LANES
            ]
        post(grad.at[m, 1 - core], from_core.at[m], partner, core_send.at[m], core_recv.at[m])

    for m in range(2):
        drain(from_core.at[m], core_recv.at[m])
        half[m] = grad[m, core] + from_core[m]
        if m:
            half[1, LEVELS : LEVELS + 1, :] = lax.dot_general(
                jnp.ones((16, COLS), BF16), dlog[...], contract_last, preferred_element_type=F32
            )[0:1]
        for dx, dy in same_core:
            p, dev = chip_peer(dx, dy, 0)
            post(
                half.at[m, pl.ds(p * ROWS_EACH, ROWS_EACH)], from_plane.at[m, p_me], dev,
                plane_send.at[m], plane_recv.at[m],
            )
        from_plane[m, p_me] = half[m, mine, :]

    hi = jnp.zeros((LEVELS, LANES), F32)
    lo = jnp.zeros((LEVELS, LANES), F32)
    lane_l = lane_id[0:LEVELS]
    for i in range(ROWS):
        x = adj[:, i, :]
        adj_slabs[i, 0:LEVELS, :] = x
        hi = jnp.where(lane_l == i, pltpu.roll(x, i + 1, 1), hi)
        lo = jnp.where(lane_l == i, pltpu.roll(x, i, 1) if i else x, lo)
    edge2_hi[0:LEVELS, :] = hi
    edge2_lo[0:LEVELS, :] = lo
    for j in range(COLS // width):
        cols = slice(j * width, (j + 1) * width)
        out = jnp.dot(wi_b[...], dpre[:, cols], preferred_element_type=F32)
        for s in range(width // LANES):
            i = j * (width // LANES) + s
            din[i] = out[0:PAD, s * LANES : (s + 1) * LANES] * inv_radius

    scale = 1.0 / math.sqrt(count)
    for m in range(2):
        drain(from_plane.at[m, pl.ds(0, CHIPS - 1)], plane_recv.at[m])
        mid[m] = jnp.sum(from_plane[m], axis=0)
        from_z[m, z_me] = mid[m]
        send_z(mid.at[m], from_z.at[m], z_send.at[m], z_recv.at[m])

    halo2_copies = send_halo(
        1, (adj_slabs.at[ROWS - 1], adj_slabs.at[0], edge2_hi, edge2_lo), halo2
    )
    for m in range(2):
        drain(from_z.at[m, pl.ds(0, DEPTH - 1)], z_recv.at[m])
        chunk[m] = jnp.sum(from_z[m], axis=0) * scale
        place = full.at[m, core, mine]
        for dx, dy in far_steps:
            post(chunk.at[m], place, chip_peer(dx, dy, 0)[1], gather_send.at[m], far_recv.at[m])
            post(chunk.at[m], place, chip_peer(dx, dy, 1)[1], fwd_send.at[m], fwd_recv.at[m])
        for dx, dy in near_steps:
            post(chunk.at[m], place, chip_peer(dx, dy, 0)[1], gather_send.at[m], gather_recv.at[m])
        post(chunk.at[m], place, partner, fwd_send.at[m], fwd_recv.at[m])
        full[m, core, mine, :] = chunk[m]

    for copy in halo2_copies:
        copy.wait_recv()
    for i in range(ROWS):
        centre, near = neighbours(adj_slabs, halo2, i)
        wet = row_f < slabs[i, LEVELS : LEVELS + 1, :]
        din[i] = flux(centre, near, i) + jnp.where(wet, din[i], 0.0)

    peers_rows = pl.ds(0, (CHIPS - 1) * ROWS_EACH)
    for m in range(2):
        drain(full.at[m, core, pl.ds(0, len(near_steps) * ROWS_EACH)], gather_recv.at[m])
        for dx, dy in near_steps:
            place = full.at[m, core, pl.ds(chip_peer(dx, dy, 0)[0] * ROWS_EACH, ROWS_EACH)]
            post(place, place, partner, fwd_send.at[m], fwd_recv.at[m])

    def await_all(m):
        drain(full.at[m, core, pl.ds(0, len(far_steps) * ROWS_EACH)], far_recv.at[m])
        drain(full.at[m, 1 - core], fwd_recv.at[m])

    def deliver(m, ref):
        for c in range(2):
            for h in range(2):
                n = 2 * c + h
                ref[:, n * LANES : (n + 1) * LANES] = full[m, c, h * PAD : h * PAD + LEVELS, :]

    await_all(0)
    weighted = jnp.zeros((PAD, LANES), F32)
    for c in range(2):
        for h in range(2):
            n = 2 * c + h
            part = full[0, c, h * PAD : (h + 1) * PAD, :]
            weighted = weighted + wi_f[0:PAD, n * LANES : (n + 1) * LANES] * part
            gb_in_ref[:, n * LANES : (n + 1) * LANES] = part[LEVELS : LEVELS + 1, :]
    level_sum = radius * jnp.sum(weighted, axis=1, keepdims=True) * math.sqrt(count)
    level_scale = level_sum / (count * radius * radius * radius)
    for i in range(ROWS):
        out_ref[:, i, :] = (din[i] - wet_slab(i) * level_scale)[0:LEVELS]
    deliver(0, gw_in_ref)
    await_all(1)
    deliver(1, gw_out_ref)
    gb_out_ref[...] = full[1, 0, LEVELS : LEVELS + 1, :] + full[1, 1, LEVELS : LEVELS + 1, :]

    for copy in halo_copies + halo2_copies:
        copy.wait_send()
    drain(small_r1.at[pl.ds(0, PLANE - 1)], small_send.at[0])
    drain(small_r2.at[pl.ds(0, DEPTH - 1)], small_send.at[1])
    for m in range(2):
        drain(from_core.at[m], core_send.at[m])
        drain(from_plane.at[m, pl.ds(0, CHIPS - 1)], plane_send.at[m])
        drain(from_z.at[m, pl.ds(0, DEPTH - 1)], z_send.at[m])
        drain(full.at[m, core, peers_rows], gather_send.at[m])
        drain(full.at[m, core], fwd_send.at[m])


def store_results(
    out_v, gw_in_v, gb_in_v, gw_out_v, gb_out_v, out_h, gw_in_h, gb_in_h, gw_out_h, gb_out_h,
    gb_in_flat, gb_out_flat, sems,
):
    pairs = (
        (out_v, out_h), (gw_in_v, gw_in_h), (gw_out_v, gw_out_h),
        (gb_in_flat, gb_in_h), (gb_out_flat, gb_out_h),
    )
    copies = [pltpu.make_async_copy(src, dst, sems.at[n]) for n, (src, dst) in enumerate(pairs)]
    for copy in copies[:3]:
        copy.start()
    gb_in_flat[...] = gb_in_v[...].reshape(HIDDEN)
    gb_out_flat[...] = gb_out_v[...].reshape(LANES)[0:LEVELS]
    for copy in copies[3:]:
        copy.start()
    for copy in copies:
        copy.wait()


def shards(tracer, cotangent, land_mask, bottom, kappa, w_in, b_in, w_out, b_out):
    vmem = pl.BlockSpec(memory_space=pltpu.VMEM)
    hbm = pl.BlockSpec(memory_space=pltpu.HBM)
    slab = (ROWS, PAD, LANES)
    levels = (LEVELS, ROWS, LANES)
    edge = (PAD, LANES)
    flat = (2 * PAD, LANES)
    piece = (ROWS_EACH, LANES)

    def v(*shape, dtype=F32):
        return pltpu.VMEM(shape, dtype)

    def sems(n):
        return pltpu.SemaphoreType.DMA((n,))

    scratch = [
        v(*levels), v(*levels), v(ROWS, LANES, dtype=jnp.int32), v(ROWS, LANES, dtype=jnp.int32),
        pltpu.SMEM((LEVELS,), F32), v(LEVELS, HIDDEN, dtype=BF16), v(HIDDEN),
        v(LEVELS, HIDDEN, dtype=BF16), pltpu.SMEM((LEVELS,), F32),
        v(*slab), v(*slab), v(*edge), v(*edge), v(*edge), v(*edge),
        v(4, *edge), v(4, *edge), v(4 * ROWS, LANES),
        v(1, LANES), v(PLANE, 1, LANES), v(1, LANES), v(DEPTH, 1, LANES),
        v(LANES, HIDDEN), v(LANES, HIDDEN), v(LANES, HIDDEN, dtype=BF16),
        v(HIDDEN, LANES, dtype=BF16), v(LANES, HIDDEN, dtype=BF16), v(HIDDEN, LANES, dtype=BF16),
        v(LANES, COLS, dtype=BF16), v(HIDDEN, COLS, dtype=BF16), v(HIDDEN, COLS),
        v(HIDDEN, COLS, dtype=BF16), v(LANES, COLS, dtype=BF16), v(*slab),
        v(*levels), v(*levels), v(*levels), v(*levels), v(LEVELS + 1, ROWS, LANES),
        v(*levels), v(*levels), v(*levels), v(LANES, ROWS, LANES),
        v(2, 2, *flat), v(2, *flat), v(2, *flat), v(2, CHIPS, *piece),
        v(2, *piece), v(2, DEPTH, *piece), v(2, *piece), v(2, 2, *flat),
        sems(9), sems(2), sems(2), sems(2), sems(2), sems(2), sems(2),
        sems(2), sems(2), sems(2), sems(2), sems(2), sems(2), sems(2), sems(8), sems(8),
    ]
    shapes = (
        jax.ShapeDtypeStruct(tracer.shape, F32),
        jax.ShapeDtypeStruct((LEVELS, HIDDEN), F32),
        jax.ShapeDtypeStruct((1, HIDDEN), F32),
        jax.ShapeDtypeStruct((LEVELS, HIDDEN), F32),
        jax.ShapeDtypeStruct((1, LANES), F32),
    )
    operands = (tracer, cotangent, land_mask, bottom, kappa, w_in, b_in, w_out.T, b_out)
    results = pl.pallas_call(
        kernel,
        out_shape=shapes,
        in_specs=[hbm] * 9,
        out_specs=(vmem,) * 5,
        scratch_shapes=scratch,
        compiler_params=pltpu.CompilerParams(
            collective_id=0, has_side_effects=True, vmem_limit_bytes=40 * 1024 * 1024
        ),
        name="step_adjoint",
    )(*(pltpu.with_memory_space_constraint(a, pltpu.HBM) for a in operands))
    out, gw_in, gb_in, gw_out, gb_out = pl.pallas_call(
        store_results,
        out_shape=shapes[:2]
        + (jax.ShapeDtypeStruct((HIDDEN,), F32), shapes[3], jax.ShapeDtypeStruct((LEVELS,), F32)),
        in_specs=[vmem] * 5,
        out_specs=(hbm,) * 5,
        scratch_shapes=[v(HIDDEN), v(LEVELS), sems(5)],
        compiler_params=pltpu.CompilerParams(vmem_limit_bytes=1024 * 1024),
        name="store_results",
    )(*results)
    return out, gw_in, gb_in, gw_out.T, gb_out


def solution(mesh):
    placed = (
        P(None, "lat", "lon"),
        P(None, "lat", "lon"),
        P("lat", "lon"),
        P("lat", "lon"),
        P(),
        P(),
        P(),
        P(),
        P(),
    )
    return jax.shard_map(
        shards,
        mesh=mesh,
        in_specs=placed,
        out_specs=(P(None, "lat", "lon"), P(), P(), P(), P()),
        check_vma=False,
    )
```

```python
import functools
import math

import jax
import jax.numpy as jnp
from jax import lax
from jax.experimental import pallas as pl
from jax.experimental.pallas import tpu as pltpu
from jax.sharding import PartitionSpec as P

MESH = pl.DeviceIdType.MESH
F32 = jnp.float32
BF16 = jnp.bfloat16

spread_coef = 0.15
level_eps = 1e-05

LEVELS = 100
ROWS = 8
LANES = 128
HIDDEN = 512
COLS = ROWS * LANES
PAD = 104
LAT = 8
LON = 32
SIDE = 4
CHIPS = SIDE * SIDE
PLANE = 2 * CHIPS
DEPTH = 8
HALF = HIDDEN // 2
ROWS_EACH = 2 * PAD // CHIPS


def ring(d, n):
    return min(d, n - d)


CHIP_STEPS = sorted(
    ((dx, dy) for dx in range(SIDE) for dy in range(SIDE)),
    key=lambda s: -(ring(s[0], SIDE) + ring(s[1], SIDE)),
)
Z_STEPS = sorted(range(1, DEPTH), key=lambda d: -ring(d, DEPTH))


def kernel(
    tracer_hbm, cot_hbm, land_hbm, bottom_hbm, kappa_hbm, w_in_hbm, b_in_hbm, w_out_hbm, b_out_hbm,
    out_ref, gw_in_ref, gb_in_ref, gw_out_ref, gb_out_ref,
    tr_v, cot_v, land_v, bottom_v, kappa_s, w_in_v, b_in_v, w_out_v, b_out_s,
    slabs, adj_slabs, edge_hi, edge_lo, edge2_hi, edge2_lo, halo, halo2, near_depth,
    small_src, small_r1, small_mid, small_r2,
    wi_f, wo_f, wi_b, w1t, wot, wo_b,
    inp, hid, slope, dpre, dlog, din,
    logit, mixed, val_x, val_y, mul_x, mul_y, gate, adj, dlev,
    grad, from_core, half, from_plane, mid, from_z, chunk, full,
    load_sems, small_send, small_recv, core_send, core_recv, plane_send, plane_recv,
    z_send, z_recv, gather_send, gather_recv, fwd_send, fwd_recv, halo_send, halo_recv,
):
    lat = lax.axis_index("lat")
    lon = lax.axis_index("lon")
    y_me = lat % SIDE
    x_me = (lat // SIDE) * 2 + lon // 16
    z_me = (lon // 2) % DEPTH
    core = lon % 2
    p_me = x_me * SIDE + y_me
    q_me = p_me * 2 + core
    mine = pl.ds(p_me * ROWS_EACH, ROWS_EACH)
    lon_z = z_me * 2

    loads = []
    for n, (src, dst) in enumerate(
        (
            (tracer_hbm, tr_v), (land_hbm, land_v), (bottom_hbm, bottom_v), (w_in_hbm, w_in_v),
            (b_in_hbm, b_in_v), (w_out_hbm, w_out_v), (cot_hbm, cot_v), (kappa_hbm, kappa_s),
            (b_out_hbm, b_out_s),
        )
    ):
        loads.append(pltpu.make_async_copy(src, dst, load_sems.at[n]))
    for load in loads[:3]:
        load.start()

    xs = [(x_me + d) % SIDE for d in range(SIDE)]
    ys = [(y_me + d) % SIDE for d in range(SIDE)]

    def chip_peer(dx, dy, dc):
        to_core = core if dc == 0 else 1 - core
        dev = ((xs[dx] // 2) * SIDE + ys[dy], (xs[dx] % 2) * 16 + lon_z + to_core)
        return xs[dx] * SIDE + ys[dy], dev

    def z_peer(d):
        return (lat, (lon // 16) * 16 + ((z_me + d) % DEPTH) * 2 + core)

    everyone = [(dx, dy, dc) for dx, dy in CHIP_STEPS for dc in (0, 1) if dx or dy or dc]
    same_core = [(dx, dy) for dx, dy in CHIP_STEPS if dx or dy]
    partner = (lat, lon + 1 - 2 * core)

    barrier = pltpu.get_barrier_semaphore()

    def greet(dev):
        pl.semaphore_signal(barrier, inc=1, device_id=dev, device_id_type=MESH)

    greet(z_peer(Z_STEPS[0]))
    for step in everyone:
        greet(chip_peer(*step)[1])
    for d in Z_STEPS[1:]:
        greet(z_peer(d))
    greet((lat, (lon + 2 * core - 1 + LON) % LON))
    for load in loads[3:]:
        load.start()

    row_id = lax.broadcasted_iota(jnp.int32, (PAD, LANES), 0)
    lane_id = lax.broadcasted_iota(jnp.int32, (PAD, LANES), 1)
    row_f = row_id.astype(F32)
    diag = row_id == lane_id

    def as_row(column):
        return jnp.sum(jnp.where(diag, column, 0.0), axis=0, keepdims=True)

    def as_column(row):
        return jnp.sum(jnp.where(diag, row, 0.0), axis=1, keepdims=True)

    for n in range(3):
        loads[n].wait()
    depth_all = (land_v[...] * bottom_v[...]).astype(F32)
    energy = jnp.zeros((PAD, LANES), F32)
    for i in range(ROWS):
        slabs[i, 0:LEVELS, :] = tr_v[:, i, :]
        slabs[i, LEVELS:PAD, :] = jnp.broadcast_to(depth_all[i : i + 1, :], (PAD - LEVELS, LANES))
        wet_x = jnp.where(row_f < depth_all[i : i + 1, :], slabs[i], 0.0)
        energy = energy + wet_x * wet_x
    small_src[...] = as_row(jnp.sum(energy, axis=1, keepdims=True))
    small_r1[q_me] = small_src[...]

    pl.semaphore_wait(barrier, PLANE - 1 + DEPTH - 1 + 1)

    def post(src, dst, dev, send, recv):
        pltpu.make_async_remote_copy(
            src, dst, send, recv, device_id=dev, device_id_type=MESH
        ).start()

    def send_z(src, dst, send, recv):
        for d in Z_STEPS:
            post(src, dst.at[z_me], z_peer(d), send, recv)

    def drain(ref, sem):
        pltpu.make_async_copy(ref, ref, sem).wait()

    def send_halo(k, pieces, dst):
        up = (lat + 1) % LAT
        down = (lat + LAT - 1) % LAT
        right = (lon + 1) % LON
        left = (lon + LON - 1) % LON
        targets = ((up, lon), (down, lon), (lat, right), (lat, left))
        copies = []
        for n, (src, dev) in enumerate(zip(pieces, targets)):
            copy = pltpu.make_async_remote_copy(
                src, dst.at[n], halo_send.at[4 * k + n], halo_recv.at[4 * k + n],
                device_id=dev, device_id_type=MESH,
            )
            copy.start()
            copies.append(copy)
        return copies

    for step in everyone:
        post(small_src, small_r1.at[q_me], chip_peer(*step)[1], small_send.at[0], small_recv.at[0])
    hi = jnp.zeros((PAD, LANES), F32)
    lo = jnp.zeros((PAD, LANES), F32)
    for i in range(ROWS):
        x = slabs[i]
        hi = jnp.where(lane_id == i, pltpu.roll(x, i + 1, 1), hi)
        lo = jnp.where(lane_id == i, pltpu.roll(x, i, 1) if i else x, lo)
    edge_hi[...] = hi
    edge_lo[...] = lo
    halo_copies = send_halo(0, (slabs.at[ROWS - 1], slabs.at[0], edge_hi, edge_lo), halo)

    for n in range(3, 6):
        loads[n].wait()
    bias = b_in_v[...].reshape(1, HIDDEN)
    bias_hi = bias.astype(BF16).astype(F32)
    bias_mid = (bias - bias_hi).astype(BF16).astype(F32)
    bias_lo = bias - bias_hi - bias_mid
    wi_f[LEVELS:LANES, :] = jnp.zeros((LANES - LEVELS, HIDDEN), F32)
    wi_f[0:LEVELS, :] = w_in_v[...].astype(F32)
    wi_f[LEVELS : LEVELS + 1, :] = bias_hi
    wi_f[LEVELS + 1 : LEVELS + 2, :] = bias_mid
    wi_f[LEVELS + 2 : LEVELS + 3, :] = bias_lo
    wi_b[...] = wi_f[...].astype(BF16)
    w1t[...] = wi_f[...].T.astype(BF16)
    wo_f[LEVELS:LANES, :] = jnp.zeros((LANES - LEVELS, HIDDEN), F32)
    wo_f[0:LEVELS, :] = w_out_v[...].astype(F32)
    wot[...] = wo_f[...].astype(BF16)
    wo_b[...] = wo_f[...].T.astype(BF16)
    dlev[LEVELS:LANES] = jnp.zeros((LANES - LEVELS, ROWS, LANES), F32)
    for i in range(ROWS):
        adj_slabs[i, LEVELS:PAD, :] = jnp.zeros((PAD - LEVELS, LANES), F32)
    edge2_hi[LEVELS:PAD, :] = jnp.zeros((PAD - LEVELS, LANES), F32)
    edge2_lo[LEVELS:PAD, :] = jnp.zeros((PAD - LEVELS, LANES), F32)
    inp[PAD - 8 : LANES, :] = jnp.zeros((LANES - PAD + 8, COLS), BF16)
    for n in range(6, 9):
        loads[n].wait()

    drain(small_r1.at[pl.ds(0, PLANE - 1)], small_recv.at[0])
    small_mid[...] = jnp.sum(small_r1[...], axis=0)
    small_r2[z_me] = small_mid[...]
    send_z(small_mid, small_r2, small_send.at[1], small_recv.at[1])

    for copy in halo_copies:
        copy.wait_recv()

    def neighbours(field, edges, i):
        centre = field[i]
        below = field[i + 1] if i + 1 < ROWS else edges[1]
        above = field[i - 1] if i else edges[0]
        from_left = pltpu.roll(edges[2], LANES - i, 1) if i else edges[2]
        left = jnp.where(lane_id == 0, from_left, pltpu.roll(centre, 1, 1))
        right = jnp.where(
            lane_id == LANES - 1, pltpu.roll(edges[3], LANES - 1 - i, 1), pltpu.roll(centre, LANES - 1, 1)
        )
        return centre, (below, above, left, right)

    def flux(centre, near, i):
        total = jnp.zeros((PAD, LANES), F32)
        for n in range(4):
            total = total + jnp.where(
                row_f < near_depth[n * ROWS + i : n * ROWS + i + 1, :], near[n] - centre, 0.0
            )
        return centre + spread_coef * total

    has_above = jnp.where(lat > 0, 1.0, 0.0)
    has_below = jnp.where(lat < LAT - 1, 1.0, 0.0)
    for i in range(ROWS):
        centre, near = neighbours(slabs, halo, i)
        own = centre[LEVELS : LEVELS + 1, :]
        for n in range(4):
            other = near[n][LEVELS : LEVELS + 1, :]
            if n == 0 and i == ROWS - 1:
                other = other * has_below
            if n == 1 and i == 0:
                other = other * has_above
            near_depth[n * ROWS + i : n * ROWS + i + 1, :] = jnp.minimum(own, other)
        mixed[:, i, :] = flux(centre, near, i)[0:LEVELS]

    drain(small_r2.at[pl.ds(0, DEPTH - 1)], small_recv.at[1])
    energy_all = as_column(jnp.sum(small_r2[...], axis=0))
    count = float(LAT * LON * COLS)
    radius = jnp.sqrt(energy_all / count + level_eps)
    inv_radius = 1.0 / radius

    def wet_slab(i):
        x = slabs[i]
        return jnp.where(row_f < x[LEVELS : LEVELS + 1, :], x, 0.0)

    one_rows = jnp.where(row_id < LEVELS + 3, 1.0, 0.0)
    for i in range(ROWS):
        scaled = jnp.where(row_id < LEVELS, wet_slab(i) * inv_radius, one_rows)
        scaled = jnp.concatenate([scaled, jnp.zeros((LANES - PAD, LANES), F32)], axis=0)
        inp[:, i * LANES : (i + 1) * LANES] = scaled.astype(BF16)

    width = 256
    for j in range(COLS // width):
        cols = slice(j * width, (j + 1) * width)
        pre = jnp.dot(w1t[...], inp[:, cols], preferred_element_type=F32)
        sig = 1.0 / (1.0 + jnp.exp(-pre))
        act = pre * sig
        hid[:, cols] = act.astype(BF16)
        slope[:, cols] = sig * (1.0 + pre * (1.0 - sig))
        out = jnp.dot(wot[...], hid[:, cols], preferred_element_type=F32)
        for s in range(width // LANES):
            logit[:, j * (width // LANES) + s, :] = out[0:LEVELS, s * LANES : (s + 1) * LANES]

    depth = depth_all
    middle = LEVELS // 2

    def level_terms(k):
        x = logit[k] + b_out_s[k]
        ex = jnp.exp(-jnp.abs(x))
        soft = jnp.maximum(x, 0.0) + jnp.log1p(ex)
        sig = jnp.where(x >= 0.0, 1.0, ex) / (1.0 + ex)
        kf = (k + 1).astype(F32)
        open_face = kf < depth
        kap = kappa_s[k]
        down = jnp.where(open_face, kap + soft, 0.0)
        up = jnp.where(open_face, kap, 0.0)
        gate[k] = jnp.where(open_face, sig, 0.0)
        return down, up

    def eliminate(s, carry):
        down_p, up_p, r_p, v_p, w_p, sb_n, u_n, z_n = carry
        k = s
        down, up = level_terms(k)
        pivot = 1.0 + down + up_p - down_p * up_p * r_p
        r = 1.0 / pivot
        v = (mixed[k] + down_p * v_p) * r
        w = (cot_v[k] + up_p * w_p) * r
        val_x[k] = v
        val_y[k] = w
        mul_x[k] = up * r
        mul_y[k] = down * r
        b = LEVELS - 1 - s
        down_b, up_b = level_terms(b)
        up_above = jnp.where(b.astype(F32) < depth, kappa_s[b - 1], 0.0)
        pivot_b = 1.0 + down_b + up_above - down_b * up_b * sb_n
        sb = 1.0 / pivot_b
        u = (mixed[b] + up_b * u_n) * sb
        zz = (cot_v[b] + down_b * z_n) * sb
        val_x[b] = u
        val_y[b] = zz
        mul_y[b] = up_above * sb
        mul_x[b + 1] = down_b * sb_n
        return down, up, r, v, w, sb, u, zz

    zero = jnp.zeros((ROWS, LANES), F32)
    down_m, up_m, r_m, v_m, w_m, sb_m, u_m, z_m = lax.fori_loop(
        0, middle, eliminate, (zero,) * 8, unroll=5
    )
    ratio_x = up_m * r_m
    ratio_y = down_m * r_m
    back_x = down_m * sb_m
    back_y = up_m * sb_m
    inv_det = 1.0 / (1.0 - ratio_x * back_x)
    x_top = (v_m + ratio_x * u_m) * inv_det
    x_bot = u_m + back_x * x_top
    y_top = (w_m + ratio_y * z_m) * inv_det
    y_bot = z_m + back_y * y_top
    adj[middle - 1] = y_top
    adj[middle] = y_bot
    dlev[middle - 1] = gate[middle - 1] * x_top * (y_bot - y_top)

    def substitute(s, carry):
        x_t, y_t, x_b, y_b = carry
        k = middle - 1 - s
        x_n = val_x[k] + mul_x[k] * x_t
        y_n = val_y[k] + mul_y[k] * y_t
        adj[k] = y_n
        dlev[k] = gate[k] * x_n * (y_t - y_n)
        b = middle + s
        x_c = val_x[b] + mul_x[b] * x_b
        y_c = val_y[b] + mul_y[b] * y_b
        adj[b] = y_c
        dlev[b - 1] = gate[b - 1] * x_b * (y_c - y_b)
        return x_n, y_n, x_c, y_c

    lax.fori_loop(1, middle, substitute, (x_top, y_top, x_bot, y_bot), unroll=7)
    dlev[LEVELS - 1] = zero

    for i in range(ROWS):
        dlog[:, i * LANES : (i + 1) * LANES] = dlev[:, i, :].astype(BF16)
    for j in range(COLS // width):
        cols = slice(j * width, (j + 1) * width)
        back = jnp.dot(wo_b[...], dlog[:, cols], preferred_element_type=F32)
        dpre[:, cols] = (back * slope[:, cols]).astype(BF16)
    contract_last = (((1,), (1,)), ((), ()))
    sources = ((inp, dpre), (dlog, hid))

    for m, (small, big) in enumerate(sources):
        value = lax.dot_general(small[...], big[...], contract_last, preferred_element_type=F32)
        for n in range(4):
            grad[m, n // 2, (n % 2) * PAD : (n % 2 + 1) * PAD, :] = value[
                0:PAD, n * LANES : (n + 1) * LANES
            ]
        post(grad.at[m, 1 - core], from_core.at[m], partner, core_send.at[m], core_recv.at[m])

    for m in range(2):
        drain(from_core.at[m], core_recv.at[m])
        half[m] = grad[m, core] + from_core[m]
        if m:
            half[1, LEVELS : LEVELS + 1, :] = lax.dot_general(
                jnp.ones((16, COLS), BF16), dlog[...], contract_last, preferred_element_type=F32
            )[0:1]
    for dx, dy in same_core:
        p, dev = chip_peer(dx, dy, 0)
        post(
            half.at[:, pl.ds(p * ROWS_EACH, ROWS_EACH)], from_plane.at[p_me], dev,
            plane_send.at[0], plane_recv.at[0],
        )
    for m in range(2):
        from_plane[p_me, m] = half[m, mine, :]

    hi = jnp.zeros((LEVELS, LANES), F32)
    lo = jnp.zeros((LEVELS, LANES), F32)
    lane_l = lane_id[0:LEVELS]
    for i in range(ROWS):
        x = adj[:, i, :]
        adj_slabs[i, 0:LEVELS, :] = x
        hi = jnp.where(lane_l == i, pltpu.roll(x, i + 1, 1), hi)
        lo = jnp.where(lane_l == i, pltpu.roll(x, i, 1) if i else x, lo)
    edge2_hi[0:LEVELS, :] = hi
    edge2_lo[0:LEVELS, :] = lo
    for j in range(COLS // width):
        cols = slice(j * width, (j + 1) * width)
        out = jnp.dot(wi_b[...], dpre[:, cols], preferred_element_type=F32)
        for s in range(width // LANES):
            i = j * (width // LANES) + s
            din[i] = out[0:PAD, s * LANES : (s + 1) * LANES] * inv_radius

    scale = 1.0 / math.sqrt(count)
    drain(from_plane.at[pl.ds(0, CHIPS - 1)], plane_recv.at[0])
    mid[...] = jnp.sum(from_plane[...], axis=0)
    from_z[z_me] = mid[...]
    send_z(mid, from_z, z_send.at[0], z_recv.at[0])

    halo2_copies = send_halo(
        1, (adj_slabs.at[ROWS - 1], adj_slabs.at[0], edge2_hi, edge2_lo), halo2
    )
    drain(from_z.at[pl.ds(0, DEPTH - 1)], z_recv.at[0])
    chunk[...] = jnp.sum(from_z[...], axis=0) * scale
    for dx, dy in same_core:
        _, dev = chip_peer(dx, dy, 0)
        post(chunk, full.at[core, :, mine], dev, gather_send.at[0], gather_recv.at[0])
    for m in range(2):
        full[core, m, mine, :] = chunk[m]

    for copy in halo2_copies:
        copy.wait_recv()
    for i in range(ROWS):
        centre, near = neighbours(adj_slabs, halo2, i)
        wet = row_f < slabs[i, LEVELS : LEVELS + 1, :]
        din[i] = flux(centre, near, i) + jnp.where(wet, din[i], 0.0)

    peers_rows = pl.ds(0, (CHIPS - 1) * ROWS_EACH)
    drain(full.at[core, :, peers_rows], gather_recv.at[0])
    for m in range(2):
        post(full.at[core, m], full.at[core, m], partner, fwd_send.at[m], fwd_recv.at[m])

    def deliver(m, ref):
        for c in range(2):
            for h in range(2):
                n = 2 * c + h
                ref[:, n * LANES : (n + 1) * LANES] = full[c, m, h * PAD : h * PAD + LEVELS, :]

    drain(full.at[1 - core, 0], fwd_recv.at[0])
    weighted = jnp.zeros((PAD, LANES), F32)
    for c in range(2):
        for h in range(2):
            n = 2 * c + h
            part = full[c, 0, h * PAD : (h + 1) * PAD, :]
            weighted = weighted + wi_f[0:PAD, n * LANES : (n + 1) * LANES] * part
            gb_in_ref[:, n * LANES : (n + 1) * LANES] = part[LEVELS : LEVELS + 1, :]
    level_sum = radius * jnp.sum(weighted, axis=1, keepdims=True) * math.sqrt(count)
    level_scale = level_sum / (count * radius * radius * radius)
    for i in range(ROWS):
        out_ref[:, i, :] = (din[i] - wet_slab(i) * level_scale)[0:LEVELS]
    deliver(0, gw_in_ref)
    drain(full.at[1 - core, 1], fwd_recv.at[1])
    deliver(1, gw_out_ref)
    gb_out_ref[...] = full[0, 1, LEVELS : LEVELS + 1, :] + full[1, 1, LEVELS : LEVELS + 1, :]

    for copy in halo_copies + halo2_copies:
        copy.wait_send()
    drain(small_r1.at[pl.ds(0, PLANE - 1)], small_send.at[0])
    drain(small_r2.at[pl.ds(0, DEPTH - 1)], small_send.at[1])
    drain(from_plane.at[pl.ds(0, CHIPS - 1)], plane_send.at[0])
    drain(from_z.at[pl.ds(0, DEPTH - 1)], z_send.at[0])
    drain(full.at[core, :, peers_rows], gather_send.at[0])
    for m in range(2):
        drain(from_core.at[m], core_send.at[m])
        drain(full.at[core, m], fwd_send.at[m])


def store_results(
    out_v, gw_in_v, gb_in_v, gw_out_v, gb_out_v, out_h, gw_in_h, gb_in_h, gw_out_h, gb_out_h,
    gb_in_flat, gb_out_flat, sems,
):
    pairs = (
        (out_v, out_h), (gw_in_v, gw_in_h), (gw_out_v, gw_out_h),
        (gb_in_flat, gb_in_h), (gb_out_flat, gb_out_h),
    )
    copies = [pltpu.make_async_copy(src, dst, sems.at[n]) for n, (src, dst) in enumerate(pairs)]
    for copy in copies[:3]:
        copy.start()
    gb_in_flat[...] = gb_in_v[...].reshape(HIDDEN)
    gb_out_flat[...] = gb_out_v[...].reshape(LANES)[0:LEVELS]
    for copy in copies[3:]:
        copy.start()
    for copy in copies:
        copy.wait()


def shards(tracer, cotangent, land_mask, bottom, kappa, w_in, b_in, w_out, b_out):
    vmem = pl.BlockSpec(memory_space=pltpu.VMEM)
    hbm = pl.BlockSpec(memory_space=pltpu.HBM)
    slab = (ROWS, PAD, LANES)
    levels = (LEVELS, ROWS, LANES)
    edge = (PAD, LANES)
    flat = (2 * PAD, LANES)
    piece = (ROWS_EACH, LANES)

    def v(*shape, dtype=F32):
        return pltpu.VMEM(shape, dtype)

    def sems(n):
        return pltpu.SemaphoreType.DMA((n,))

    scratch = [
        v(*levels), v(*levels), v(ROWS, LANES, dtype=jnp.int32), v(ROWS, LANES, dtype=jnp.int32),
        pltpu.SMEM((LEVELS,), F32), v(LEVELS, HIDDEN, dtype=BF16), v(HIDDEN),
        v(LEVELS, HIDDEN, dtype=BF16), pltpu.SMEM((LEVELS,), F32),
        v(*slab), v(*slab), v(*edge), v(*edge), v(*edge), v(*edge),
        v(4, *edge), v(4, *edge), v(4 * ROWS, LANES),
        v(1, LANES), v(PLANE, 1, LANES), v(1, LANES), v(DEPTH, 1, LANES),
        v(LANES, HIDDEN), v(LANES, HIDDEN), v(LANES, HIDDEN, dtype=BF16),
        v(HIDDEN, LANES, dtype=BF16), v(LANES, HIDDEN, dtype=BF16), v(HIDDEN, LANES, dtype=BF16),
        v(LANES, COLS, dtype=BF16), v(HIDDEN, COLS, dtype=BF16), v(HIDDEN, COLS),
        v(HIDDEN, COLS, dtype=BF16), v(LANES, COLS, dtype=BF16), v(*slab),
        v(*levels), v(*levels), v(*levels), v(*levels), v(LEVELS + 1, ROWS, LANES),
        v(*levels), v(*levels), v(*levels), v(LANES, ROWS, LANES),
        v(2, 2, *flat), v(2, *flat), v(2, *flat), v(CHIPS, 2, *piece),
        v(2, *piece), v(DEPTH, 2, *piece), v(2, *piece), v(2, 2, *flat),
        sems(9), sems(2), sems(2), sems(2), sems(2), sems(1), sems(1),
        sems(1), sems(1), sems(1), sems(1), sems(2), sems(2), sems(8), sems(8),
    ]
    shapes = (
        jax.ShapeDtypeStruct(tracer.shape, F32),
        jax.ShapeDtypeStruct((LEVELS, HIDDEN), F32),
        jax.ShapeDtypeStruct((1, HIDDEN), F32),
        jax.ShapeDtypeStruct((LEVELS, HIDDEN), F32),
        jax.ShapeDtypeStruct((1, LANES), F32),
    )
    operands = (tracer, cotangent, land_mask, bottom, kappa, w_in, b_in, w_out.T, b_out)
    results = pl.pallas_call(
        kernel,
        out_shape=shapes,
        in_specs=[hbm] * 9,
        out_specs=(vmem,) * 5,
        scratch_shapes=scratch,
        compiler_params=pltpu.CompilerParams(
            collective_id=0, has_side_effects=True, vmem_limit_bytes=40 * 1024 * 1024
        ),
        name="step_adjoint",
    )(*(pltpu.with_memory_space_constraint(a, pltpu.HBM) for a in operands))
    out, gw_in, gb_in, gw_out, gb_out = pl.pallas_call(
        store_results,
        out_shape=shapes[:2]
        + (jax.ShapeDtypeStruct((HIDDEN,), F32), shapes[3], jax.ShapeDtypeStruct((LEVELS,), F32)),
        in_specs=[vmem] * 5,
        out_specs=(hbm,) * 5,
        scratch_shapes=[v(HIDDEN), v(LEVELS), sems(5)],
        compiler_params=pltpu.CompilerParams(vmem_limit_bytes=1024 * 1024),
        name="store_results",
    )(*results)
    return out, gw_in, gb_in, gw_out.T, gb_out


def solution(mesh):
    placed = (
        P(None, "lat", "lon"),
        P(None, "lat", "lon"),
        P("lat", "lon"),
        P("lat", "lon"),
        P(),
        P(),
        P(),
        P(),
        P(),
    )
    return jax.shard_map(
        shards,
        mesh=mesh,
        in_specs=placed,
        out_specs=(P(None, "lat", "lon"), P(), P(), P(), P()),
        check_vma=False,
    )
```

```python
import functools
import math

import jax
import jax.numpy as jnp
from jax import lax
from jax.experimental import pallas as pl
from jax.experimental.pallas import tpu as pltpu
from jax.sharding import PartitionSpec as P

MESH = pl.DeviceIdType.MESH
F32 = jnp.float32
BF16 = jnp.bfloat16

spread_coef = 0.15
level_eps = 1e-05

LEVELS = 100
ROWS = 8
LANES = 128
HIDDEN = 512
COLS = ROWS * LANES
PAD = 104
LAT = 8
LON = 32
SIDE = 4
CHIPS = SIDE * SIDE
PLANE = 2 * CHIPS
DEPTH = 8
HALF = HIDDEN // 2
ROWS_EACH = 2 * PAD // CHIPS


def ring(d, n):
    return min(d, n - d)


CHIP_STEPS = sorted(
    ((dx, dy) for dx in range(SIDE) for dy in range(SIDE)),
    key=lambda s: -(ring(s[0], SIDE) + ring(s[1], SIDE)),
)
Z_STEPS = sorted(range(1, DEPTH), key=lambda d: -ring(d, DEPTH))


def kernel(
    tracer_hbm, cot_hbm, land_hbm, bottom_hbm, kappa_hbm, w_in_hbm, b_in_hbm, w_out_hbm, b_out_hbm,
    out_ref, gw_in_ref, gb_in_ref, gw_out_ref, gb_out_ref,
    tr_v, cot_v, land_v, bottom_v, kappa_s, w_in_v, b_in_v, w_out_v, b_out_s,
    slabs, adj_slabs, edge_hi, edge_lo, edge2_hi, edge2_lo, halo, halo2, near_depth,
    small_src, small_r1, small_mid, small_r2,
    wi_f, wo_f, wi_b, w1t, wot, wo_b,
    inp, hid, slope, dpre, dlog, din,
    logit, mixed, val_x, val_y, mul_x, mul_y, gate, adj, dlev,
    grad, from_core, half, from_plane, mid, from_z, chunk, full,
    load_sems, small_send, small_recv, core_send, core_recv, plane_send, plane_recv,
    z_send, z_recv, gather_send, gather_recv, fwd_send, fwd_recv, halo_send, halo_recv,
):
    lat = lax.axis_index("lat")
    lon = lax.axis_index("lon")
    y_me = lat % SIDE
    x_me = (lat // SIDE) * 2 + lon // 16
    z_me = (lon // 2) % DEPTH
    core = lon % 2
    p_me = x_me * SIDE + y_me
    q_me = p_me * 2 + core
    mine = pl.ds(p_me * ROWS_EACH, ROWS_EACH)
    lon_z = z_me * 2

    loads = []
    for n, (src, dst) in enumerate(
        (
            (tracer_hbm, tr_v), (land_hbm, land_v), (bottom_hbm, bottom_v), (w_in_hbm, w_in_v),
            (b_in_hbm, b_in_v), (w_out_hbm, w_out_v), (cot_hbm, cot_v), (kappa_hbm, kappa_s),
            (b_out_hbm, b_out_s),
        )
    ):
        loads.append(pltpu.make_async_copy(src, dst, load_sems.at[n]))
    for load in loads[:3]:
        load.start()

    xs = [(x_me + d) % SIDE for d in range(SIDE)]
    ys = [(y_me + d) % SIDE for d in range(SIDE)]

    def chip_peer(dx, dy, dc):
        to_core = core if dc == 0 else 1 - core
        dev = ((xs[dx] // 2) * SIDE + ys[dy], (xs[dx] % 2) * 16 + lon_z + to_core)
        return xs[dx] * SIDE + ys[dy], dev

    def z_peer(d):
        return (lat, (lon // 16) * 16 + ((z_me + d) % DEPTH) * 2 + core)

    everyone = [(dx, dy, dc) for dx, dy in CHIP_STEPS for dc in (0, 1) if dx or dy or dc]
    same_core = [(dx, dy) for dx, dy in CHIP_STEPS if dx or dy]
    partner = (lat, lon + 1 - 2 * core)

    barrier = pltpu.get_barrier_semaphore()

    def greet(dev):
        pl.semaphore_signal(barrier, inc=1, device_id=dev, device_id_type=MESH)

    greet(z_peer(Z_STEPS[0]))
    for step in everyone:
        greet(chip_peer(*step)[1])
    for d in Z_STEPS[1:]:
        greet(z_peer(d))
    greet((lat, (lon + 2 * core - 1 + LON) % LON))
    for load in loads[3:]:
        load.start()

    row_id = lax.broadcasted_iota(jnp.int32, (PAD, LANES), 0)
    lane_id = lax.broadcasted_iota(jnp.int32, (PAD, LANES), 1)
    row_f = row_id.astype(F32)
    diag = row_id == lane_id

    def as_row(column):
        return jnp.sum(jnp.where(diag, column, 0.0), axis=0, keepdims=True)

    def as_column(row):
        return jnp.sum(jnp.where(diag, row, 0.0), axis=1, keepdims=True)

    for n in range(3):
        loads[n].wait()
    depth_all = (land_v[...] * bottom_v[...]).astype(F32)
    energy = jnp.zeros((PAD, LANES), F32)
    for i in range(ROWS):
        slabs[i, 0:LEVELS, :] = tr_v[:, i, :]
        slabs[i, LEVELS:PAD, :] = jnp.broadcast_to(depth_all[i : i + 1, :], (PAD - LEVELS, LANES))
        wet_x = jnp.where(row_f < depth_all[i : i + 1, :], slabs[i], 0.0)
        energy = energy + wet_x * wet_x
    small_src[...] = as_row(jnp.sum(energy, axis=1, keepdims=True))
    small_r1[q_me] = small_src[...]

    pl.semaphore_wait(barrier, PLANE - 1 + DEPTH - 1 + 1)

    def post(src, dst, dev, send, recv):
        pltpu.make_async_remote_copy(
            src, dst, send, recv, device_id=dev, device_id_type=MESH
        ).start()

    def send_z(src, dst, send, recv):
        for d in Z_STEPS:
            post(src, dst.at[z_me], z_peer(d), send, recv)

    def drain(ref, sem):
        pltpu.make_async_copy(ref, ref, sem).wait()

    def send_halo(k, pieces, dst):
        up = (lat + 1) % LAT
        down = (lat + LAT - 1) % LAT
        right = (lon + 1) % LON
        left = (lon + LON - 1) % LON
        targets = ((up, lon), (down, lon), (lat, right), (lat, left))
        copies = []
        for n, (src, dev) in enumerate(zip(pieces, targets)):
            copy = pltpu.make_async_remote_copy(
                src, dst.at[n], halo_send.at[4 * k + n], halo_recv.at[4 * k + n],
                device_id=dev, device_id_type=MESH,
            )
            copy.start()
            copies.append(copy)
        return copies

    for step in everyone:
        post(small_src, small_r1.at[q_me], chip_peer(*step)[1], small_send.at[0], small_recv.at[0])
    hi = jnp.zeros((PAD, LANES), F32)
    lo = jnp.zeros((PAD, LANES), F32)
    for i in range(ROWS):
        x = slabs[i]
        hi = jnp.where(lane_id == i, pltpu.roll(x, i + 1, 1), hi)
        lo = jnp.where(lane_id == i, pltpu.roll(x, i, 1) if i else x, lo)
    edge_hi[...] = hi
    edge_lo[...] = lo
    halo_copies = send_halo(0, (slabs.at[ROWS - 1], slabs.at[0], edge_hi, edge_lo), halo)

    for n in range(3, 6):
        loads[n].wait()
    bias = b_in_v[...].reshape(1, HIDDEN)
    bias_hi = bias.astype(BF16).astype(F32)
    bias_mid = (bias - bias_hi).astype(BF16).astype(F32)
    bias_lo = bias - bias_hi - bias_mid
    wi_f[LEVELS:LANES, :] = jnp.zeros((LANES - LEVELS, HIDDEN), F32)
    wi_f[0:LEVELS, :] = w_in_v[...].astype(F32)
    wi_f[LEVELS : LEVELS + 1, :] = bias_hi
    wi_f[LEVELS + 1 : LEVELS + 2, :] = bias_mid
    wi_f[LEVELS + 2 : LEVELS + 3, :] = bias_lo
    wi_b[...] = wi_f[...].astype(BF16)
    w1t[...] = wi_f[...].T.astype(BF16)
    wo_f[LEVELS:LANES, :] = jnp.zeros((LANES - LEVELS, HIDDEN), F32)
    wo_f[0:LEVELS, :] = w_out_v[...].astype(F32)
    wot[...] = wo_f[...].astype(BF16)
    wo_b[...] = wo_f[...].T.astype(BF16)
    dlev[LEVELS:LANES] = jnp.zeros((LANES - LEVELS, ROWS, LANES), F32)
    for i in range(ROWS):
        adj_slabs[i, LEVELS:PAD, :] = jnp.zeros((PAD - LEVELS, LANES), F32)
    edge2_hi[LEVELS:PAD, :] = jnp.zeros((PAD - LEVELS, LANES), F32)
    edge2_lo[LEVELS:PAD, :] = jnp.zeros((PAD - LEVELS, LANES), F32)
    inp[PAD - 8 : LANES, :] = jnp.zeros((LANES - PAD + 8, COLS), BF16)
    for n in range(6, 9):
        loads[n].wait()

    drain(small_r1.at[pl.ds(0, PLANE - 1)], small_recv.at[0])
    small_mid[...] = jnp.sum(small_r1[...], axis=0)
    small_r2[z_me] = small_mid[...]
    send_z(small_mid, small_r2, small_send.at[1], small_recv.at[1])

    for copy in halo_copies:
        copy.wait_recv()

    def neighbours(field, edges, i):
        centre = field[i]
        below = field[i + 1] if i + 1 < ROWS else edges[1]
        above = field[i - 1] if i else edges[0]
        from_left = pltpu.roll(edges[2], LANES - i, 1) if i else edges[2]
        left = jnp.where(lane_id == 0, from_left, pltpu.roll(centre, 1, 1))
        right = jnp.where(
            lane_id == LANES - 1, pltpu.roll(edges[3], LANES - 1 - i, 1), pltpu.roll(centre, LANES - 1, 1)
        )
        return centre, (below, above, left, right)

    def flux(centre, near, i):
        total = jnp.zeros((PAD, LANES), F32)
        for n in range(4):
            total = total + jnp.where(
                row_f < near_depth[n * ROWS + i : n * ROWS + i + 1, :], near[n] - centre, 0.0
            )
        return centre + spread_coef * total

    has_above = jnp.where(lat > 0, 1.0, 0.0)
    has_below = jnp.where(lat < LAT - 1, 1.0, 0.0)
    for i in range(ROWS):
        centre, near = neighbours(slabs, halo, i)
        own = centre[LEVELS : LEVELS + 1, :]
        for n in range(4):
            other = near[n][LEVELS : LEVELS + 1, :]
            if n == 0 and i == ROWS - 1:
                other = other * has_below
            if n == 1 and i == 0:
                other = other * has_above
            near_depth[n * ROWS + i : n * ROWS + i + 1, :] = jnp.minimum(own, other)
        mixed[:, i, :] = flux(centre, near, i)[0:LEVELS]

    drain(small_r2.at[pl.ds(0, DEPTH - 1)], small_recv.at[1])
    energy_all = as_column(jnp.sum(small_r2[...], axis=0))
    count = float(LAT * LON * COLS)
    radius = jnp.sqrt(energy_all / count + level_eps)
    inv_radius = 1.0 / radius

    def wet_slab(i):
        x = slabs[i]
        return jnp.where(row_f < x[LEVELS : LEVELS + 1, :], x, 0.0)

    one_rows = jnp.where(row_id < LEVELS + 3, 1.0, 0.0)
    for i in range(ROWS):
        scaled = jnp.where(row_id < LEVELS, wet_slab(i) * inv_radius, one_rows)
        scaled = jnp.concatenate([scaled, jnp.zeros((LANES - PAD, LANES), F32)], axis=0)
        inp[:, i * LANES : (i + 1) * LANES] = scaled.astype(BF16)

    width = 256
    for j in range(COLS // width):
        cols = slice(j * width, (j + 1) * width)
        pre = jnp.dot(w1t[...], inp[:, cols], preferred_element_type=F32)
        sig = 1.0 / (1.0 + jnp.exp(-pre))
        act = pre * sig
        hid[:, cols] = act.astype(BF16)
        slope[:, cols] = sig * (1.0 + pre * (1.0 - sig))
        out = jnp.dot(wot[...], hid[:, cols], preferred_element_type=F32)
        for s in range(width // LANES):
            logit[:, j * (width // LANES) + s, :] = out[0:LEVELS, s * LANES : (s + 1) * LANES]

    depth = depth_all
    middle = LEVELS // 2

    def level_terms(k):
        x = logit[k] + b_out_s[k]
        ex = jnp.exp(-jnp.abs(x))
        soft = jnp.maximum(x, 0.0) + jnp.log1p(ex)
        sig = jnp.where(x >= 0.0, 1.0, ex) / (1.0 + ex)
        kf = (k + 1).astype(F32)
        open_face = kf < depth
        kap = kappa_s[k]
        down = jnp.where(open_face, kap + soft, 0.0)
        up = jnp.where(open_face, kap, 0.0)
        gate[k] = jnp.where(open_face, sig, 0.0)
        return down, up

    def eliminate(s, carry):
        down_p, up_p, r_p, v_p, w_p, sb_n, u_n, z_n = carry
        k = s
        down, up = level_terms(k)
        pivot = 1.0 + down + up_p - down_p * up_p * r_p
        r = 1.0 / pivot
        v = (mixed[k] + down_p * v_p) * r
        w = (cot_v[k] + up_p * w_p) * r
        val_x[k] = v
        val_y[k] = w
        mul_x[k] = up * r
        mul_y[k] = down * r
        b = LEVELS - 1 - s
        down_b, up_b = level_terms(b)
        up_above = jnp.where(b.astype(F32) < depth, kappa_s[b - 1], 0.0)
        pivot_b = 1.0 + down_b + up_above - down_b * up_b * sb_n
        sb = 1.0 / pivot_b
        u = (mixed[b] + up_b * u_n) * sb
        zz = (cot_v[b] + down_b * z_n) * sb
        val_x[b] = u
        val_y[b] = zz
        mul_y[b] = up_above * sb
        mul_x[b + 1] = down_b * sb_n
        return down, up, r, v, w, sb, u, zz

    zero = jnp.zeros((ROWS, LANES), F32)
    down_m, up_m, r_m, v_m, w_m, sb_m, u_m, z_m = lax.fori_loop(
        0, middle, eliminate, (zero,) * 8, unroll=5
    )
    ratio_x = up_m * r_m
    ratio_y = down_m * r_m
    back_x = down_m * sb_m
    back_y = up_m * sb_m
    inv_det = 1.0 / (1.0 - ratio_x * back_x)
    x_top = (v_m + ratio_x * u_m) * inv_det
    x_bot = u_m + back_x * x_top
    y_top = (w_m + ratio_y * z_m) * inv_det
    y_bot = z_m + back_y * y_top
    adj[middle - 1] = y_top
    adj[middle] = y_bot
    dlev[middle - 1] = gate[middle - 1] * x_top * (y_bot - y_top)

    def substitute(s, carry):
        x_t, y_t, x_b, y_b = carry
        k = middle - 1 - s
        x_n = val_x[k] + mul_x[k] * x_t
        y_n = val_y[k] + mul_y[k] * y_t
        adj[k] = y_n
        dlev[k] = gate[k] * x_n * (y_t - y_n)
        b = middle + s
        x_c = val_x[b] + mul_x[b] * x_b
        y_c = val_y[b] + mul_y[b] * y_b
        adj[b] = y_c
        dlev[b - 1] = gate[b - 1] * x_b * (y_c - y_b)
        return x_n, y_n, x_c, y_c

    lax.fori_loop(1, middle, substitute, (x_top, y_top, x_bot, y_bot), unroll=7)
    dlev[LEVELS - 1] = zero

    for i in range(ROWS):
        dlog[:, i * LANES : (i + 1) * LANES] = dlev[:, i, :].astype(BF16)
    for j in range(COLS // width):
        cols = slice(j * width, (j + 1) * width)
        back = jnp.dot(wo_b[...], dlog[:, cols], preferred_element_type=F32)
        dpre[:, cols] = (back * slope[:, cols]).astype(BF16)
    contract_last = (((1,), (1,)), ((), ()))
    sources = ((inp, dpre), (dlog, hid))

    for m, (small, big) in enumerate(sources):
        value = lax.dot_general(small[...], big[...], contract_last, preferred_element_type=F32)
        for n in range(4):
            grad[m, n // 2, (n % 2) * PAD : (n % 2 + 1) * PAD, :] = value[
                0:PAD, n * LANES : (n + 1) * LANES
            ]
        post(grad.at[m, 1 - core], from_core.at[m], partner, core_send.at[m], core_recv.at[m])

    bout_row = lax.dot_general(
        jnp.ones((16, COLS), BF16), dlog[...], contract_last, preferred_element_type=F32
    )[0:1]

    for m in range(2):
        drain(from_core.at[m], core_recv.at[m])
        half[m] = grad[m, core] + from_core[m]
        if m:
            half[1, LEVELS : LEVELS + 1, :] = bout_row
        for dx, dy in same_core:
            p, dev = chip_peer(dx, dy, 0)
            post(
                half.at[m, pl.ds(p * ROWS_EACH, ROWS_EACH)], from_plane.at[m, p_me], dev,
                plane_send.at[m], plane_recv.at[m],
            )
        from_plane[m, p_me] = half[m, mine, :]

    hi = jnp.zeros((LEVELS, LANES), F32)
    lo = jnp.zeros((LEVELS, LANES), F32)
    lane_l = lane_id[0:LEVELS]
    for i in range(ROWS):
        x = adj[:, i, :]
        adj_slabs[i, 0:LEVELS, :] = x
        hi = jnp.where(lane_l == i, pltpu.roll(x, i + 1, 1), hi)
        lo = jnp.where(lane_l == i, pltpu.roll(x, i, 1) if i else x, lo)
    edge2_hi[0:LEVELS, :] = hi
    edge2_lo[0:LEVELS, :] = lo
    for j in range(COLS // width):
        cols = slice(j * width, (j + 1) * width)
        out = jnp.dot(wi_b[...], dpre[:, cols], preferred_element_type=F32)
        for s in range(width // LANES):
            i = j * (width // LANES) + s
            din[i] = out[0:PAD, s * LANES : (s + 1) * LANES] * inv_radius

    scale = 1.0 / math.sqrt(count)
    for m in range(2):
        drain(from_plane.at[m, pl.ds(0, CHIPS - 1)], plane_recv.at[m])
        mid[m] = jnp.sum(from_plane[m], axis=0)
        from_z[m, z_me] = mid[m]
        send_z(mid.at[m], from_z.at[m], z_send.at[m], z_recv.at[m])

    halo2_copies = send_halo(
        1, (adj_slabs.at[ROWS - 1], adj_slabs.at[0], edge2_hi, edge2_lo), halo2
    )
    for m in range(2):
        drain(from_z.at[m, pl.ds(0, DEPTH - 1)], z_recv.at[m])
        chunk[m] = jnp.sum(from_z[m], axis=0) * scale
        for dx, dy in same_core:
            _, dev = chip_peer(dx, dy, 0)
            post(chunk.at[m], full.at[m, core, mine], dev, gather_send.at[m], gather_recv.at[m])
        full[m, core, mine, :] = chunk[m]

    for copy in halo2_copies:
        copy.wait_recv()
    for i in range(ROWS):
        centre, near = neighbours(adj_slabs, halo2, i)
        wet = row_f < slabs[i, LEVELS : LEVELS + 1, :]
        din[i] = flux(centre, near, i) + jnp.where(wet, din[i], 0.0)

    peers_rows = pl.ds(0, (CHIPS - 1) * ROWS_EACH)
    for m in range(2):
        drain(full.at[m, core, peers_rows], gather_recv.at[m])
        post(full.at[m, core], full.at[m, core], partner, fwd_send.at[m], fwd_recv.at[m])

    def deliver(m, ref):
        for c in range(2):
            for h in range(2):
                n = 2 * c + h
                ref[:, n * LANES : (n + 1) * LANES] = full[m, c, h * PAD : h * PAD + LEVELS, :]

    drain(full.at[0, 1 - core], fwd_recv.at[0])
    weighted = jnp.zeros((PAD, LANES), F32)
    for c in range(2):
        for h in range(2):
            n = 2 * c + h
            part = full[0, c, h * PAD : (h + 1) * PAD, :]
            weighted = weighted + wi_f[0:PAD, n * LANES : (n + 1) * LANES] * part
            gb_in_ref[:, n * LANES : (n + 1) * LANES] = part[LEVELS : LEVELS + 1, :]
    level_sum = radius * jnp.sum(weighted, axis=1, keepdims=True) * math.sqrt(count)
    level_scale = level_sum / (count * radius * radius * radius)
    for i in range(ROWS):
        out_ref[:, i, :] = (din[i] - wet_slab(i) * level_scale)[0:LEVELS]
    deliver(0, gw_in_ref)
    drain(full.at[1, 1 - core], fwd_recv.at[1])
    deliver(1, gw_out_ref)
    gb_out_ref[...] = full[1, 0, LEVELS : LEVELS + 1, :] + full[1, 1, LEVELS : LEVELS + 1, :]

    for copy in halo_copies + halo2_copies:
        copy.wait_send()
    drain(small_r1.at[pl.ds(0, PLANE - 1)], small_send.at[0])
    drain(small_r2.at[pl.ds(0, DEPTH - 1)], small_send.at[1])
    for m in range(2):
        drain(from_core.at[m], core_send.at[m])
        drain(from_plane.at[m, pl.ds(0, CHIPS - 1)], plane_send.at[m])
        drain(from_z.at[m, pl.ds(0, DEPTH - 1)], z_send.at[m])
        drain(full.at[m, core, peers_rows], gather_send.at[m])
        drain(full.at[m, core], fwd_send.at[m])


def store_results(
    out_v, gw_in_v, gb_in_v, gw_out_v, gb_out_v, out_h, gw_in_h, gb_in_h, gw_out_h, gb_out_h,
    gb_in_flat, gb_out_flat, sems,
):
    pairs = (
        (out_v, out_h), (gw_in_v, gw_in_h), (gw_out_v, gw_out_h),
        (gb_in_flat, gb_in_h), (gb_out_flat, gb_out_h),
    )
    copies = [pltpu.make_async_copy(src, dst, sems.at[n]) for n, (src, dst) in enumerate(pairs)]
    for copy in copies[:3]:
        copy.start()
    gb_in_flat[...] = gb_in_v[...].reshape(HIDDEN)
    gb_out_flat[...] = gb_out_v[...].reshape(LANES)[0:LEVELS]
    for copy in copies[3:]:
        copy.start()
    for copy in copies:
        copy.wait()


def shards(tracer, cotangent, land_mask, bottom, kappa, w_in, b_in, w_out, b_out):
    vmem = pl.BlockSpec(memory_space=pltpu.VMEM)
    hbm = pl.BlockSpec(memory_space=pltpu.HBM)
    slab = (ROWS, PAD, LANES)
    levels = (LEVELS, ROWS, LANES)
    edge = (PAD, LANES)
    flat = (2 * PAD, LANES)
    piece = (ROWS_EACH, LANES)

    def v(*shape, dtype=F32):
        return pltpu.VMEM(shape, dtype)

    def sems(n):
        return pltpu.SemaphoreType.DMA((n,))

    scratch = [
        v(*levels), v(*levels), v(ROWS, LANES, dtype=jnp.int32), v(ROWS, LANES, dtype=jnp.int32),
        pltpu.SMEM((LEVELS,), F32), v(LEVELS, HIDDEN, dtype=BF16), v(HIDDEN),
        v(LEVELS, HIDDEN, dtype=BF16), pltpu.SMEM((LEVELS,), F32),
        v(*slab), v(*slab), v(*edge), v(*edge), v(*edge), v(*edge),
        v(4, *edge), v(4, *edge), v(4 * ROWS, LANES),
        v(1, LANES), v(PLANE, 1, LANES), v(1, LANES), v(DEPTH, 1, LANES),
        v(LANES, HIDDEN), v(LANES, HIDDEN), v(LANES, HIDDEN, dtype=BF16),
        v(HIDDEN, LANES, dtype=BF16), v(LANES, HIDDEN, dtype=BF16), v(HIDDEN, LANES, dtype=BF16),
        v(LANES, COLS, dtype=BF16), v(HIDDEN, COLS, dtype=BF16), v(HIDDEN, COLS),
        v(HIDDEN, COLS, dtype=BF16), v(LANES, COLS, dtype=BF16), v(*slab),
        v(*levels), v(*levels), v(*levels), v(*levels), v(LEVELS + 1, ROWS, LANES),
        v(*levels), v(*levels), v(*levels), v(LANES, ROWS, LANES),
        v(2, 2, *flat), v(2, *flat), v(2, *flat), v(2, CHIPS, *piece),
        v(2, *piece), v(2, DEPTH, *piece), v(2, *piece), v(2, 2, *flat),
        sems(9), sems(2), sems(2), sems(2), sems(2), sems(2), sems(2),
        sems(2), sems(2), sems(2), sems(2), sems(2), sems(2), sems(8), sems(8),
    ]
    shapes = (
        jax.ShapeDtypeStruct(tracer.shape, F32),
        jax.ShapeDtypeStruct((LEVELS, HIDDEN), F32),
        jax.ShapeDtypeStruct((1, HIDDEN), F32),
        jax.ShapeDtypeStruct((LEVELS, HIDDEN), F32),
        jax.ShapeDtypeStruct((1, LANES), F32),
    )
    operands = (tracer, cotangent, land_mask, bottom, kappa, w_in, b_in, w_out.T, b_out)
    results = pl.pallas_call(
        kernel,
        out_shape=shapes,
        in_specs=[hbm] * 9,
        out_specs=(vmem,) * 5,
        scratch_shapes=scratch,
        compiler_params=pltpu.CompilerParams(
            collective_id=0, has_side_effects=True, vmem_limit_bytes=40 * 1024 * 1024
        ),
        name="step_adjoint",
    )(*(pltpu.with_memory_space_constraint(a, pltpu.HBM) for a in operands))
    out, gw_in, gb_in, gw_out, gb_out = pl.pallas_call(
        store_results,
        out_shape=shapes[:2]
        + (jax.ShapeDtypeStruct((HIDDEN,), F32), shapes[3], jax.ShapeDtypeStruct((LEVELS,), F32)),
        in_specs=[vmem] * 5,
        out_specs=(hbm,) * 5,
        scratch_shapes=[v(HIDDEN), v(LEVELS), sems(5)],
        compiler_params=pltpu.CompilerParams(vmem_limit_bytes=1024 * 1024),
        name="store_results",
    )(*results)
    return out, gw_in, gb_in, gw_out.T, gb_out


def solution(mesh):
    placed = (
        P(None, "lat", "lon"),
        P(None, "lat", "lon"),
        P("lat", "lon"),
        P("lat", "lon"),
        P(),
        P(),
        P(),
        P(),
        P(),
    )
    return jax.shard_map(
        shards,
        mesh=mesh,
        in_specs=placed,
        out_specs=(P(None, "lat", "lon"), P(), P(), P(), P()),
        check_vma=False,
    )
```
